32 devices in a mesh: fsdp: 4 (over x, core), ctx: 2 (over y), tp: 4 (over z).
Axes of the slice: x: 2, y: 2, z: 4, core: 2. Of those that a mesh axis runs over, the one named last changes fastest.
Arguments:
- tokens: bfloat16 [8, 2048, 768], P('fsdp', 'ctx'), may hold values from -6 to 6
- gain_one: bfloat16 [768], P('fsdp'), may hold values from 0.5 to 1.5
- w_qkv: bfloat16 [768, 3, 768], P('fsdp', None, 'tp'), may hold values from -0.21875 to 0.21875
- kernel: bfloat16 [3, 3, 12, 64], P(None, None, 'tp', 'fsdp'), may hold values from -3 to 3
- w_out: bfloat16 [768, 768], P('tp', 'fsdp'), may hold values from -3 to 3
- gain_two: bfloat16 [768], P('fsdp'), may hold values from 0.5 to 1.5
- w_up: bfloat16 [768, 3072], P('fsdp', 'tp'), may hold values from -0.21875 to 0.21875
- w_down: bfloat16 [3072, 768], P('tp', 'fsdp'), may hold values from -0.109375 to 0.109375
- block_ids: int32 [8, 2048], P('fsdp'), may hold values from 0 to 15, never falling along the last dimension, each value on 1 to 256 neighbouring positions
- seq_ids: int32 [8, 2], P('fsdp'), may hold values from 0 to 1, as said below
- cotangent: bfloat16 [8, 2048, 768], P('fsdp', 'ctx'), may hold values from -6 to 6
Outputs:
- block_out: bfloat16 [8, 2048, 768], P('fsdp', 'ctx')
- input_grad: float32 [8, 2048, 768], P('fsdp', 'ctx')
- grad_gain_one: float32 [768], P('fsdp')
- grad_w_qkv: float32 [768, 3, 768], P('fsdp', None, 'tp')
- grad_kernel: float32 [3, 3, 12, 64], P(None, None, 'tp', 'fsdp')
- grad_w_out: float32 [768, 768], P('tp', 'fsdp')
- grad_gain_two: float32 [768], P('fsdp')
- grad_w_up: float32 [768, 3072], P('fsdp', 'tp')
- grad_w_down: float32 [3072, 768], P('tp', 'fsdp')
The draws below stay inside these ranges and needn't reach their ends.
Inputs may be any that keep to these rules, and one draw needn't show every extreme that they name: `block_ids`: along a row block ids never fall; a block holds 1 to 256 tokens and some block holds exactly 256. `seq_ids`: along a row the ids never fall; a row is one sequence (all ids 0) or two sequences of 1024 tokens each (ids 0, then 1).
All inputs are finite; a program needn't handle non-finite values.
Results may differ from the reference program's by a relative error of at most 0.038.
Values may be sent and summed in bfloat16 or wider, within the bound.
A program may use at most 256 MiB of HBM per device.

```python
import math
import jax
import jax.numpy as jnp
import numpy as np
from jax import lax

D = 768
HEADS = 12
HD = 64
FF = 3072
TAPS = 3
BLOCK = 256
LENGTH = 2048
GROUP = 1024
SEQS = 8


def draw_seq_ids(key, part):
    pieces = LENGTH // GROUP
    split_rows = jax.random.randint(key, (SEQS, 1), 0, 2)
    first_row = jnp.arange(SEQS)[:, None] == 0
    split_rows = jnp.where(first_row, 1, split_rows)
    column = jnp.arange(pieces)[None, :]
    return (split_rows * (column >= pieces // 2)).astype(jnp.int32)


def shard_levels(rng, shape, shards, least, top_value):
    loudness = 1.0
    for axis_at, blocks in shards:
        heights = jax.random.uniform(jax.random.fold_in(jax.random.fold_in(rng, 6), axis_at), (blocks,), jnp.float32, least / len(shards), top_value / len(shards))
        loudness = loudness * jnp.repeat(jnp.exp(heights), shape[axis_at] // blocks).reshape((-1,) + (1,) * (len(shape) - 1 - axis_at))
    return loudness


def profile(amount, total, reach, lean):
    loads = [(1 << 20) // math.isqrt(rank ** lean) + 1 for rank in range(2, amount + 1)]
    spare, holding = total - reach - (amount - 1), [1] * (amount - 1)
    while spare > 0:
        free = [i for i in range(amount - 1) if holding[i] < reach]
        whole, remaining = sum([loads[i] for i in free]), spare
        for i in free:
            more = min(reach - holding[i], max(1, remaining * loads[i] // whole), spare)
            holding[i] = holding[i] + more
            spare = spare - more
    return np.array([reach] + holding)


def ragged_sizes(rng, amount, total, bound, skew):
    if amount == 2:
        one = jax.random.randint(rng, (), max(1, total - bound), min(bound, total - 1) + 1)
        return jnp.stack([one, total - one])
    sizes = jnp.asarray(profile(amount, total, bound, skew), jnp.int32)
    couples = (amount - 1) // 2
    giver, sink = sizes[1:1 + 2 * couples:2], sizes[2:2 + 2 * couples:2]
    margin = jnp.minimum(giver - 1, bound - sink)
    moved = jax.random.randint(jax.random.fold_in(rng, 1), (couples,), 0, 1 << 20) % (margin + 1)
    sizes = sizes.at[1:1 + 2 * couples:2].set(giver - moved).at[2:2 + 2 * couples:2].set(sink + moved)
    return sizes[jax.random.permutation(jax.random.fold_in(rng, 2), amount)]


def gaussian(rng, shape, deviation, most, shards=(), kind=jnp.bfloat16):
    entries = jax.random.normal(rng, shape, jnp.float32) * deviation
    if len(shards) > 0:
        entries = shard_levels(rng, shape, shards, -0.22, 0.18) * entries
    return jnp.clip(entries, min=-most, max=most).astype(kind)


def setup_inputs(seed: int = 0) -> dict:
    key_of = jax.random.split(jax.random.key(seed), 12)
    tokens = gaussian(key_of[0], (SEQS, LENGTH, D), 1.0, 6.0, ((0, 4), (1, 2)))
    gain_one = jnp.clip(1.0 + 0.1 * jax.random.normal(key_of[1], (D,), jnp.float32), 0.5, 1.5).astype(jnp.bfloat16)
    w_qkv = gaussian(key_of[2], (D, 3, D), D ** -0.5, 0.21875, ((0, 4), (2, 4)))
    kernel = gaussian(key_of[3], (TAPS, 3, HEADS, HD), 0.6, 3.0, ((2, 4), (3, 4)))
    w_out = gaussian(key_of[4], (D, D), (D // 192) ** -0.5, 3.0, ((0, 4), (1, 4)))
    gain_two = jnp.clip(1.0 + 0.1 * jax.random.normal(key_of[5], (D,), jnp.float32), 0.5, 1.5).astype(jnp.bfloat16)
    w_up = gaussian(key_of[6], (D, FF), D ** -0.5, 0.21875, ((0, 4), (1, 4)))
    w_down = gaussian(key_of[7], (FF, D), FF ** -0.5, 0.109375, ((0, 4), (1, 4)))
    block_ids = jax.vmap(lambda own: jnp.searchsorted(jnp.cumsum(ragged_sizes(own, 2 * LENGTH // BLOCK, LENGTH, BLOCK, 1)), jnp.arange(LENGTH), side="right"))(jax.random.split(key_of[8], SEQS)).reshape((SEQS, LENGTH)).astype(jnp.int32)
    seq_ids = draw_seq_ids(jax.random.fold_in(key_of[11], 71), 0)
    cotangent = gaussian(key_of[10], (SEQS, LENGTH, D), 1.0, 6.0, ((0, 4), (1, 2)))
    return {"tokens": tokens, "gain_one": gain_one, "w_qkv": w_qkv, "kernel": kernel, "w_out": w_out, "gain_two": gain_two, "w_up": w_up, "w_down": w_down, "block_ids": block_ids, "seq_ids": seq_ids, "cotangent": cotangent}


@jax.custom_vjp
def low(v):
    return lax.optimization_barrier(v.astype(jnp.bfloat16)).astype(jnp.float32)

@jax.custom_vjp
def low_back(v):
    return v

def low_keep(v):
    return (low(v), None)

def low_pass(kept, grad):
    return (grad,)

def back_keep(v):
    return (v, None)

def back_low(kept, grad):
    return (low(grad),)
low.defvjp(low_keep, low_pass)
low_back.defvjp(back_keep, back_low)

def norm_scaled(values, gain_full):
    return values * lax.rsqrt(lax.optimization_barrier(jnp.mean(values * values, axis=-1, keepdims=True)) + 1e-06) * gain_full

def layer_rows(states, gain_first, qkv_full, conv_taps, out_full, gain_second, up_full, down_full, block_row, owner_row):
    highest = lax.Precision.HIGHEST
    length = states.shape[0]
    normed = low(norm_scaled(states, gain_first))
    linear = low_back(low(jnp.einsum('td,dce->tce', normed, qkv_full, precision=highest)))
    tap_weights = conv_taps.reshape(conv_taps.shape[0], 3, -1)
    mixed_conv = tap_weights[0] * linear
    for offset in range(1, tap_weights.shape[0]):
        shifted = jnp.concatenate([jnp.zeros((offset,) + linear.shape[1:], jnp.float32), linear[:length - offset]], axis=0)
        earlier = jnp.concatenate([jnp.full((offset,), -1, jnp.int32), owner_row[:length - offset]])
        same_seq = (earlier == owner_row).astype(jnp.float32)
        mixed_conv = mixed_conv + tap_weights[offset] * shifted * same_seq[:, None, None]
    triple = low(mixed_conv)
    allowed = (owner_row[:, None] == owner_row[None, :]) & (block_row[None, :] <= block_row[:, None])
    score_scale = HD ** (-0.5)

    def head_attend(head_parts):
        queries, key_heads, value_heads = head_parts
        scores = low_back(jnp.dot(queries, key_heads.T, precision=highest) * score_scale)
        probs = jax.nn.softmax(jnp.where(allowed, scores, -1e+30), axis=-1)
        return jnp.dot(low(probs), value_heads, precision=highest)
    heads_first = triple.reshape(length, 3, HEADS, HD).transpose(1, 2, 0, 3)
    attended = lax.map(jax.checkpoint(head_attend), (heads_first[0], heads_first[1], heads_first[2]))
    attended = low_back(low(attended.transpose(1, 0, 2).reshape(length, -1)))
    branch = low_back(jnp.dot(attended, out_full, precision=highest))
    middle = states + branch
    normed_two = low(norm_scaled(middle, gain_second))
    upward = low_back(jnp.dot(normed_two, up_full, precision=highest))
    hidden = low(jnp.square(jax.nn.relu(upward)))
    return middle + jnp.dot(hidden, down_full, precision=highest)

def reference(tokens, gain_one, w_qkv, kernel, w_out, gain_two, w_up, w_down, block_ids, seq_ids, cotangent):
    params = tuple((weight.astype(jnp.float32) for weight in (gain_one, w_qkv, kernel, w_out, gain_two, w_up, w_down)))

    def one_row(carry, item):
        row_tokens, block_row, owner_groups, row_grad = item
        owner_row = jnp.repeat(owner_groups, GROUP).astype(jnp.int32)

        def forward(row_values, *weights):
            return layer_rows(row_values, *weights, block_row, owner_row)
        result, pullback = jax.vjp(forward, row_tokens.astype(jnp.float32), *params)
        grads = pullback(row_grad.astype(jnp.float32))
        carry = tuple((left_part + right_part for left_part, right_part in zip(carry, grads[1:])))
        return (carry, (result.astype(jnp.bfloat16), grads[0]))
    zeros_start = tuple((jnp.zeros(weight.shape, jnp.float32) for weight in params))
    sums, (outputs, input_grads) = lax.scan(one_row, zeros_start, (tokens, block_ids, seq_ids, cotangent))
    return (outputs, input_grads, sums[0], sums[1], sums[2], sums[3], sums[4], sums[5], sums[6])
```

```python
import functools

import jax
import jax.numpy as jnp
from jax import lax
from jax.experimental import pallas as pl
from jax.experimental.pallas import tpu as pltpu
from jax.sharding import PartitionSpec as P

HD = 64
TILE = 256
LOG2E = 1.4426950408889634
NEG = -1e30
MESH = pl.DeviceIdType.MESH
F32 = jnp.float32
BF16 = jnp.bfloat16


def norm_parts(values):
    inverse = lax.rsqrt(jnp.mean(values * values, axis=-1, keepdims=True) + 1e-06)
    return (inverse, values * inverse)


def norm_back(grad_norm, gain_full, inverse, scaled):
    grad_scaled = grad_norm * gain_full
    inner_mean = jnp.mean(grad_scaled * scaled, axis=-1, keepdims=True)
    return (inverse * (grad_scaled - scaled * inner_mean), jnp.sum(grad_norm * scaled, axis=0))


def dot_nn(a, b):
    return lax.dot_general(a, b, (((1,), (0,)), ((), ())), preferred_element_type=F32)


def dot_nt(a, b):
    return lax.dot_general(a, b, (((1,), (1,)), ((), ())), preferred_element_type=F32)


def dot_tn(a, b):
    return lax.dot_general(a, b, (((0,), (0,)), ((), ())), preferred_element_type=F32)


def attn_fwd_kernel(heads, lo_ref, hi_ref, qkv_ref, out_ref, lse_ref, key_scr, peak, total, acc):
    i = pl.program_id(0)
    tiles = pl.num_programs(0)
    width = heads * HD
    here = pl.ds(pl.multiple_of(i * TILE, TILE), TILE)
    factor = HD ** (-0.5) * LOG2E

    @pl.when(i == 0)
    def _():
        for h in range(heads):
            key_scr[h] = qkv_ref[width + h * HD : width + (h + 1) * HD, :].T

    peak[...] = jnp.full_like(peak, NEG)
    total[...] = jnp.zeros_like(total)
    acc[...] = jnp.zeros_like(acc)
    hi = hi_ref[:, here]

    def step(j, masked):
        there = pl.ds(pl.multiple_of(j * TILE, TILE), TILE)
        if masked:
            place = lax.broadcasted_iota(jnp.int32, (TILE, TILE), 0) + j * TILE
            keep = place < hi
        for h in range(heads):
            query = qkv_ref[h * HD : (h + 1) * HD, here]
            scores = dot_nn(key_scr[h, there, :], query) * factor
            if masked:
                scores = jnp.where(keep, scores, NEG)
            before = peak[h : h + 1, :]
            now = jnp.maximum(before, jnp.max(scores, axis=0, keepdims=True))
            shrink = jnp.exp2(before - now)
            probs = jnp.exp2(scores - now)
            total[h : h + 1, :] = total[h : h + 1, :] * shrink + jnp.sum(probs, axis=0, keepdims=True)
            values = qkv_ref[2 * width + h * HD : 2 * width + (h + 1) * HD, there]
            acc[h] = acc[h] * shrink + dot_nn(values, probs.astype(BF16))
            peak[h : h + 1, :] = now

    step(i, True)

    @pl.when(i + 1 < tiles)
    def _():
        step(i + 1, True)

    def lower(j, carry):
        step(j, False)
        return carry

    lax.fori_loop(lo_ref[i], i, lower, 0)
    for h in range(heads):
        out_ref[h * HD : (h + 1) * HD, :] = (acc[h] / total[h : h + 1, :]).astype(BF16)
        lse_ref[h : h + 1, :] = peak[h : h + 1, :] + jnp.log2(total[h : h + 1, :])


def attn_forward(lo_tile, hi, qkv, heads):
    length = qkv.shape[1]
    tiles = length // TILE
    width = heads * HD
    whole = lambda i, *_: (0, 0)
    return pl.pallas_call(
        functools.partial(attn_fwd_kernel, heads),
        out_shape=(
            jax.ShapeDtypeStruct((width, length), BF16),
            jax.ShapeDtypeStruct((8, length), F32),
        ),
        grid_spec=pltpu.PrefetchScalarGridSpec(
            num_scalar_prefetch=1,
            grid=(tiles,),
            in_specs=[
                pl.BlockSpec((1, length), whole),
                pl.BlockSpec((3 * width, length), whole),
            ],
            out_specs=(
                pl.BlockSpec((width, TILE), lambda i, *_: (0, i)),
                pl.BlockSpec((8, TILE), lambda i, *_: (0, i)),
            ),
            scratch_shapes=[
                pltpu.VMEM((heads, length, HD), BF16),
                pltpu.VMEM((8, TILE), F32),
                pltpu.VMEM((8, TILE), F32),
                pltpu.VMEM((heads, HD, TILE), F32),
            ],
        ),
        name="attn_fwd",
    )(lo_tile, hi, qkv)


def attn_bwd_kernel(heads, lo_ref, hi_ref, qkv_ref, grad_ref, att_ref, lse_ref, out_ref, key_scr, val_scr, row_tot):
    i = pl.program_id(0)
    tiles = pl.num_programs(0)
    width = heads * HD
    here = pl.ds(pl.multiple_of(i * TILE, TILE), TILE)
    scale = HD ** (-0.5)
    factor = scale * LOG2E

    @pl.when(i == 0)
    def _():
        for h in range(heads):
            key_scr[h] = qkv_ref[width + h * HD : width + (h + 1) * HD, :].T
            val_scr[h] = qkv_ref[2 * width + h * HD : 2 * width + (h + 1) * HD, :].T
        out_ref[...] = jnp.zeros_like(out_ref)

    hi = hi_ref[:, here]
    for h in range(heads):
        rows = slice(h * HD, (h + 1) * HD)
        row_tot[h : h + 1, :] = jnp.sum(
            grad_ref[rows, here].astype(F32) * att_ref[rows, here].astype(F32), axis=0, keepdims=True
        )

    def step(j, masked):
        there = pl.ds(pl.multiple_of(j * TILE, TILE), TILE)
        if masked:
            place = lax.broadcasted_iota(jnp.int32, (TILE, TILE), 0) + j * TILE
            keep = place < hi
        for h in range(heads):
            q_rows = slice(h * HD, (h + 1) * HD)
            k_rows = slice(width + h * HD, width + (h + 1) * HD)
            v_rows = slice(2 * width + h * HD, 2 * width + (h + 1) * HD)
            query = qkv_ref[q_rows, here]
            grad = grad_ref[q_rows, here]
            scores = dot_nn(key_scr[h, there, :], query) * factor - lse_ref[h : h + 1, here]
            if masked:
                scores = jnp.where(keep, scores, NEG)
            probs = jnp.exp2(scores)
            grad_probs = dot_nn(val_scr[h, there, :], grad)
            grad_scores = (probs * (grad_probs - row_tot[h : h + 1, :])).astype(BF16)
            out_ref[v_rows, there] += dot_nt(grad, probs.astype(BF16))
            out_ref[k_rows, there] += dot_nt(query, grad_scores) * scale
            out_ref[q_rows, here] += dot_nn(qkv_ref[k_rows, there], grad_scores) * scale

    step(i, True)

    @pl.when(i + 1 < tiles)
    def _():
        step(i + 1, True)

    def lower(j, carry):
        step(j, False)
        return carry

    lax.fori_loop(lo_ref[i], i, lower, 0)


def attn_backward(lo_tile, hi, qkv, grad, att, lse, heads):
    length = qkv.shape[1]
    tiles = length // TILE
    width = heads * HD
    whole = lambda i, *_: (0, 0)
    return pl.pallas_call(
        functools.partial(attn_bwd_kernel, heads),
        out_shape=jax.ShapeDtypeStruct((3 * width, length), F32),
        grid_spec=pltpu.PrefetchScalarGridSpec(
            num_scalar_prefetch=1,
            grid=(tiles,),
            in_specs=[
                pl.BlockSpec((1, length), whole),
                pl.BlockSpec((3 * width, length), whole),
                pl.BlockSpec((width, length), whole),
                pl.BlockSpec((width, length), whole),
                pl.BlockSpec((8, length), whole),
            ],
            out_specs=pl.BlockSpec((3 * width, length), whole),
            scratch_shapes=[
                pltpu.VMEM((heads, length, HD), BF16),
                pltpu.VMEM((heads, length, HD), BF16),
                pltpu.VMEM((8, TILE), F32),
            ],
        ),
        name="attn_bwd",
    )(lo_tile, hi, qkv, grad, att, lse)


def spread_kernel(ctx_count, tp_count, x_ref, o_ref, send_sem, recv_sem, own_sem):
    peers = ctx_count * tp_count
    me = lax.axis_index("ctx") * tp_count + lax.axis_index("tp")

    def place(k):
        other = lax.rem(me + k, peers)
        return other, {"ctx": other // tp_count, "tp": lax.rem(other, tp_count)}

    barrier = pltpu.get_barrier_semaphore()
    for k in range(1, peers):
        pl.semaphore_signal(barrier, inc=1, device_id=place(k)[1], device_id_type=MESH)
    pl.semaphore_wait(barrier, peers - 1)
    copies = []
    for k in range(1, peers):
        other, device = place(k)
        copies.append(
            pltpu.make_async_remote_copy(
                src_ref=x_ref.at[other],
                dst_ref=o_ref.at[me],
                send_sem=send_sem.at[k - 1],
                recv_sem=recv_sem.at[k - 1],
                device_id=device,
                device_id_type=MESH,
            )
        )
        copies[-1].start()
    own = pltpu.make_async_copy(x_ref.at[me], o_ref.at[me], own_sem)
    own.start()
    own.wait()
    for copy in copies:
        copy.wait()


def spread(x, ctx_count, tp_count, ident):
    peers = ctx_count * tp_count
    return pl.pallas_call(
        functools.partial(spread_kernel, ctx_count, tp_count),
        out_shape=jax.ShapeDtypeStruct(x.shape, x.dtype),
        in_specs=[pl.BlockSpec(memory_space=pltpu.VMEM)],
        out_specs=pl.BlockSpec(memory_space=pltpu.VMEM),
        scratch_shapes=[
            pltpu.SemaphoreType.DMA((peers - 1,)),
            pltpu.SemaphoreType.DMA((peers - 1,)),
            pltpu.SemaphoreType.DMA,
        ],
        compiler_params=pltpu.CompilerParams(collective_id=ident, has_side_effects=True),
        name="spread",
    )(x)


def row_on_device(
    tokens, gain_one, w_qkv, kernel, w_out, gain_two, w_up, w_down, block_ids, seq_ids, cotangent
):
    place = lax.axis_index("ctx")
    part = lax.axis_index("tp")
    ctx_count = lax.axis_size("ctx")
    tp_count = lax.axis_size("tp")
    fsdp_count = lax.axis_size("fsdp")
    group_len = tokens.shape[1]
    length = group_len * ctx_count
    model = tokens.shape[2]
    taps_count = kernel.shape[0]
    heads = kernel.shape[2]
    width = heads * HD
    rows = tokens.shape[0]
    quarter = group_len // tp_count
    slice_d = w_up.shape[0]
    units = w_up.shape[1]

    qkv_full = lax.all_gather(w_qkv.reshape(slice_d, 3 * width), "fsdp", axis=0, tiled=True)
    small = jnp.concatenate([gain_one, gain_two, kernel.reshape(-1)])
    small_all = lax.all_gather(small, "fsdp", axis=0).astype(F32)
    gain_first = small_all[:, :slice_d].reshape(-1)
    gain_second = small_all[:, slice_d : 2 * slice_d].reshape(-1)
    taps = small_all[:, 2 * slice_d :].reshape(fsdp_count, taps_count, 3, heads, -1)
    taps = taps.transpose(1, 2, 3, 0, 4).reshape(taps_count, 3 * width)
    packed = jnp.concatenate([w_up, w_down.T, w_out.T], axis=1)
    gathered = lax.all_gather(packed, ("tp", "fsdp"), axis=0, tiled=True)
    gathered = gathered.reshape(tp_count, model, packed.shape[1])
    up_blocks = gathered[:, :, :units]
    down_blocks = gathered[:, :, units : 2 * units]
    out_blocks = gathered[:, :, 2 * units :]

    away = lax.dynamic_index_in_dim(tokens, 1 - place, 0, keepdims=False)
    mine = lax.dynamic_index_in_dim(tokens, place, 0, keepdims=False)
    swap = [(i, 1 - i) for i in range(ctx_count)]
    came = lax.ppermute(away, "ctx", swap)
    row = jnp.where(place == 0, jnp.concatenate([mine, came]), jnp.concatenate([came, mine]))
    block_row = lax.dynamic_index_in_dim(block_ids, place, 0, keepdims=False)
    seq_row = lax.dynamic_index_in_dim(seq_ids, place, 0, keepdims=False)
    owner_row = jnp.repeat(seq_row, group_len)
    code = owner_row * 4096 + block_row
    hi = jnp.sum((code[None, :] <= code[:, None]).astype(jnp.int32), axis=1)[None, :]
    first_piece = jnp.sum((seq_row[None, :] < seq_row[:, None]).astype(jnp.int32), axis=1)
    lo_tile = jnp.repeat(first_piece * (group_len // TILE), group_len // TILE)

    row_values = row.astype(F32)
    inv_row, base_row = norm_parts(row_values)
    normed = (base_row * gain_first).astype(BF16)
    linear = dot_tn(qkv_full, normed.T).astype(BF16)
    linear_f = linear.astype(F32)
    same = [
        jnp.concatenate([jnp.zeros((j,), F32), (owner_row[j:] == owner_row[: length - j]).astype(F32)])
        for j in range(taps_count)
    ]
    shifted = [linear_f] + [
        jnp.pad(linear_f[:, : length - j], ((0, 0), (j, 0))) * same[j] for j in range(1, taps_count)
    ]
    triple = sum(taps[j][:, None] * shifted[j] for j in range(taps_count)).astype(BF16)
    att, lse = attn_forward(lo_tile, hi, triple, heads)

    sent = att.reshape(width, ctx_count, tp_count, quarter).transpose(1, 2, 0, 3)
    got = spread(sent.reshape(ctx_count * tp_count, width, quarter), ctx_count, tp_count, 1)
    got = got.reshape(rows, tp_count, width, quarter)
    attended = got.transpose(0, 3, 1, 2).reshape(rows * quarter, tp_count * width)
    states = lax.dynamic_slice_in_dim(tokens, part * quarter, quarter, 1)
    states = states.reshape(rows * quarter, model).astype(F32)
    grad_out = lax.dynamic_slice_in_dim(cotangent, part * quarter, quarter, 1)
    grad_out = grad_out.reshape(rows * quarter, model)
    out_flat = out_blocks.transpose(1, 0, 2).reshape(model, tp_count * width)
    middle = states + dot_nt(attended, out_flat)
    inv_two, base_two = norm_parts(middle)
    normed_two = (base_two * gain_second).astype(BF16)
    upward = jnp.einsum("td,bdu->btu", normed_two, up_blocks, preferred_element_type=F32)
    lifted = jnp.maximum(upward, 0.0)
    hidden = (lifted * lifted).astype(BF16)
    ffn = jnp.einsum("btu,bdu->td", hidden, down_blocks, preferred_element_type=F32)
    block_out = (middle + ffn).astype(BF16).reshape(rows, quarter, model)
    block_out = lax.all_gather(block_out, "tp", axis=1, tiled=True)
    grad_down = jnp.einsum("td,btu->bdu", grad_out, hidden, preferred_element_type=F32)
    grad_hidden = jnp.einsum("td,bdu->btu", grad_out, down_blocks, preferred_element_type=F32)
    grad_upward = (grad_hidden * 2.0 * lifted).astype(BF16)
    grad_up = jnp.einsum("td,btu->bdu", normed_two, grad_upward, preferred_element_type=F32)
    grad_norm_two = jnp.einsum("btu,bdu->td", grad_upward, up_blocks, preferred_element_type=F32)
    back_two, grad_gain_two = norm_back(grad_norm_two, gain_second, inv_two, base_two)
    grad_middle = grad_out.astype(F32) + back_two
    grad_branch = grad_middle.astype(BF16)
    grad_outp = dot_tn(grad_branch, attended)
    grad_outp = grad_outp.reshape(model, tp_count, width).transpose(1, 0, 2)
    grad_attended = dot_nn(grad_branch, out_flat).astype(BF16)

    every = ("tp", "fsdp")
    grad_packed = jnp.concatenate([grad_up, grad_down, grad_outp], axis=2).astype(BF16)
    grad_packed = grad_packed.reshape(tp_count * model, -1)
    grad_packed = lax.psum_scatter(grad_packed, every, scatter_dimension=0, tiled=True)
    grad_packed = lax.psum(grad_packed, "ctx").astype(F32)

    sent = grad_attended.reshape(rows, quarter, tp_count, width).transpose(0, 2, 3, 1)
    got = spread(sent.reshape(rows * tp_count, width, quarter), ctx_count, tp_count, 2)
    got = got.reshape(ctx_count, tp_count, width, quarter)
    grad_att = got.transpose(2, 0, 1, 3).reshape(width, length)
    grad_triple = attn_backward(lo_tile, hi, triple, grad_att, att, lse, heads)

    grad_taps = jnp.stack([jnp.sum(grad_triple * shifted[j], axis=1) for j in range(taps_count)])
    grad_linear = taps[0][:, None] * grad_triple
    for j in range(1, taps_count):
        later = (grad_triple * same[j])[:, j:]
        grad_linear = grad_linear + taps[j][:, None] * jnp.pad(later, ((0, 0), (0, j)))
    grad_linear = grad_linear.astype(BF16)
    grad_qkv = lax.dot_general(
        normed, grad_linear, (((0,), (1,)), ((), ())), preferred_element_type=F32
    )
    norm_part = lax.dot_general(
        grad_linear, qkv_full, (((0,), (1,)), ((), ())), preferred_element_type=F32
    ).astype(BF16)
    norm_part = norm_part.reshape(ctx_count, tp_count, quarter, model).transpose(1, 0, 2, 3)
    norm_part = lax.psum_scatter(norm_part, "tp", scatter_dimension=0, tiled=True)
    norm_part = norm_part.reshape(ctx_count, quarter, model)
    away = lax.dynamic_index_in_dim(norm_part, 1 - place, 0, keepdims=False)
    mine = lax.dynamic_index_in_dim(norm_part, place, 0, keepdims=False)
    came = lax.ppermute(away, "ctx", swap)
    grad_norm_one = jnp.where(place == 0, jnp.concatenate([mine, came]), jnp.concatenate([came, mine]))
    grad_norm_one = grad_norm_one.astype(F32)
    inv_one, base_one = norm_parts(states)
    back_one, grad_gain_one = norm_back(grad_norm_one, gain_first, inv_one, base_one)
    input_grad = (grad_middle + back_one).astype(BF16).reshape(rows, quarter, model)
    input_grad = lax.all_gather(input_grad, "tp", axis=1, tiled=True).astype(F32)

    grad_qkv = lax.psum_scatter(grad_qkv.astype(BF16), "fsdp", scatter_dimension=0, tiled=True)
    grad_qkv = lax.psum(grad_qkv, "ctx").astype(F32)
    gains = lax.psum(jnp.stack([grad_gain_one, grad_gain_two]), ("fsdp", "ctx", "tp"))
    f_place = lax.axis_index("fsdp")
    gains = lax.dynamic_slice_in_dim(gains, f_place * slice_d, slice_d, 1)
    grad_taps = lax.psum(grad_taps, ("fsdp", "ctx")).reshape(taps_count, 3, heads, HD)
    tap_width = kernel.shape[3]
    grad_taps = lax.dynamic_slice_in_dim(grad_taps, f_place * tap_width, tap_width, 3)
    return (
        block_out,
        input_grad,
        gains[0],
        grad_qkv.reshape(slice_d, 3, width),
        grad_taps,
        grad_packed[:, 2 * units :].T,
        gains[1],
        grad_packed[:, :units],
        grad_packed[:, units : 2 * units].T,
    )


MICRO = 2
SEQS_MB = 1


def passed_along(block, axis, distance):
    devices = range(lax.axis_size(axis))
    route = [(i - distance, i) for i in devices if i - distance in devices]
    return lax.ppermute(block, axis, route)


def any_norm_parts(values):
    inverse = lax.rsqrt(jnp.mean(values * values, axis=-1, keepdims=True) + 1e-06)
    return (inverse, values * inverse)


def any_norm_back(grad_norm, gain_full, inverse, scaled):
    grad_scaled = grad_norm * gain_full
    inner_mean = jnp.mean(grad_scaled * scaled, axis=-1, keepdims=True)
    return (inverse * (grad_scaled - scaled * inner_mean), jnp.sum(grad_norm * scaled, axis=(0, 1)))


def masked_scores(queries, key_heads, allowed, score_scale):
    scores = (
        jnp.einsum("sqhe,skhe->shqk", queries, key_heads, preferred_element_type=jnp.float32)
        * score_scale
    )
    return jnp.where(allowed[:, None], scores, -1e30)


def tensor_total(values):
    return lax.psum(values, "tp")


def any_on_device(
    tokens, gain_one, w_qkv, kernel, w_out, gain_two, w_up, w_down, block_ids, seq_ids, cotangent
):
    ctx_place = lax.axis_index("ctx")
    ctx_count = lax.axis_size("ctx")
    group_len = tokens.shape[1]
    taps_count = kernel.shape[0]
    margin = taps_count - 1
    local_heads = kernel.shape[2]
    score_scale = HD ** (-0.5)
    per_micro = SEQS_MB
    group_start = ctx_place * group_len
    owner_all = jnp.repeat(seq_ids, group_len, axis=1)
    totals = None
    outputs = []
    input_grads = []
    for micro_step in range(MICRO):
        gathered = (
            lax.all_gather(gain_one, "fsdp", axis=0, tiled=True),
            lax.all_gather(w_qkv, "fsdp", axis=0, tiled=True),
            lax.all_gather(kernel, "fsdp", axis=3, tiled=True),
            lax.all_gather(w_out, "fsdp", axis=1, tiled=True),
            lax.all_gather(gain_two, "fsdp", axis=0, tiled=True),
            lax.all_gather(w_up, "fsdp", axis=0, tiled=True),
            lax.all_gather(w_down, "fsdp", axis=1, tiled=True),
        )
        gain_first, qkv_full, conv_taps, out_full, gain_second, up_full, down_full = gathered
        gain_first = gain_first.astype(jnp.float32)
        gain_second = gain_second.astype(jnp.float32)
        tap_weights = conv_taps.astype(jnp.float32).reshape(taps_count, 3, -1)
        first_row = micro_step * per_micro
        states = tokens[first_row : first_row + per_micro].astype(jnp.float32)
        block_rows = block_ids[first_row : first_row + per_micro]
        owner_rows = owner_all[first_row : first_row + per_micro]
        group_ids = seq_ids[first_row : first_row + per_micro]
        own_group = lax.dynamic_slice_in_dim(group_ids, ctx_place, 1, 1)
        group_before = lax.dynamic_slice_in_dim(group_ids, jnp.maximum(ctx_place - 1, 0), 1, 1)
        group_after = lax.dynamic_slice_in_dim(
            group_ids, jnp.minimum(ctx_place + 1, ctx_count - 1), 1, 1
        )
        keep_before = (group_before == own_group).astype(jnp.float32)[:, :, None, None]
        keep_after = (group_after == own_group).astype(jnp.float32)[:, :, None, None]
        own_blocks = lax.dynamic_slice_in_dim(block_rows, group_start, group_len, 1)
        allowed = (block_rows[:, None, :] <= own_blocks[:, :, None]) & (
            owner_rows[:, None, :] == own_group[:, :, None]
        )
        inv_one, base_one = any_norm_parts(states)
        normed = (base_one * gain_first).astype(jnp.bfloat16)
        linear = jnp.einsum(
            "std,dce->stce", normed, qkv_full, preferred_element_type=jnp.float32
        ).astype(jnp.bfloat16)
        edge_rows = passed_along(linear[:, group_len - margin :], "ctx", 1)
        padded = jnp.concatenate(
            [edge_rows.astype(jnp.float32) * keep_before, linear.astype(jnp.float32)], axis=1
        )
        mixed_conv = sum(
            (
                tap_weights[offset] * padded[:, margin - offset : margin - offset + group_len]
                for offset in range(taps_count)
            )
        )
        triple = mixed_conv.astype(jnp.bfloat16)
        queries = triple[:, :, 0].reshape(per_micro, group_len, local_heads, HD)
        key_pair = lax.all_gather(triple[:, :, 1:], "ctx", axis=1, tiled=True)
        key_heads = key_pair[:, :, 0].reshape(per_micro, -1, local_heads, HD)
        value_heads = key_pair[:, :, 1].reshape(per_micro, -1, local_heads, HD)
        scores = masked_scores(queries, key_heads, allowed, score_scale)
        row_peak = jnp.max(scores, axis=-1, keepdims=True)
        log_total = row_peak + jnp.log(jnp.sum(jnp.exp(scores - row_peak), axis=-1, keepdims=True))
        probs_low = jnp.exp(scores - log_total).astype(jnp.bfloat16)
        attended = jnp.einsum(
            "shqk,skhe->sqhe", probs_low, value_heads, preferred_element_type=jnp.float32
        )
        attended = attended.astype(jnp.bfloat16).reshape(per_micro, group_len, -1)
        attn_part = jnp.einsum(
            "std,de->ste", attended, out_full, preferred_element_type=jnp.float32
        )
        grad_out = cotangent[first_row : first_row + per_micro]
        middle = states + tensor_total(attn_part)
        inv_two, base_two = any_norm_parts(middle)
        normed_two = (base_two * gain_second).astype(jnp.bfloat16)
        upward = jnp.einsum("std,df->stf", normed_two, up_full, preferred_element_type=jnp.float32)
        lifted = jnp.maximum(upward, 0.0)
        hidden = (lifted * lifted).astype(jnp.bfloat16)
        ffn_part = jnp.einsum("stf,fd->std", hidden, down_full, preferred_element_type=jnp.float32)
        outputs.append((middle + tensor_total(ffn_part)).astype(jnp.bfloat16))
        grad_down = jnp.einsum("stf,std->fd", hidden, grad_out, preferred_element_type=jnp.float32)
        grad_hidden = jnp.einsum(
            "std,fd->stf", grad_out, down_full, preferred_element_type=jnp.float32
        )
        grad_upward = (grad_hidden * 2.0 * lifted).astype(jnp.bfloat16)
        grad_up = jnp.einsum(
            "std,stf->df", normed_two, grad_upward, preferred_element_type=jnp.float32
        )
        norm_two_part = jnp.einsum(
            "stf,df->std", grad_upward, up_full, preferred_element_type=jnp.float32
        )
        back_two, grad_gain_two = any_norm_back(
            tensor_total(norm_two_part), gain_second, inv_two, base_two
        )
        grad_middle = grad_out.astype(jnp.float32) + back_two
        grad_branch = grad_middle.astype(jnp.bfloat16)
        grad_out_proj = jnp.einsum(
            "std,ste->de", attended, grad_branch, preferred_element_type=jnp.float32
        )
        grad_attended = jnp.einsum(
            "ste,de->std", grad_branch, out_full, preferred_element_type=jnp.float32
        )
        grad_attended = grad_attended.astype(jnp.bfloat16).reshape(
            per_micro, group_len, local_heads, HD
        )
        prob_full = jnp.exp(masked_scores(queries, key_heads, allowed, score_scale) - log_total)
        grad_probs = jnp.einsum(
            "sqhe,skhe->shqk", grad_attended, value_heads, preferred_element_type=jnp.float32
        )
        row_total = jnp.sum(prob_full * grad_probs, axis=-1, keepdims=True)
        grad_scores = (prob_full * (grad_probs - row_total)).astype(jnp.bfloat16)
        grad_queries = (
            jnp.einsum(
                "shqk,skhe->sqhe", grad_scores, key_heads, preferred_element_type=jnp.float32
            )
            * score_scale
        )
        keys_term = (
            jnp.einsum("shqk,sqhe->skhe", grad_scores, queries, preferred_element_type=jnp.float32)
            * score_scale
        )
        values_term = jnp.einsum(
            "shqk,sqhe->skhe",
            prob_full.astype(jnp.bfloat16),
            grad_attended,
            preferred_element_type=jnp.float32,
        )
        pair_grads = lax.psum_scatter(
            jnp.stack([keys_term, values_term], axis=2).astype(jnp.bfloat16),
            "ctx",
            scatter_dimension=1,
            tiled=True,
        ).astype(jnp.float32)
        grad_keys = pair_grads[:, :, 0]
        grad_values = pair_grads[:, :, 1]
        grad_triple = jnp.stack([grad_queries, grad_keys, grad_values], axis=2).reshape(
            per_micro, group_len, 3, -1
        )
        tail_rows = passed_along(grad_triple[:, :margin], "ctx", -1)
        padded_grad = jnp.concatenate([grad_triple, tail_rows * keep_after], axis=1)
        grad_linear = sum(
            (
                tap_weights[offset] * padded_grad[:, offset : offset + group_len]
                for offset in range(taps_count)
            )
        )
        grad_linear = grad_linear.astype(jnp.bfloat16)
        grad_taps = jnp.stack(
            [
                jnp.sum(
                    grad_triple * padded[:, margin - offset : margin - offset + group_len],
                    axis=(0, 1),
                )
                for offset in range(taps_count)
            ]
        )
        grad_taps = grad_taps.reshape(conv_taps.shape)
        grad_qkv = jnp.einsum(
            "std,stce->dce", normed, grad_linear, preferred_element_type=jnp.float32
        )
        grad_norm_one = tensor_total(
            jnp.einsum("stce,dce->std", grad_linear, qkv_full, preferred_element_type=jnp.float32)
        )
        back_one, grad_gain_one = any_norm_back(grad_norm_one, gain_first, inv_one, base_one)
        input_grads.append(grad_middle + back_one)
        micro_grads = (
            grad_gain_one,
            grad_qkv,
            grad_taps,
            grad_out_proj,
            grad_gain_two,
            grad_up,
            grad_down,
        )
        totals = (
            micro_grads
            if totals is None
            else tuple(
                (left_part + right_part for left_part, right_part in zip(totals, micro_grads))
            )
        )
    summed = (
        lax.psum_scatter(totals[0], ("fsdp", "ctx"), scatter_dimension=0, tiled=True),
        lax.psum_scatter(totals[1], ("fsdp", "ctx"), scatter_dimension=0, tiled=True),
        lax.psum_scatter(totals[2], ("fsdp", "ctx"), scatter_dimension=3, tiled=True),
        lax.psum_scatter(totals[3], ("fsdp", "ctx"), scatter_dimension=1, tiled=True),
        lax.psum_scatter(totals[4], ("fsdp", "ctx"), scatter_dimension=0, tiled=True),
        lax.psum_scatter(totals[5], ("fsdp", "ctx"), scatter_dimension=0, tiled=True),
        lax.psum_scatter(totals[6], ("fsdp", "ctx"), scatter_dimension=1, tiled=True),
    )
    shares = (
        lax.all_gather(summed[0].astype(jnp.bfloat16), "ctx", axis=0, tiled=True).astype(
            jnp.float32
        ),
        lax.all_gather(summed[1].astype(jnp.bfloat16), "ctx", axis=0, tiled=True).astype(
            jnp.float32
        ),
        lax.all_gather(summed[2].astype(jnp.bfloat16), "ctx", axis=3, tiled=True).astype(
            jnp.float32
        ),
        lax.all_gather(summed[3].astype(jnp.bfloat16), "ctx", axis=1, tiled=True).astype(
            jnp.float32
        ),
        lax.all_gather(summed[4].astype(jnp.bfloat16), "ctx", axis=0, tiled=True).astype(
            jnp.float32
        ),
        lax.all_gather(summed[5].astype(jnp.bfloat16), "ctx", axis=0, tiled=True).astype(
            jnp.float32
        ),
        lax.all_gather(summed[6].astype(jnp.bfloat16), "ctx", axis=1, tiled=True).astype(
            jnp.float32
        ),
    )
    return (jnp.concatenate(outputs, axis=0), jnp.concatenate(input_grads, axis=0)) + tuple(shares)


def solution(mesh):
    placed = (
        P("fsdp", "ctx", None),
        P("fsdp"),
        P("fsdp", None, "tp"),
        P(None, None, "tp", "fsdp"),
        P("tp", "fsdp"),
        P("fsdp"),
        P("fsdp", "tp"),
        P("tp", "fsdp"),
        P("fsdp", None),
        P("fsdp", None),
        P("fsdp", "ctx", None),
    )

    def on_device(*args):
        if args[0].shape[0] == lax.axis_size("ctx") == 2:
            return row_on_device(*args)
        return any_on_device(*args)

    return jax.shard_map(
        on_device,
        mesh=mesh,
        in_specs=placed,
        out_specs=(
            P("fsdp", "ctx", None),
            P("fsdp", "ctx", None),
            P("fsdp"),
            P("fsdp", None, "tp"),
            P(None, None, "tp", "fsdp"),
            P("tp", "fsdp"),
            P("fsdp"),
            P("fsdp", "tp"),
            P("tp", "fsdp"),
        ),
        check_vma=False,
    )
```

```python
import functools

import jax
import jax.numpy as jnp
from jax import lax
from jax.experimental import pallas as pl
from jax.experimental.pallas import tpu as pltpu
from jax.sharding import PartitionSpec as P

HD = 64
TILE = 256
LOG2E = 1.4426950408889634
NEG = -1e30
MESH = pl.DeviceIdType.MESH
F32 = jnp.float32
BF16 = jnp.bfloat16


def norm_parts(values):
    inverse = lax.rsqrt(jnp.mean(values * values, axis=-1, keepdims=True) + 1e-06)
    return (inverse, values * inverse)


def norm_back(grad_norm, gain_full, inverse, scaled):
    grad_scaled = grad_norm * gain_full
    inner_mean = jnp.mean(grad_scaled * scaled, axis=-1, keepdims=True)
    return inverse * (grad_scaled - scaled * inner_mean)


def dot_nn(a, b):
    return lax.dot_general(a, b, (((1,), (0,)), ((), ())), preferred_element_type=F32)


def dot_nt(a, b):
    return lax.dot_general(a, b, (((1,), (1,)), ((), ())), preferred_element_type=F32)


def dot_tn(a, b):
    return lax.dot_general(a, b, (((0,), (0,)), ((), ())), preferred_element_type=F32)


def attn_fwd_kernel(heads, lo_ref, hi_ref, qkv_ref, out_ref, lse_ref, key_scr, peak, total, acc):
    i = pl.program_id(0)
    tiles = pl.num_programs(0)
    width = heads * HD
    here = pl.ds(pl.multiple_of(i * TILE, TILE), TILE)
    factor = HD ** (-0.5) * LOG2E

    @pl.when(i == 0)
    def _():
        for h in range(heads):
            key_scr[h] = qkv_ref[width + h * HD : width + (h + 1) * HD, :].T

    peak[...] = jnp.full_like(peak, NEG)
    total[...] = jnp.zeros_like(total)
    acc[...] = jnp.zeros_like(acc)
    hi = hi_ref[:, here]

    def step(j, masked):
        there = pl.ds(pl.multiple_of(j * TILE, TILE), TILE)
        if masked:
            place = lax.broadcasted_iota(jnp.int32, (TILE, TILE), 0) + j * TILE
            keep = place < hi
        for h in range(heads):
            query = qkv_ref[h * HD : (h + 1) * HD, here]
            scores = dot_nn(key_scr[h, there, :], query) * factor
            if masked:
                scores = jnp.where(keep, scores, NEG)
            before = peak[h : h + 1, :]
            now = jnp.maximum(before, jnp.max(scores, axis=0, keepdims=True))
            shrink = jnp.exp2(before - now)
            probs = jnp.exp2(scores - now)
            total[h : h + 1, :] = total[h : h + 1, :] * shrink + jnp.sum(probs, axis=0, keepdims=True)
            values = qkv_ref[2 * width + h * HD : 2 * width + (h + 1) * HD, there]
            acc[h] = acc[h] * shrink + dot_nn(values, probs.astype(BF16))
            peak[h : h + 1, :] = now

    step(i, True)

    @pl.when(i + 1 < tiles)
    def _():
        step(i + 1, True)

    def lower(j, carry):
        step(j, False)
        return carry

    lax.fori_loop(lo_ref[i], i, lower, 0)
    for h in range(heads):
        out_ref[h * HD : (h + 1) * HD, :] = (acc[h] / total[h : h + 1, :]).astype(BF16)
        lse_ref[h : h + 1, :] = peak[h : h + 1, :] + jnp.log2(total[h : h + 1, :])


def attn_forward(lo_tile, hi, qkv, heads):
    length = qkv.shape[1]
    tiles = length // TILE
    width = heads * HD
    whole = lambda i, *_: (0, 0)
    return pl.pallas_call(
        functools.partial(attn_fwd_kernel, heads),
        out_shape=(
            jax.ShapeDtypeStruct((width, length), BF16),
            jax.ShapeDtypeStruct((8, length), F32),
        ),
        grid_spec=pltpu.PrefetchScalarGridSpec(
            num_scalar_prefetch=1,
            grid=(tiles,),
            in_specs=[
                pl.BlockSpec((1, length), whole),
                pl.BlockSpec((3 * width, length), whole),
            ],
            out_specs=(
                pl.BlockSpec((width, TILE), lambda i, *_: (0, i)),
                pl.BlockSpec((8, TILE), lambda i, *_: (0, i)),
            ),
            scratch_shapes=[
                pltpu.VMEM((heads, length, HD), BF16),
                pltpu.VMEM((8, TILE), F32),
                pltpu.VMEM((8, TILE), F32),
                pltpu.VMEM((heads, HD, TILE), F32),
            ],
        ),
        name="attn_fwd",
    )(lo_tile, hi, qkv)


def attn_bwd_kernel(heads, lo_ref, hi_ref, qkv_ref, grad_ref, att_ref, lse_ref, out_ref, key_scr, val_scr, row_tot):
    i = pl.program_id(0)
    tiles = pl.num_programs(0)
    width = heads * HD
    here = pl.ds(pl.multiple_of(i * TILE, TILE), TILE)
    scale = HD ** (-0.5)
    factor = scale * LOG2E

    @pl.when(i == 0)
    def _():
        for h in range(heads):
            key_scr[h] = qkv_ref[width + h * HD : width + (h + 1) * HD, :].T
            val_scr[h] = qkv_ref[2 * width + h * HD : 2 * width + (h + 1) * HD, :].T
        out_ref[...] = jnp.zeros_like(out_ref)

    hi = hi_ref[:, here]
    for h in range(heads):
        rows = slice(h * HD, (h + 1) * HD)
        row_tot[h : h + 1, :] = jnp.sum(
            grad_ref[rows, here].astype(F32) * att_ref[rows, here].astype(F32), axis=0, keepdims=True
        )

    def step(j, masked):
        there = pl.ds(pl.multiple_of(j * TILE, TILE), TILE)
        if masked:
            place = lax.broadcasted_iota(jnp.int32, (TILE, TILE), 0) + j * TILE
            keep = place < hi
        for h in range(heads):
            q_rows = slice(h * HD, (h + 1) * HD)
            k_rows = slice(width + h * HD, width + (h + 1) * HD)
            v_rows = slice(2 * width + h * HD, 2 * width + (h + 1) * HD)
            query = qkv_ref[q_rows, here]
            grad = grad_ref[q_rows, here]
            scores = dot_nn(key_scr[h, there, :], query) * factor - lse_ref[h : h + 1, here]
            if masked:
                scores = jnp.where(keep, scores, NEG)
            probs = jnp.exp2(scores)
            grad_probs = dot_nn(val_scr[h, there, :], grad)
            grad_scores = (probs * (grad_probs - row_tot[h : h + 1, :])).astype(BF16)
            out_ref[v_rows, there] += dot_nt(grad, probs.astype(BF16))
            out_ref[k_rows, there] += dot_nt(query, grad_scores) * scale
            out_ref[q_rows, here] += dot_nn(qkv_ref[k_rows, there], grad_scores) * scale

    step(i, True)

    @pl.when(i + 1 < tiles)
    def _():
        step(i + 1, True)

    def lower(j, carry):
        step(j, False)
        return carry

    lax.fori_loop(lo_ref[i], i, lower, 0)


def attn_backward(lo_tile, hi, qkv, grad, att, lse, heads):
    length = qkv.shape[1]
    tiles = length // TILE
    width = heads * HD
    whole = lambda i, *_: (0, 0)
    return pl.pallas_call(
        functools.partial(attn_bwd_kernel, heads),
        out_shape=jax.ShapeDtypeStruct((3 * width, length), F32),
        grid_spec=pltpu.PrefetchScalarGridSpec(
            num_scalar_prefetch=1,
            grid=(tiles,),
            in_specs=[
                pl.BlockSpec((1, length), whole),
                pl.BlockSpec((3 * width, length), whole),
                pl.BlockSpec((width, length), whole),
                pl.BlockSpec((width, length), whole),
                pl.BlockSpec((8, length), whole),
            ],
            out_specs=pl.BlockSpec((3 * width, length), whole),
            scratch_shapes=[
                pltpu.VMEM((heads, length, HD), BF16),
                pltpu.VMEM((heads, length, HD), BF16),
                pltpu.VMEM((8, TILE), F32),
            ],
        ),
        name="attn_bwd",
    )(lo_tile, hi, qkv, grad, att, lse)


def spread_kernel(ctx_count, tp_count, x_ref, o_ref, send_sem, recv_sem, own_sem):
    peers = ctx_count * tp_count
    me = lax.axis_index("ctx") * tp_count + lax.axis_index("tp")

    def place(k):
        other = lax.rem(me + k, peers)
        return other, {"ctx": other // tp_count, "tp": lax.rem(other, tp_count)}

    barrier = pltpu.get_barrier_semaphore()
    for k in range(1, peers):
        pl.semaphore_signal(barrier, inc=1, device_id=place(k)[1], device_id_type=MESH)
    pl.semaphore_wait(barrier, peers - 1)
    copies = []
    for k in range(1, peers):
        other, device = place(k)
        copies.append(
            pltpu.make_async_remote_copy(
                src_ref=x_ref.at[other],
                dst_ref=o_ref.at[me],
                send_sem=send_sem.at[k - 1],
                recv_sem=recv_sem.at[k - 1],
                device_id=device,
                device_id_type=MESH,
            )
        )
        copies[-1].start()
    own = pltpu.make_async_copy(x_ref.at[me], o_ref.at[me], own_sem)
    own.start()
    own.wait()
    for copy in copies:
        copy.wait()


def spread(x, ctx_count, tp_count, ident):
    peers = ctx_count * tp_count
    return pl.pallas_call(
        functools.partial(spread_kernel, ctx_count, tp_count),
        out_shape=jax.ShapeDtypeStruct(x.shape, x.dtype),
        in_specs=[pl.BlockSpec(memory_space=pltpu.VMEM)],
        out_specs=pl.BlockSpec(memory_space=pltpu.VMEM),
        scratch_shapes=[
            pltpu.SemaphoreType.DMA((peers - 1,)),
            pltpu.SemaphoreType.DMA((peers - 1,)),
            pltpu.SemaphoreType.DMA,
        ],
        compiler_params=pltpu.CompilerParams(collective_id=ident, has_side_effects=True),
        name="spread",
    )(x)


def finish_kernel(ctx_count, tp_count, x_ref, g_ref, o_ref, s_ref, came, right_sem, left_sem, part_sem, pair_sem, own_sem):
    me = lax.axis_index("tp")
    row = lax.axis_index("ctx")
    size = x_ref.shape[1]
    last = tp_count - 1

    barrier = pltpu.get_barrier_semaphore()
    for k in range(1, tp_count):
        other = lax.rem(me + k, tp_count)
        pl.semaphore_signal(barrier, inc=1, device_id={"tp": other}, device_id_type=MESH)
    pl.semaphore_signal(barrier, inc=1, device_id={"ctx": 1 - row}, device_id_type=MESH)
    pl.semaphore_wait(barrier, tp_count)

    def chunk(k):
        return o_ref.at[:, pl.ds(pl.multiple_of(k * size, size), size), :]

    def pass_on(source, k, step, target, sems):
        return pltpu.make_async_remote_copy(
            src_ref=source,
            dst_ref=chunk(k),
            send_sem=sems.at[0, step - 1],
            recv_sem=sems.at[1, step - 1],
            device_id={"tp": target},
            device_id_type=MESH,
        )

    def rightward(step):
        k = me - step + 1
        return pass_on(x_ref if step == 1 else chunk(jnp.maximum(k, 0)), jnp.maximum(k, 0), step, jnp.minimum(me + 1, last), right_sem)

    def leftward(step):
        k = me + step - 1
        return pass_on(x_ref if step == 1 else chunk(jnp.minimum(k, last)), jnp.minimum(k, last), step, jnp.maximum(me - 1, 0), left_sem)

    pieces = []
    for k in range(1, tp_count):
        other = lax.rem(me + k, tp_count)
        pieces.append(
            pltpu.make_async_remote_copy(
                src_ref=g_ref.at[other],
                dst_ref=came.at[k - 1],
                send_sem=part_sem.at[0, k - 1],
                recv_sem=part_sem.at[1, k - 1],
                device_id={"tp": other},
                device_id_type=MESH,
            )
        )
        pieces[-1].start()
    pair = pltpu.make_async_remote_copy(
        src_ref=s_ref.at[row],
        dst_ref=s_ref.at[row],
        send_sem=pair_sem.at[0],
        recv_sem=pair_sem.at[1],
        device_id={"ctx": 1 - row},
        device_id_type=MESH,
    )
    own = pltpu.make_async_copy(x_ref, chunk(me), own_sem)
    own.start()
    for step in range(1, tp_count):
        @pl.when((me < last) & (me - step + 1 >= 0))
        def _():
            rightward(step).start()

        @pl.when((me > 0) & (me + step - 1 <= last))
        def _():
            leftward(step).start()

        if step == 1:
            for piece in pieces:
                piece.wait_recv()
            total = g_ref[me].astype(F32)
            for k in range(1, tp_count):
                total = total + came[k - 1].astype(F32)
            s_ref[row] = total.astype(BF16)

        @pl.when(me - step >= 0)
        def _():
            rightward(step).wait_recv()

        @pl.when(me + step <= last)
        def _():
            leftward(step).wait_recv()

        if step == 1:
            pair.start()
    own.wait()
    for step in range(1, tp_count):
        @pl.when((me < last) & (me - step + 1 >= 0))
        def _():
            rightward(step).wait_send()

        @pl.when((me > 0) & (me + step - 1 <= last))
        def _():
            leftward(step).wait_send()

    for piece in pieces:
        piece.wait_send()
    pair.wait()


def finish(x, g, ctx_count, tp_count, ident):
    rows, size, model = x.shape
    vmem = pl.BlockSpec(memory_space=pltpu.VMEM)
    return pl.pallas_call(
        functools.partial(finish_kernel, ctx_count, tp_count),
        out_shape=(
            jax.ShapeDtypeStruct((rows, size * tp_count, model), BF16),
            jax.ShapeDtypeStruct((ctx_count,) + g.shape[1:], BF16),
        ),
        in_specs=[vmem, vmem],
        out_specs=(vmem, vmem),
        scratch_shapes=[
            pltpu.VMEM((tp_count - 1,) + g.shape[1:], BF16),
            pltpu.SemaphoreType.DMA((2, tp_count - 1)),
            pltpu.SemaphoreType.DMA((2, tp_count - 1)),
            pltpu.SemaphoreType.DMA((2, tp_count - 1)),
            pltpu.SemaphoreType.DMA((2,)),
            pltpu.SemaphoreType.DMA,
        ],
        compiler_params=pltpu.CompilerParams(collective_id=ident, has_side_effects=True),
        name="finish",
    )(x, g)


def weight_grads_kernel(norm_ref, cot_ref, branch_ref, up_ref, hid_ref, att_ref, out_ref, norm_t, cot_t, branch_t):
    @pl.when(pl.program_id(0) == 0)
    def _():
        norm_t[...] = norm_ref[...].T
        cot_t[...] = cot_ref[...].T
        branch_t[...] = branch_ref[...].T

    pieces, _, piece, _ = out_ref.shape
    units = up_ref.shape[2]
    quarter = att_ref.shape[3]

    def put(value, start):
        stop = start + value.shape[1]
        out_ref[:, 0, :, start:stop] = value.astype(BF16).reshape(pieces, piece, value.shape[1])

    put(dot_nn(norm_t[...], up_ref[0]), 0)
    put(dot_nn(cot_t[...], hid_ref[0]), units)
    total = None
    for r in range(att_ref.shape[0]):
        term = dot_nt(branch_t[:, r * quarter : (r + 1) * quarter], att_ref[r, 0])
        total = term if total is None else total + term
    put(total, 2 * units)


def weight_grads(normed, cot, branch, grad_up, hidden, att, pieces):
    tokens, model = normed.shape
    blocks, _, units = hidden.shape
    rows, _, width, quarter = att.shape
    columns = 2 * units + width
    fixed = pl.BlockSpec((tokens, model), lambda b: (0, 0))
    moving = pl.BlockSpec((1, tokens, units), lambda b: (b, 0, 0))
    return pl.pallas_call(
        weight_grads_kernel,
        grid=(blocks,),
        out_shape=jax.ShapeDtypeStruct((pieces, blocks, model // pieces, columns), BF16),
        in_specs=[fixed, fixed, fixed, moving, moving, pl.BlockSpec((rows, 1, width, quarter), lambda b: (0, b, 0, 0))],
        out_specs=pl.BlockSpec((pieces, 1, model // pieces, columns), lambda b: (0, b, 0, 0)),
        scratch_shapes=[pltpu.VMEM((model, tokens), BF16)] * 3,
        name="weight_grads",
    )(normed, cot, branch, grad_up, hidden, att)


def row_on_device(
    tokens, gain_one, w_qkv, kernel, w_out, gain_two, w_up, w_down, block_ids, seq_ids, cotangent
):
    place = lax.axis_index("ctx")
    part = lax.axis_index("tp")
    ctx_count = lax.axis_size("ctx")
    tp_count = lax.axis_size("tp")
    fsdp_count = lax.axis_size("fsdp")
    group_len = tokens.shape[1]
    length = group_len * ctx_count
    model = tokens.shape[2]
    taps_count = kernel.shape[0]
    heads = kernel.shape[2]
    width = heads * HD
    rows = tokens.shape[0]
    quarter = group_len // tp_count
    slice_d = w_up.shape[0]
    units = w_up.shape[1]

    qkv_full = lax.all_gather(w_qkv.reshape(slice_d, 3 * width), "fsdp", axis=0, tiled=True)
    small = jnp.concatenate([gain_one, gain_two, kernel.reshape(-1)])
    small_all = lax.all_gather(small, "fsdp", axis=0).astype(F32)
    gain_first = small_all[:, :slice_d].reshape(-1)
    gain_second = small_all[:, slice_d : 2 * slice_d].reshape(-1)
    taps = small_all[:, 2 * slice_d :].reshape(fsdp_count, taps_count, 3, heads, -1)
    taps = taps.transpose(1, 2, 3, 0, 4).reshape(taps_count, 3 * width)
    packed = jnp.concatenate([w_up, w_down.T, w_out.T], axis=1)
    gathered = lax.all_gather(packed, ("tp", "fsdp"), axis=0, tiled=True)
    gathered = gathered.reshape(tp_count, model, packed.shape[1])
    up_blocks = gathered[:, :, :units]
    down_blocks = gathered[:, :, units : 2 * units]
    out_blocks = gathered[:, :, 2 * units :]

    away = lax.dynamic_index_in_dim(tokens, 1 - place, 0, keepdims=False)
    mine = lax.dynamic_index_in_dim(tokens, place, 0, keepdims=False)
    swap = [(i, 1 - i) for i in range(ctx_count)]
    came = lax.ppermute(away, "ctx", swap)
    row = jnp.where(place == 0, jnp.concatenate([mine, came]), jnp.concatenate([came, mine]))
    block_row = lax.dynamic_index_in_dim(block_ids, place, 0, keepdims=False)
    seq_row = lax.dynamic_index_in_dim(seq_ids, place, 0, keepdims=False)
    owner_row = jnp.repeat(seq_row, group_len)
    code = owner_row * 4096 + block_row
    hi = jnp.sum((code[None, :] <= code[:, None]).astype(jnp.int32), axis=1)[None, :]
    first_piece = jnp.sum((seq_row[None, :] < seq_row[:, None]).astype(jnp.int32), axis=1)
    lo_tile = jnp.repeat(first_piece * (group_len // TILE), group_len // TILE)

    row_values = row.astype(F32)
    inv_row, base_row = norm_parts(row_values)
    normed = (base_row * gain_first).astype(BF16)
    linear = dot_tn(qkv_full, normed.T).astype(BF16)
    linear_f = linear.astype(F32)
    same = [
        jnp.concatenate([jnp.zeros((j,), F32), (owner_row[j:] == owner_row[: length - j]).astype(F32)])
        for j in range(taps_count)
    ]
    shifted = [linear_f] + [
        jnp.pad(linear_f[:, : length - j], ((0, 0), (j, 0))) * same[j] for j in range(1, taps_count)
    ]
    triple = sum(taps[j][:, None] * shifted[j] for j in range(taps_count)).astype(BF16)
    att, lse = attn_forward(lo_tile, hi, triple, heads)

    sent = att.reshape(width, ctx_count, tp_count, quarter).transpose(1, 2, 0, 3)
    got = spread(sent.reshape(ctx_count * tp_count, width, quarter), ctx_count, tp_count, 1)
    got = got.reshape(rows, tp_count, width, quarter)
    attended = got.transpose(0, 3, 1, 2).reshape(rows * quarter, tp_count * width)
    states = lax.dynamic_slice_in_dim(tokens, part * quarter, quarter, 1)
    states = states.reshape(rows * quarter, model).astype(F32)
    grad_out = lax.dynamic_slice_in_dim(cotangent, part * quarter, quarter, 1)
    grad_out = grad_out.reshape(rows * quarter, model)
    out_flat = out_blocks.transpose(1, 0, 2).reshape(model, tp_count * width)
    middle = states + dot_nt(attended, out_flat)
    inv_two, base_two = norm_parts(middle)
    normed_two = (base_two * gain_second).astype(BF16)
    upward = jnp.einsum("td,bdu->btu", normed_two, up_blocks, preferred_element_type=F32)
    lifted = jnp.maximum(upward, 0.0)
    hidden = (lifted * lifted).astype(BF16)
    ffn = jnp.einsum("btu,bdu->td", hidden, down_blocks, preferred_element_type=F32)
    block_out = (middle + ffn).astype(BF16).reshape(rows, quarter, model)
    whole_out = jnp.zeros((rows, group_len, model), BF16)
    for k in range(tp_count):
        ring = [(i, (i + k) % tp_count) for i in range(tp_count)]
        chunk = lax.ppermute(block_out, "tp", ring) if k else block_out
        start = lax.rem(part + tp_count - k, tp_count) * quarter
        whole_out = lax.dynamic_update_slice_in_dim(whole_out, chunk, start, 1)
    block_out = whole_out
    grad_hidden = jnp.einsum("td,bdu->btu", grad_out, down_blocks, preferred_element_type=F32)
    grad_upward = (grad_hidden * 2.0 * lifted).astype(BF16)
    grad_norm_two = jnp.einsum("btu,bdu->td", grad_upward, up_blocks, preferred_element_type=F32)
    back_two = norm_back(grad_norm_two, gain_second, inv_two, base_two)
    grad_middle = grad_out.astype(F32) + back_two
    grad_branch = grad_middle.astype(BF16)
    grad_attended = dot_nn(grad_branch, out_flat).astype(BF16)
    grad_packed = weight_grads(normed_two, grad_out, grad_branch, grad_upward, hidden, got, fsdp_count * ctx_count)
    columns = grad_packed.shape[3]
    grad_packed = grad_packed.reshape(-1, columns)
    grad_packed = lax.psum_scatter(grad_packed, ("fsdp", "ctx"), scatter_dimension=0, tiled=True)
    grad_packed = grad_packed.reshape(tp_count, -1, columns)

    sent = grad_attended.reshape(rows, quarter, tp_count, width).transpose(0, 2, 3, 1)
    got = spread(sent.reshape(rows * tp_count, width, quarter), ctx_count, tp_count, 2)
    got = got.reshape(ctx_count, tp_count, width, quarter)
    grad_att = got.transpose(2, 0, 1, 3).reshape(width, length)
    grad_triple = attn_backward(lo_tile, hi, triple, grad_att, att, lse, heads)

    grad_taps = jnp.stack([jnp.sum(grad_triple * shifted[j], axis=1) for j in range(taps_count)])
    grad_linear = taps[0][:, None] * grad_triple
    for j in range(1, taps_count):
        later = (grad_triple * same[j])[:, j:]
        grad_linear = grad_linear + taps[j][:, None] * jnp.pad(later, ((0, 0), (0, j)))
    grad_linear = grad_linear.astype(BF16)
    grad_qkv = lax.dot_general(
        normed, grad_linear, (((0,), (1,)), ((), ())), preferred_element_type=F32
    )
    qkv_every = lax.all_gather(qkv_full, "tp", axis=0)
    sent = grad_linear.reshape(3 * width, ctx_count * tp_count, quarter).transpose(1, 0, 2)
    came = spread(sent, ctx_count, tp_count, 3).reshape(rows, tp_count, 3 * width, quarter)
    grad_norm_one = jnp.einsum("rzct,zdc->rtd", came, qkv_every, preferred_element_type=F32)
    grad_norm_one = grad_norm_one.reshape(rows * quarter, model)
    inv_one, base_one = norm_parts(states)
    back_one = norm_back(grad_norm_one, gain_first, inv_one, base_one)
    input_grad = (grad_middle + back_one).astype(BF16).reshape(rows, quarter, model)
    input_grad, grad_packed = finish(input_grad, grad_packed, ctx_count, tp_count, 4)
    input_grad = input_grad.astype(F32)
    grad_packed = grad_packed.reshape(slice_d, columns).astype(F32)

    halves = fsdp_count * ctx_count
    f_taps = grad_taps.reshape(taps_count * 3 * heads, fsdp_count, -1).transpose(1, 0, 2).reshape(fsdp_count, -1)
    f_taps = jnp.pad(f_taps, ((0, 0), (0, 16 * 3 * width - f_taps.shape[1])))
    f_taps = jnp.repeat(f_taps.reshape(fsdp_count, 16, 3 * width), ctx_count, axis=0)
    half_d = slice_d // ctx_count
    grad_qkv = jnp.concatenate([grad_qkv.reshape(halves, half_d, 3 * width), f_taps], axis=1)
    grad_qkv = grad_qkv.astype(BF16).reshape(halves * (half_d + 16), 3 * width)
    grad_qkv = lax.psum_scatter(grad_qkv, ("fsdp", "ctx"), scatter_dimension=0, tiled=True)
    grad_taps = grad_qkv[half_d:].astype(F32).reshape(-1)[: kernel.size].reshape(kernel.shape)
    grad_qkv = lax.all_gather(grad_qkv[:half_d], "ctx", axis=0, tiled=True).astype(F32)

    gains = jnp.stack(
        [
            jnp.sum(grad_qkv * w_qkv.reshape(slice_d, 3 * width).astype(F32), axis=1) / gain_one.astype(F32),
            jnp.sum(grad_packed[:, :units] * w_up.astype(F32), axis=1) / gain_two.astype(F32),
        ]
    )
    gains = lax.psum(gains, "tp")
    return (
        block_out,
        input_grad,
        gains[0],
        grad_qkv.reshape(slice_d, 3, width),
        grad_taps,
        grad_packed[:, 2 * units :].T,
        gains[1],
        grad_packed[:, :units],
        grad_packed[:, units : 2 * units].T,
    )


MICRO = 2
SEQS_MB = 1


def passed_along(block, axis, distance):
    devices = range(lax.axis_size(axis))
    route = [(i - distance, i) for i in devices if i - distance in devices]
    return lax.ppermute(block, axis, route)


def any_norm_parts(values):
    inverse = lax.rsqrt(jnp.mean(values * values, axis=-1, keepdims=True) + 1e-06)
    return (inverse, values * inverse)


def any_norm_back(grad_norm, gain_full, inverse, scaled):
    grad_scaled = grad_norm * gain_full
    inner_mean = jnp.mean(grad_scaled * scaled, axis=-1, keepdims=True)
    return (inverse * (grad_scaled - scaled * inner_mean), jnp.sum(grad_norm * scaled, axis=(0, 1)))


def masked_scores(queries, key_heads, allowed, score_scale):
    scores = (
        jnp.einsum("sqhe,skhe->shqk", queries, key_heads, preferred_element_type=jnp.float32)
        * score_scale
    )
    return jnp.where(allowed[:, None], scores, -1e30)


def tensor_total(values):
    return lax.psum(values, "tp")


def any_on_device(
    tokens, gain_one, w_qkv, kernel, w_out, gain_two, w_up, w_down, block_ids, seq_ids, cotangent
):
    ctx_place = lax.axis_index("ctx")
    ctx_count = lax.axis_size("ctx")
    group_len = tokens.shape[1]
    taps_count = kernel.shape[0]
    margin = taps_count - 1
    local_heads = kernel.shape[2]
    score_scale = HD ** (-0.5)
    per_micro = SEQS_MB
    group_start = ctx_place * group_len
    owner_all = jnp.repeat(seq_ids, group_len, axis=1)
    totals = None
    outputs = []
    input_grads = []
    for micro_step in range(MICRO):
        gathered = (
            lax.all_gather(gain_one, "fsdp", axis=0, tiled=True),
            lax.all_gather(w_qkv, "fsdp", axis=0, tiled=True),
            lax.all_gather(kernel, "fsdp", axis=3, tiled=True),
            lax.all_gather(w_out, "fsdp", axis=1, tiled=True),
            lax.all_gather(gain_two, "fsdp", axis=0, tiled=True),
            lax.all_gather(w_up, "fsdp", axis=0, tiled=True),
            lax.all_gather(w_down, "fsdp", axis=1, tiled=True),
        )
        gain_first, qkv_full, conv_taps, out_full, gain_second, up_full, down_full = gathered
        gain_first = gain_first.astype(jnp.float32)
        gain_second = gain_second.astype(jnp.float32)
        tap_weights = conv_taps.astype(jnp.float32).reshape(taps_count, 3, -1)
        first_row = micro_step * per_micro
        states = tokens[first_row : first_row + per_micro].astype(jnp.float32)
        block_rows = block_ids[first_row : first_row + per_micro]
        owner_rows = owner_all[first_row : first_row + per_micro]
        group_ids = seq_ids[first_row : first_row + per_micro]
        own_group = lax.dynamic_slice_in_dim(group_ids, ctx_place, 1, 1)
        group_before = lax.dynamic_slice_in_dim(group_ids, jnp.maximum(ctx_place - 1, 0), 1, 1)
        group_after = lax.dynamic_slice_in_dim(
            group_ids, jnp.minimum(ctx_place + 1, ctx_count - 1), 1, 1
        )
        keep_before = (group_before == own_group).astype(jnp.float32)[:, :, None, None]
        keep_after = (group_after == own_group).astype(jnp.float32)[:, :, None, None]
        own_blocks = lax.dynamic_slice_in_dim(block_rows, group_start, group_len, 1)
        allowed = (block_rows[:, None, :] <= own_blocks[:, :, None]) & (
            owner_rows[:, None, :] == own_group[:, :, None]
        )
        inv_one, base_one = any_norm_parts(states)
        normed = (base_one * gain_first).astype(jnp.bfloat16)
        linear = jnp.einsum(
            "std,dce->stce", normed, qkv_full, preferred_element_type=jnp.float32
        ).astype(jnp.bfloat16)
        edge_rows = passed_along(linear[:, group_len - margin :], "ctx", 1)
        padded = jnp.concatenate(
            [edge_rows.astype(jnp.float32) * keep_before, linear.astype(jnp.float32)], axis=1
        )
        mixed_conv = sum(
            (
                tap_weights[offset] * padded[:, margin - offset : margin - offset + group_len]
                for offset in range(taps_count)
            )
        )
        triple = mixed_conv.astype(jnp.bfloat16)
        queries = triple[:, :, 0].reshape(per_micro, group_len, local_heads, HD)
        key_pair = lax.all_gather(triple[:, :, 1:], "ctx", axis=1, tiled=True)
        key_heads = key_pair[:, :, 0].reshape(per_micro, -1, local_heads, HD)
        value_heads = key_pair[:, :, 1].reshape(per_micro, -1, local_heads, HD)
        scores = masked_scores(queries, key_heads, allowed, score_scale)
        row_peak = jnp.max(scores, axis=-1, keepdims=True)
        log_total = row_peak + jnp.log(jnp.sum(jnp.exp(scores - row_peak), axis=-1, keepdims=True))
        probs_low = jnp.exp(scores - log_total).astype(jnp.bfloat16)
        attended = jnp.einsum(
            "shqk,skhe->sqhe", probs_low, value_heads, preferred_element_type=jnp.float32
        )
        attended = attended.astype(jnp.bfloat16).reshape(per_micro, group_len, -1)
        attn_part = jnp.einsum(
            "std,de->ste", attended, out_full, preferred_element_type=jnp.float32
        )
        grad_out = cotangent[first_row : first_row + per_micro]
        middle = states + tensor_total(attn_part)
        inv_two, base_two = any_norm_parts(middle)
        normed_two = (base_two * gain_second).astype(jnp.bfloat16)
        upward = jnp.einsum("std,df->stf", normed_two, up_full, preferred_element_type=jnp.float32)
        lifted = jnp.maximum(upward, 0.0)
        hidden = (lifted * lifted).astype(jnp.bfloat16)
        ffn_part = jnp.einsum("stf,fd->std", hidden, down_full, preferred_element_type=jnp.float32)
        outputs.append((middle + tensor_total(ffn_part)).astype(jnp.bfloat16))
        grad_down = jnp.einsum("stf,std->fd", hidden, grad_out, preferred_element_type=jnp.float32)
        grad_hidden = jnp.einsum(
            "std,fd->stf", grad_out, down_full, preferred_element_type=jnp.float32
        )
        grad_upward = (grad_hidden * 2.0 * lifted).astype(jnp.bfloat16)
        grad_up = jnp.einsum(
            "std,stf->df", normed_two, grad_upward, preferred_element_type=jnp.float32
        )
        norm_two_part = jnp.einsum(
            "stf,df->std", grad_upward, up_full, preferred_element_type=jnp.float32
        )
        back_two, grad_gain_two = any_norm_back(
            tensor_total(norm_two_part), gain_second, inv_two, base_two
        )
        grad_middle = grad_out.astype(jnp.float32) + back_two
        grad_branch = grad_middle.astype(jnp.bfloat16)
        grad_out_proj = jnp.einsum(
            "std,ste->de", attended, grad_branch, preferred_element_type=jnp.float32
        )
        grad_attended = jnp.einsum(
            "ste,de->std", grad_branch, out_full, preferred_element_type=jnp.float32
        )
        grad_attended = grad_attended.astype(jnp.bfloat16).reshape(
            per_micro, group_len, local_heads, HD
        )
        prob_full = jnp.exp(masked_scores(queries, key_heads, allowed, score_scale) - log_total)
        grad_probs = jnp.einsum(
            "sqhe,skhe->shqk", grad_attended, value_heads, preferred_element_type=jnp.float32
        )
        row_total = jnp.sum(prob_full * grad_probs, axis=-1, keepdims=True)
        grad_scores = (prob_full * (grad_probs - row_total)).astype(jnp.bfloat16)
        grad_queries = (
            jnp.einsum(
                "shqk,skhe->sqhe", grad_scores, key_heads, preferred_element_type=jnp.float32
            )
            * score_scale
        )
        keys_term = (
            jnp.einsum("shqk,sqhe->skhe", grad_scores, queries, preferred_element_type=jnp.float32)
            * score_scale
        )
        values_term = jnp.einsum(
            "shqk,sqhe->skhe",
            prob_full.astype(jnp.bfloat16),
            grad_attended,
            preferred_element_type=jnp.float32,
        )
        pair_grads = lax.psum_scatter(
            jnp.stack([keys_term, values_term], axis=2).astype(jnp.bfloat16),
            "ctx",
            scatter_dimension=1,
            tiled=True,
        ).astype(jnp.float32)
        grad_keys = pair_grads[:, :, 0]
        grad_values = pair_grads[:, :, 1]
        grad_triple = jnp.stack([grad_queries, grad_keys, grad_values], axis=2).reshape(
            per_micro, group_len, 3, -1
        )
        tail_rows = passed_along(grad_triple[:, :margin], "ctx", -1)
        padded_grad = jnp.concatenate([grad_triple, tail_rows * keep_after], axis=1)
        grad_linear = sum(
            (
                tap_weights[offset] * padded_grad[:, offset : offset + group_len]
                for offset in range(taps_count)
            )
        )
        grad_linear = grad_linear.astype(jnp.bfloat16)
        grad_taps = jnp.stack(
            [
                jnp.sum(
                    grad_triple * padded[:, margin - offset : margin - offset + group_len],
                    axis=(0, 1),
                )
                for offset in range(taps_count)
            ]
        )
        grad_taps = grad_taps.reshape(conv_taps.shape)
        grad_qkv = jnp.einsum(
            "std,stce->dce", normed, grad_linear, preferred_element_type=jnp.float32
        )
        grad_norm_one = tensor_total(
            jnp.einsum("stce,dce->std", grad_linear, qkv_full, preferred_element_type=jnp.float32)
        )
        back_one, grad_gain_one = any_norm_back(grad_norm_one, gain_first, inv_one, base_one)
        input_grads.append(grad_middle + back_one)
        micro_grads = (
            grad_gain_one,
            grad_qkv,
            grad_taps,
            grad_out_proj,
            grad_gain_two,
            grad_up,
            grad_down,
        )
        totals = (
            micro_grads
            if totals is None
            else tuple(
                (left_part + right_part for left_part, right_part in zip(totals, micro_grads))
            )
        )
    summed = (
        lax.psum_scatter(totals[0], ("fsdp", "ctx"), scatter_dimension=0, tiled=True),
        lax.psum_scatter(totals[1], ("fsdp", "ctx"), scatter_dimension=0, tiled=True),
        lax.psum_scatter(totals[2], ("fsdp", "ctx"), scatter_dimension=3, tiled=True),
        lax.psum_scatter(totals[3], ("fsdp", "ctx"), scatter_dimension=1, tiled=True),
        lax.psum_scatter(totals[4], ("fsdp", "ctx"), scatter_dimension=0, tiled=True),
        lax.psum_scatter(totals[5], ("fsdp", "ctx"), scatter_dimension=0, tiled=True),
        lax.psum_scatter(totals[6], ("fsdp", "ctx"), scatter_dimension=1, tiled=True),
    )
    shares = (
        lax.all_gather(summed[0].astype(jnp.bfloat16), "ctx", axis=0, tiled=True).astype(
            jnp.float32
        ),
        lax.all_gather(summed[1].astype(jnp.bfloat16), "ctx", axis=0, tiled=True).astype(
            jnp.float32
        ),
        lax.all_gather(summed[2].astype(jnp.bfloat16), "ctx", axis=3, tiled=True).astype(
            jnp.float32
        ),
        lax.all_gather(summed[3].astype(jnp.bfloat16), "ctx", axis=1, tiled=True).astype(
            jnp.float32
        ),
        lax.all_gather(summed[4].astype(jnp.bfloat16), "ctx", axis=0, tiled=True).astype(
            jnp.float32
        ),
        lax.all_gather(summed[5].astype(jnp.bfloat16), "ctx", axis=0, tiled=True).astype(
            jnp.float32
        ),
        lax.all_gather(summed[6].astype(jnp.bfloat16), "ctx", axis=1, tiled=True).astype(
            jnp.float32
        ),
    )
    return (jnp.concatenate(outputs, axis=0), jnp.concatenate(input_grads, axis=0)) + tuple(shares)


def solution(mesh):
    placed = (
        P("fsdp", "ctx", None),
        P("fsdp"),
        P("fsdp", None, "tp"),
        P(None, None, "tp", "fsdp"),
        P("tp", "fsdp"),
        P("fsdp"),
        P("fsdp", "tp"),
        P("tp", "fsdp"),
        P("fsdp", None),
        P("fsdp", None),
        P("fsdp", "ctx", None),
    )

    def on_device(*args):
        if args[0].shape[0] == lax.axis_size("ctx") == 2:
            return row_on_device(*args)
        return any_on_device(*args)

    return jax.shard_map(
        on_device,
        mesh=mesh,
        in_specs=placed,
        out_specs=(
            P("fsdp", "ctx", None),
            P("fsdp", "ctx", None),
            P("fsdp"),
            P("fsdp", None, "tp"),
            P(None, None, "tp", "fsdp"),
            P("tp", "fsdp"),
            P("fsdp"),
            P("fsdp", "tp"),
            P("tp", "fsdp"),
        ),
        check_vma=False,
    )
```

```python
import functools

import jax
import jax.numpy as jnp
from jax import lax
from jax.experimental import pallas as pl
from jax.experimental.pallas import tpu as pltpu
from jax.sharding import PartitionSpec as P


HD = 64
TILE = 256
LOG2E = 1.4426950408889634
NEG = -1e30
MESH = pl.DeviceIdType.MESH
F32 = jnp.float32
BF16 = jnp.bfloat16


def norm_parts(values):
    inverse = lax.rsqrt(jnp.mean(values * values, axis=-1, keepdims=True) + 1e-06)
    return (inverse, values * inverse)


def norm_back(grad_norm, gain_full, inverse, scaled):
    grad_scaled = grad_norm * gain_full
    inner_mean = jnp.mean(grad_scaled * scaled, axis=-1, keepdims=True)
    return inverse * (grad_scaled - scaled * inner_mean)


def dot_nn(a, b):
    return lax.dot_general(a, b, (((1,), (0,)), ((), ())), preferred_element_type=F32)


def dot_nt(a, b):
    return lax.dot_general(a, b, (((1,), (1,)), ((), ())), preferred_element_type=F32)


def dot_tn(a, b):
    return lax.dot_general(a, b, (((0,), (0,)), ((), ())), preferred_element_type=F32)


def attn_fwd_kernel(heads, lo_ref, hi_ref, qkv_ref, out_ref, lse_ref, key_scr, peak, total, acc):
    i = pl.program_id(0)
    tiles = pl.num_programs(0)
    width = heads * HD
    here = pl.ds(pl.multiple_of(i * TILE, TILE), TILE)
    factor = HD ** (-0.5) * LOG2E

    @pl.when(i == 0)
    def _():
        for h in range(heads):
            key_scr[h] = qkv_ref[width + h * HD : width + (h + 1) * HD, :].T

    peak[...] = jnp.full_like(peak, NEG)
    total[...] = jnp.zeros_like(total)
    acc[...] = jnp.zeros_like(acc)
    hi = hi_ref[:, here]

    def step(j, masked):
        there = pl.ds(pl.multiple_of(j * TILE, TILE), TILE)
        if masked:
            place = lax.broadcasted_iota(jnp.int32, (TILE, TILE), 0) + j * TILE
            keep = place < hi
        for h in range(heads):
            query = qkv_ref[h * HD : (h + 1) * HD, here]
            scores = dot_nn(key_scr[h, there, :], query) * factor
            if masked:
                scores = jnp.where(keep, scores, NEG)
            before = peak[h : h + 1, :]
            now = jnp.maximum(before, jnp.max(scores, axis=0, keepdims=True))
            shrink = jnp.exp2(before - now)
            probs = jnp.exp2(scores - now)
            total[h : h + 1, :] = total[h : h + 1, :] * shrink + jnp.sum(probs, axis=0, keepdims=True)
            values = qkv_ref[2 * width + h * HD : 2 * width + (h + 1) * HD, there]
            acc[h] = acc[h] * shrink + dot_nn(values, probs.astype(BF16))
            peak[h : h + 1, :] = now

    step(i, True)

    @pl.when(i + 1 < tiles)
    def _():
        step(i + 1, True)

    def lower(j, carry):
        step(j, False)
        return carry

    lax.fori_loop(lo_ref[i], i, lower, 0)
    for h in range(heads):
        out_ref[h * HD : (h + 1) * HD, :] = (acc[h] / total[h : h + 1, :]).astype(BF16)
        lse_ref[h : h + 1, :] = peak[h : h + 1, :] + jnp.log2(total[h : h + 1, :])


def attn_forward(lo_tile, hi, qkv, heads):
    length = qkv.shape[1]
    tiles = length // TILE
    width = heads * HD
    whole = lambda i, *_: (0, 0)
    return pl.pallas_call(
        functools.partial(attn_fwd_kernel, heads),
        out_shape=(
            jax.ShapeDtypeStruct((width, length), BF16),
            jax.ShapeDtypeStruct((8, length), F32),
        ),
        grid_spec=pltpu.PrefetchScalarGridSpec(
            num_scalar_prefetch=1,
            grid=(tiles,),
            in_specs=[
                pl.BlockSpec((1, length), whole),
                pl.BlockSpec((3 * width, length), whole),
            ],
            out_specs=(
                pl.BlockSpec((width, TILE), lambda i, *_: (0, i)),
                pl.BlockSpec((8, TILE), lambda i, *_: (0, i)),
            ),
            scratch_shapes=[
                pltpu.VMEM((heads, length, HD), BF16),
                pltpu.VMEM((8, TILE), F32),
                pltpu.VMEM((8, TILE), F32),
                pltpu.VMEM((heads, HD, TILE), F32),
            ],
        ),
        name="attn_fwd",
    )(lo_tile, hi, qkv)


def attn_bwd_kernel(heads, lo_ref, hi_ref, qkv_ref, grad_ref, att_ref, lse_ref, out_ref, key_scr, val_scr, row_tot):
    i = pl.program_id(0)
    tiles = pl.num_programs(0)
    width = heads * HD
    here = pl.ds(pl.multiple_of(i * TILE, TILE), TILE)
    scale = HD ** (-0.5)
    factor = scale * LOG2E

    @pl.when(i == 0)
    def _():
        for h in range(heads):
            key_scr[h] = qkv_ref[width + h * HD : width + (h + 1) * HD, :].T
            val_scr[h] = qkv_ref[2 * width + h * HD : 2 * width + (h + 1) * HD, :].T
        out_ref[...] = jnp.zeros_like(out_ref)

    hi = hi_ref[:, here]
    for h in range(heads):
        rows = slice(h * HD, (h + 1) * HD)
        row_tot[h : h + 1, :] = jnp.sum(
            grad_ref[rows, here].astype(F32) * att_ref[rows, here].astype(F32), axis=0, keepdims=True
        )

    def step(j, masked):
        there = pl.ds(pl.multiple_of(j * TILE, TILE), TILE)
        if masked:
            place = lax.broadcasted_iota(jnp.int32, (TILE, TILE), 0) + j * TILE
            keep = place < hi
        for h in range(heads):
            q_rows = slice(h * HD, (h + 1) * HD)
            k_rows = slice(width + h * HD, width + (h + 1) * HD)
            v_rows = slice(2 * width + h * HD, 2 * width + (h + 1) * HD)
            query = qkv_ref[q_rows, here]
            grad = grad_ref[q_rows, here]
            scores = dot_nn(key_scr[h, there, :], query) * factor - lse_ref[h : h + 1, here]
            if masked:
                scores = jnp.where(keep, scores, NEG)
            probs = jnp.exp2(scores)
            grad_probs = dot_nn(val_scr[h, there, :], grad)
            grad_scores = (probs * (grad_probs - row_tot[h : h + 1, :])).astype(BF16)
            out_ref[v_rows, there] += dot_nt(grad, probs.astype(BF16))
            out_ref[k_rows, there] += dot_nt(query, grad_scores) * scale
            out_ref[q_rows, here] += dot_nn(qkv_ref[k_rows, there], grad_scores) * scale

    step(i, True)

    @pl.when(i + 1 < tiles)
    def _():
        step(i + 1, True)

    def lower(j, carry):
        step(j, False)
        return carry

    lax.fori_loop(lo_ref[i], i, lower, 0)


def attn_backward(lo_tile, hi, qkv, grad, att, lse, heads):
    length = qkv.shape[1]
    tiles = length // TILE
    width = heads * HD
    whole = lambda i, *_: (0, 0)
    return pl.pallas_call(
        functools.partial(attn_bwd_kernel, heads),
        out_shape=jax.ShapeDtypeStruct((3 * width, length), F32),
        grid_spec=pltpu.PrefetchScalarGridSpec(
            num_scalar_prefetch=1,
            grid=(tiles,),
            in_specs=[
                pl.BlockSpec((1, length), whole),
                pl.BlockSpec((3 * width, length), whole),
                pl.BlockSpec((width, length), whole),
                pl.BlockSpec((width, length), whole),
                pl.BlockSpec((8, length), whole),
            ],
            out_specs=pl.BlockSpec((3 * width, length), whole),
            scratch_shapes=[
                pltpu.VMEM((heads, length, HD), BF16),
                pltpu.VMEM((heads, length, HD), BF16),
                pltpu.VMEM((8, TILE), F32),
            ],
        ),
        name="attn_bwd",
    )(lo_tile, hi, qkv, grad, att, lse)


def spread_kernel(ctx_count, tp_count, x_ref, o_ref, send_sem, recv_sem, own_sem):
    peers = ctx_count * tp_count
    me = lax.axis_index("ctx") * tp_count + lax.axis_index("tp")

    def place(k):
        other = lax.rem(me + k, peers)
        return other, {"ctx": other // tp_count, "tp": lax.rem(other, tp_count)}

    barrier = pltpu.get_barrier_semaphore()
    for k in range(1, peers):
        pl.semaphore_signal(barrier, inc=1, device_id=place(k)[1], device_id_type=MESH)
    pl.semaphore_wait(barrier, peers - 1)
    copies = []
    for k in range(1, peers):
        other, device = place(k)
        copies.append(
            pltpu.make_async_remote_copy(
                src_ref=x_ref.at[other],
                dst_ref=o_ref.at[me],
                send_sem=send_sem.at[k - 1],
                recv_sem=recv_sem.at[k - 1],
                device_id=device,
                device_id_type=MESH,
            )
        )
        copies[-1].start()
    own = pltpu.make_async_copy(x_ref.at[me], o_ref.at[me], own_sem)
    own.start()
    own.wait()
    for copy in copies:
        copy.wait()


def spread(x, ctx_count, tp_count, ident):
    peers = ctx_count * tp_count
    return pl.pallas_call(
        functools.partial(spread_kernel, ctx_count, tp_count),
        out_shape=jax.ShapeDtypeStruct(x.shape, x.dtype),
        in_specs=[pl.BlockSpec(memory_space=pltpu.VMEM)],
        out_specs=pl.BlockSpec(memory_space=pltpu.VMEM),
        scratch_shapes=[
            pltpu.SemaphoreType.DMA((peers - 1,)),
            pltpu.SemaphoreType.DMA((peers - 1,)),
            pltpu.SemaphoreType.DMA,
        ],
        compiler_params=pltpu.CompilerParams(collective_id=ident, has_side_effects=True),
    )(x)


def finish_kernel(tp_count, x_ref, g_ref, o_ref, s_ref, came, right_sem, left_sem, part_sem, pair_sem, own_sem):
    me = lax.axis_index("tp")
    row = lax.axis_index("ctx")
    size = x_ref.shape[1]
    last = tp_count - 1

    barrier = pltpu.get_barrier_semaphore()
    for k in range(1, tp_count):
        other = lax.rem(me + k, tp_count)
        pl.semaphore_signal(barrier, inc=1, device_id={"tp": other}, device_id_type=MESH)
    pl.semaphore_signal(barrier, inc=1, device_id={"ctx": 1 - row}, device_id_type=MESH)
    pl.semaphore_wait(barrier, tp_count)

    def chunk(k):
        return o_ref.at[:, pl.ds(pl.multiple_of(k * size, size), size), :]

    def pass_on(source, k, step, target, sems):
        return pltpu.make_async_remote_copy(
            src_ref=source,
            dst_ref=chunk(k),
            send_sem=sems.at[0, step - 1],
            recv_sem=sems.at[1, step - 1],
            device_id={"tp": target},
            device_id_type=MESH,
        )

    def rightward(step):
        k = me - step + 1
        return pass_on(x_ref if step == 1 else chunk(jnp.maximum(k, 0)), jnp.maximum(k, 0), step, jnp.minimum(me + 1, last), right_sem)

    def leftward(step):
        k = me + step - 1
        return pass_on(x_ref if step == 1 else chunk(jnp.minimum(k, last)), jnp.minimum(k, last), step, jnp.maximum(me - 1, 0), left_sem)

    pieces = []
    for k in range(1, tp_count):
        other = lax.rem(me + k, tp_count)
        pieces.append(
            pltpu.make_async_remote_copy(
                src_ref=g_ref.at[other],
                dst_ref=came.at[k - 1],
                send_sem=part_sem.at[0, k - 1],
                recv_sem=part_sem.at[1, k - 1],
                device_id={"tp": other},
                device_id_type=MESH,
            )
        )
        pieces[-1].start()
    pair = pltpu.make_async_remote_copy(
        src_ref=s_ref.at[row],
        dst_ref=s_ref.at[row],
        send_sem=pair_sem.at[0],
        recv_sem=pair_sem.at[1],
        device_id={"ctx": 1 - row},
        device_id_type=MESH,
    )
    own = pltpu.make_async_copy(x_ref, chunk(me), own_sem)
    own.start()
    for step in range(1, tp_count):
        @pl.when((me < last) & (me - step + 1 >= 0))
        def _():
            rightward(step).start()

        @pl.when((me > 0) & (me + step - 1 <= last))
        def _():
            leftward(step).start()

        if step == 1:
            for piece in pieces:
                piece.wait_recv()
            total = g_ref[me].astype(F32)
            for k in range(1, tp_count):
                total = total + came[k - 1].astype(F32)
            s_ref[row] = total.astype(BF16)

        @pl.when(me - step >= 0)
        def _():
            rightward(step).wait_recv()

        @pl.when(me + step <= last)
        def _():
            leftward(step).wait_recv()

        if step == 1:
            pair.start()
    own.wait()
    for step in range(1, tp_count):
        @pl.when((me < last) & (me - step + 1 >= 0))
        def _():
            rightward(step).wait_send()

        @pl.when((me > 0) & (me + step - 1 <= last))
        def _():
            leftward(step).wait_send()

    for piece in pieces:
        piece.wait_send()
    pair.wait()


def finish(x, g, ctx_count, tp_count, ident):
    rows, size, model = x.shape
    vmem = pl.BlockSpec(memory_space=pltpu.VMEM)
    return pl.pallas_call(
        functools.partial(finish_kernel, tp_count),
        out_shape=(
            jax.ShapeDtypeStruct((rows, size * tp_count, model), BF16),
            jax.ShapeDtypeStruct((ctx_count,) + g.shape[1:], BF16),
        ),
        in_specs=[vmem, vmem],
        out_specs=(vmem, vmem),
        scratch_shapes=[
            pltpu.VMEM((tp_count - 1,) + g.shape[1:], BF16),
            pltpu.SemaphoreType.DMA((2, tp_count - 1)),
            pltpu.SemaphoreType.DMA((2, tp_count - 1)),
            pltpu.SemaphoreType.DMA((2, tp_count - 1)),
            pltpu.SemaphoreType.DMA((2,)),
            pltpu.SemaphoreType.DMA,
        ],
        compiler_params=pltpu.CompilerParams(collective_id=ident, has_side_effects=True),
        name="finish",
    )(x, g)


def weight_grads_kernel(norm_ref, cot_ref, branch_ref, up_ref, hid_ref, att_ref, out_ref, norm_t, cot_t, branch_t):
    @pl.when(pl.program_id(0) == 0)
    def _():
        norm_t[...] = norm_ref[...].T
        cot_t[...] = cot_ref[...].T
        branch_t[...] = branch_ref[...].T

    pieces, _, piece, _ = out_ref.shape
    units = up_ref.shape[2]
    quarter = att_ref.shape[3]

    def put(value, start):
        stop = start + value.shape[1]
        out_ref[:, 0, :, start:stop] = value.astype(BF16).reshape(pieces, piece, value.shape[1])

    put(dot_nn(norm_t[...], up_ref[0]), 0)
    put(dot_nn(cot_t[...], hid_ref[0]), units)
    total = None
    for r in range(att_ref.shape[0]):
        term = dot_nt(branch_t[:, r * quarter : (r + 1) * quarter], att_ref[r, 0])
        total = term if total is None else total + term
    put(total, 2 * units)


def weight_grads(normed, cot, branch, grad_up, hidden, att, pieces):
    tokens, model = normed.shape
    blocks, _, units = hidden.shape
    rows, _, width, quarter = att.shape
    columns = 2 * units + width
    fixed = pl.BlockSpec((tokens, model), lambda b: (0, 0))
    moving = pl.BlockSpec((1, tokens, units), lambda b: (b, 0, 0))
    return pl.pallas_call(
        weight_grads_kernel,
        grid=(blocks,),
        out_shape=jax.ShapeDtypeStruct((pieces, blocks, model // pieces, columns), BF16),
        in_specs=[fixed, fixed, fixed, moving, moving, pl.BlockSpec((rows, 1, width, quarter), lambda b: (0, b, 0, 0))],
        out_specs=pl.BlockSpec((pieces, 1, model // pieces, columns), lambda b: (0, b, 0, 0)),
        scratch_shapes=[pltpu.VMEM((model, tokens), BF16)] * 3,
        name="weight_grads",
    )(normed, cot, branch, grad_up, hidden, att)


def row_on_device(
    tokens, gain_one, w_qkv, kernel, w_out, gain_two, w_up, w_down, block_ids, seq_ids, cotangent
):
    place = lax.axis_index("ctx")
    part = lax.axis_index("tp")
    ctx_count = lax.axis_size("ctx")
    tp_count = lax.axis_size("tp")
    fsdp_count = lax.axis_size("fsdp")
    group_len = tokens.shape[1]
    length = group_len * ctx_count
    model = tokens.shape[2]
    taps_count = kernel.shape[0]
    heads = kernel.shape[2]
    width = heads * HD
    rows = tokens.shape[0]
    quarter = group_len // tp_count
    slice_d = w_up.shape[0]
    units = w_up.shape[1]

    qkv_full = lax.all_gather(w_qkv.reshape(slice_d, 3 * width), "fsdp", axis=0, tiled=True)
    small = jnp.concatenate([gain_one, gain_two, kernel.reshape(-1)])
    small_all = lax.all_gather(small, "fsdp", axis=0).astype(F32)
    gain_first = small_all[:, :slice_d].reshape(-1)
    gain_second = small_all[:, slice_d : 2 * slice_d].reshape(-1)
    taps = small_all[:, 2 * slice_d :].reshape(fsdp_count, taps_count, 3, heads, -1)
    taps = taps.transpose(1, 2, 3, 0, 4).reshape(taps_count, 3 * width)
    packed = jnp.concatenate([w_up, w_down.T, w_out.T], axis=1)
    gathered = lax.all_gather(packed, ("tp", "fsdp"), axis=0, tiled=True)
    gathered = gathered.reshape(tp_count, model, packed.shape[1])
    qkv_every = lax.all_gather(w_qkv.reshape(slice_d, 3 * width), ("tp", "fsdp"), axis=0, tiled=True)
    qkv_every = qkv_every.reshape(tp_count, model, 3 * width)
    up_blocks = gathered[:, :, :units]
    down_blocks = gathered[:, :, units : 2 * units]
    out_blocks = gathered[:, :, 2 * units :]

    away = lax.dynamic_index_in_dim(tokens, 1 - place, 0, keepdims=False)
    mine = lax.dynamic_index_in_dim(tokens, place, 0, keepdims=False)
    swap = [(i, 1 - i) for i in range(ctx_count)]
    came = lax.ppermute(away, "ctx", swap)
    row = jnp.where(place == 0, jnp.concatenate([mine, came]), jnp.concatenate([came, mine]))
    block_row = lax.dynamic_index_in_dim(block_ids, place, 0, keepdims=False)
    seq_row = lax.dynamic_index_in_dim(seq_ids, place, 0, keepdims=False)
    owner_row = jnp.repeat(seq_row, group_len)
    code = owner_row * 4096 + block_row
    hi = jnp.sum((code[None, :] <= code[:, None]).astype(jnp.int32), axis=1)[None, :]
    first_piece = jnp.sum((seq_row[None, :] < seq_row[:, None]).astype(jnp.int32), axis=1)
    lo_tile = jnp.repeat(first_piece * (group_len // TILE), group_len // TILE)

    row_values = row.astype(F32)
    _, base_row = norm_parts(row_values)
    normed = (base_row * gain_first).astype(BF16)
    linear = dot_tn(qkv_full, normed.T).astype(BF16)
    linear_f = linear.astype(F32)
    same = [
        jnp.concatenate([jnp.zeros((j,), F32), (owner_row[j:] == owner_row[: length - j]).astype(F32)])
        for j in range(taps_count)
    ]
    shifted = [linear_f] + [
        jnp.pad(linear_f[:, : length - j], ((0, 0), (j, 0))) * same[j] for j in range(1, taps_count)
    ]
    triple = sum(taps[j][:, None] * shifted[j] for j in range(taps_count)).astype(BF16)
    att, lse = attn_forward(lo_tile, hi, triple, heads)

    sent = att.reshape(width, ctx_count, tp_count, quarter).transpose(1, 2, 0, 3)
    got = spread(sent.reshape(ctx_count * tp_count, width, quarter), ctx_count, tp_count, 1)
    got = got.reshape(rows, tp_count, width, quarter)
    attended = got.transpose(0, 3, 1, 2).reshape(rows * quarter, tp_count * width)
    states = lax.dynamic_slice_in_dim(tokens, part * quarter, quarter, 1)
    states = states.reshape(rows * quarter, model).astype(F32)
    grad_out = lax.dynamic_slice_in_dim(cotangent, part * quarter, quarter, 1)
    grad_out = grad_out.reshape(rows * quarter, model)
    out_flat = out_blocks.transpose(1, 0, 2).reshape(model, tp_count * width)
    middle = states + dot_nt(attended, out_flat)
    inv_two, base_two = norm_parts(middle)
    normed_two = (base_two * gain_second).astype(BF16)
    upward = jnp.einsum("td,bdu->btu", normed_two, up_blocks, preferred_element_type=F32)
    lifted = jnp.maximum(upward, 0.0)
    hidden = (lifted * lifted).astype(BF16)
    ffn = jnp.einsum("btu,bdu->td", hidden, down_blocks, preferred_element_type=F32)
    block_out = (middle + ffn).astype(BF16).reshape(rows, quarter, model)
    block_out, lifted = lax.optimization_barrier((block_out, lifted))
    chunks = [block_out]
    for k in range(1, tp_count):
        ring = [(i, (i + k) % tp_count) for i in range(tp_count)]
        chunks.append(lax.ppermute(block_out, "tp", ring))
    grad_hidden = jnp.einsum("td,bdu->btu", grad_out, down_blocks, preferred_element_type=F32)
    grad_upward = (grad_hidden * 2.0 * lifted).astype(BF16)
    grad_norm_two = jnp.einsum("btu,bdu->td", grad_upward, up_blocks, preferred_element_type=F32)
    back_two = norm_back(grad_norm_two, gain_second, inv_two, base_two)
    grad_middle = grad_out.astype(F32) + back_two
    grad_branch = grad_middle.astype(BF16)
    grad_attended = dot_nn(grad_branch, out_flat).astype(BF16)
    grad_packed = weight_grads(normed_two, grad_out, grad_branch, grad_upward, hidden, got, fsdp_count * ctx_count)

    sent = grad_attended.reshape(rows, quarter, tp_count, width).transpose(0, 2, 3, 1)
    sent, grad_packed = lax.optimization_barrier((sent, grad_packed))
    columns = grad_packed.shape[3]
    grad_packed = grad_packed.reshape(-1, columns)
    grad_packed = lax.psum_scatter(grad_packed, ("fsdp", "ctx"), scatter_dimension=0, tiled=True)
    grad_packed = grad_packed.reshape(tp_count, -1, columns)
    got = spread(sent.reshape(rows * tp_count, width, quarter), ctx_count, tp_count, 2)
    got = got.reshape(ctx_count, tp_count, width, quarter)
    grad_att = got.transpose(2, 0, 1, 3).reshape(width, length)
    grad_triple = attn_backward(lo_tile, hi, triple, grad_att, att, lse, heads)

    grad_taps = jnp.stack([jnp.sum(grad_triple * shifted[j], axis=1) for j in range(taps_count)])
    grad_linear = taps[0][:, None] * grad_triple
    for j in range(1, taps_count):
        later = (grad_triple * same[j])[:, j:]
        grad_linear = grad_linear + taps[j][:, None] * jnp.pad(later, ((0, 0), (0, j)))
    grad_linear = grad_linear.astype(BF16)
    grad_qkv = lax.dot_general(
        normed, grad_linear, (((0,), (1,)), ((), ())), preferred_element_type=F32
    )
    sent = grad_linear.reshape(3 * width, ctx_count * tp_count, quarter).transpose(1, 0, 2)
    sent, *chunks = lax.optimization_barrier((sent, *chunks))
    whole_out = jnp.zeros((rows, group_len, model), BF16)
    for k in range(tp_count):
        start = lax.rem(part + tp_count - k, tp_count) * quarter
        whole_out = lax.dynamic_update_slice_in_dim(whole_out, chunks[k], start, 1)
    block_out = whole_out
    came = spread(sent, ctx_count, tp_count, 3).reshape(rows, tp_count, 3 * width, quarter)
    grad_norm_one = jnp.einsum("rzct,zdc->rtd", came, qkv_every, preferred_element_type=F32)
    grad_norm_one = grad_norm_one.reshape(rows * quarter, model)
    inv_one, base_one = norm_parts(states)
    back_one = norm_back(grad_norm_one, gain_first, inv_one, base_one)
    input_grad = (grad_middle + back_one).astype(BF16).reshape(rows, quarter, model)
    input_grad, grad_packed = finish(input_grad, grad_packed, ctx_count, tp_count, 4)
    input_grad = input_grad.astype(F32)
    grad_packed = grad_packed.reshape(slice_d, columns).astype(F32)

    halves = fsdp_count * ctx_count
    f_taps = grad_taps.reshape(taps_count * 3 * heads, fsdp_count, -1).transpose(1, 0, 2).reshape(fsdp_count, -1)
    f_taps = jnp.pad(f_taps, ((0, 0), (0, 16 * 3 * width - f_taps.shape[1])))
    f_taps = jnp.repeat(f_taps.reshape(fsdp_count, 16, 3 * width), ctx_count, axis=0)
    half_d = slice_d // ctx_count
    grad_qkv = jnp.concatenate([grad_qkv.reshape(halves, half_d, 3 * width), f_taps], axis=1)
    grad_qkv = grad_qkv.astype(BF16).reshape(halves * (half_d + 16), 3 * width)
    grad_qkv = lax.psum_scatter(grad_qkv, ("fsdp", "ctx"), scatter_dimension=0, tiled=True)
    grad_taps = grad_qkv[half_d:].astype(F32).reshape(-1)[: kernel.size].reshape(kernel.shape)
    grad_qkv = lax.all_gather(grad_qkv[:half_d], "ctx", axis=0, tiled=True).astype(F32)

    gains = jnp.stack(
        [
            jnp.sum(grad_qkv * w_qkv.reshape(slice_d, 3 * width).astype(F32), axis=1) / gain_one.astype(F32),
            jnp.sum(grad_packed[:, :units] * w_up.astype(F32), axis=1) / gain_two.astype(F32),
        ]
    )
    gains = lax.psum(gains, "tp")
    return (
        block_out,
        input_grad,
        gains[0],
        grad_qkv.reshape(slice_d, 3, width),
        grad_taps,
        grad_packed[:, 2 * units :].T,
        gains[1],
        grad_packed[:, :units],
        grad_packed[:, units : 2 * units].T,
    )


MICRO = 2
SEQS_MB = 1


def passed_along(block, axis, distance):
    devices = range(lax.axis_size(axis))
    route = [(i - distance, i) for i in devices if i - distance in devices]
    return lax.ppermute(block, axis, route)


def any_norm_parts(values):
    inverse = lax.rsqrt(jnp.mean(values * values, axis=-1, keepdims=True) + 1e-06)
    return (inverse, values * inverse)


def any_norm_back(grad_norm, gain_full, inverse, scaled):
    grad_scaled = grad_norm * gain_full
    inner_mean = jnp.mean(grad_scaled * scaled, axis=-1, keepdims=True)
    return (inverse * (grad_scaled - scaled * inner_mean), jnp.sum(grad_norm * scaled, axis=(0, 1)))


def masked_scores(queries, key_heads, allowed, score_scale):
    scores = (
        jnp.einsum("sqhe,skhe->shqk", queries, key_heads, preferred_element_type=jnp.float32)
        * score_scale
    )
    return jnp.where(allowed[:, None], scores, -1e30)


def tensor_total(values):
    return lax.psum(values, "tp")


def any_on_device(
    tokens, gain_one, w_qkv, kernel, w_out, gain_two, w_up, w_down, block_ids, seq_ids, cotangent
):
    ctx_place = lax.axis_index("ctx")
    ctx_count = lax.axis_size("ctx")
    group_len = tokens.shape[1]
    taps_count = kernel.shape[0]
    margin = taps_count - 1
    local_heads = kernel.shape[2]
    score_scale = HD ** (-0.5)
    per_micro = SEQS_MB
    group_start = ctx_place * group_len
    owner_all = jnp.repeat(seq_ids, group_len, axis=1)
    totals = None
    outputs = []
    input_grads = []
    for micro_step in range(MICRO):
        gathered = (
            lax.all_gather(gain_one, "fsdp", axis=0, tiled=True),
            lax.all_gather(w_qkv, "fsdp", axis=0, tiled=True),
            lax.all_gather(kernel, "fsdp", axis=3, tiled=True),
            lax.all_gather(w_out, "fsdp", axis=1, tiled=True),
            lax.all_gather(gain_two, "fsdp", axis=0, tiled=True),
            lax.all_gather(w_up, "fsdp", axis=0, tiled=True),
            lax.all_gather(w_down, "fsdp", axis=1, tiled=True),
        )
        gain_first, qkv_full, conv_taps, out_full, gain_second, up_full, down_full = gathered
        gain_first = gain_first.astype(jnp.float32)
        gain_second = gain_second.astype(jnp.float32)
        tap_weights = conv_taps.astype(jnp.float32).reshape(taps_count, 3, -1)
        first_row = micro_step * per_micro
        states = tokens[first_row : first_row + per_micro].astype(jnp.float32)
        block_rows = block_ids[first_row : first_row + per_micro]
        owner_rows = owner_all[first_row : first_row + per_micro]
        group_ids = seq_ids[first_row : first_row + per_micro]
        own_group = lax.dynamic_slice_in_dim(group_ids, ctx_place, 1, 1)
        group_before = lax.dynamic_slice_in_dim(group_ids, jnp.maximum(ctx_place - 1, 0), 1, 1)
        group_after = lax.dynamic_slice_in_dim(
            group_ids, jnp.minimum(ctx_place + 1, ctx_count - 1), 1, 1
        )
        keep_before = (group_before == own_group).astype(jnp.float32)[:, :, None, None]
        keep_after = (group_after == own_group).astype(jnp.float32)[:, :, None, None]
        own_blocks = lax.dynamic_slice_in_dim(block_rows, group_start, group_len, 1)
        allowed = (block_rows[:, None, :] <= own_blocks[:, :, None]) & (
            owner_rows[:, None, :] == own_group[:, :, None]
        )
        inv_one, base_one = any_norm_parts(states)
        normed = (base_one * gain_first).astype(jnp.bfloat16)
        linear = jnp.einsum(
            "std,dce->stce", normed, qkv_full, preferred_element_type=jnp.float32
        ).astype(jnp.bfloat16)
        edge_rows = passed_along(linear[:, group_len - margin :], "ctx", 1)
        padded = jnp.concatenate(
            [edge_rows.astype(jnp.float32) * keep_before, linear.astype(jnp.float32)], axis=1
        )
        mixed_conv = sum(
            (
                tap_weights[offset] * padded[:, margin - offset : margin - offset + group_len]
                for offset in range(taps_count)
            )
        )
        triple = mixed_conv.astype(jnp.bfloat16)
        queries = triple[:, :, 0].reshape(per_micro, group_len, local_heads, HD)
        key_pair = lax.all_gather(triple[:, :, 1:], "ctx", axis=1, tiled=True)
        key_heads = key_pair[:, :, 0].reshape(per_micro, -1, local_heads, HD)
        value_heads = key_pair[:, :, 1].reshape(per_micro, -1, local_heads, HD)
        scores = masked_scores(queries, key_heads, allowed, score_scale)
        row_peak = jnp.max(scores, axis=-1, keepdims=True)
        log_total = row_peak + jnp.log(jnp.sum(jnp.exp(scores - row_peak), axis=-1, keepdims=True))
        probs_low = jnp.exp(scores - log_total).astype(jnp.bfloat16)
        attended = jnp.einsum(
            "shqk,skhe->sqhe", probs_low, value_heads, preferred_element_type=jnp.float32
        )
        attended = attended.astype(jnp.bfloat16).reshape(per_micro, group_len, -1)
        attn_part = jnp.einsum(
            "std,de->ste", attended, out_full, preferred_element_type=jnp.float32
        )
        grad_out = cotangent[first_row : first_row + per_micro]
        middle = states + tensor_total(attn_part)
        inv_two, base_two = any_norm_parts(middle)
        normed_two = (base_two * gain_second).astype(jnp.bfloat16)
        upward = jnp.einsum("std,df->stf", normed_two, up_full, preferred_element_type=jnp.float32)
        lifted = jnp.maximum(upward, 0.0)
        hidden = (lifted * lifted).astype(jnp.bfloat16)
        ffn_part = jnp.einsum("stf,fd->std", hidden, down_full, preferred_element_type=jnp.float32)
        outputs.append((middle + tensor_total(ffn_part)).astype(jnp.bfloat16))
        grad_down = jnp.einsum("stf,std->fd", hidden, grad_out, preferred_element_type=jnp.float32)
        grad_hidden = jnp.einsum(
            "std,fd->stf", grad_out, down_full, preferred_element_type=jnp.float32
        )
        grad_upward = (grad_hidden * 2.0 * lifted).astype(jnp.bfloat16)
        grad_up = jnp.einsum(
            "std,stf->df", normed_two, grad_upward, preferred_element_type=jnp.float32
        )
        norm_two_part = jnp.einsum(
            "stf,df->std", grad_upward, up_full, preferred_element_type=jnp.float32
        )
        back_two, grad_gain_two = any_norm_back(
            tensor_total(norm_two_part), gain_second, inv_two, base_two
        )
        grad_middle = grad_out.astype(jnp.float32) + back_two
        grad_branch = grad_middle.astype(jnp.bfloat16)
        grad_out_proj = jnp.einsum(
            "std,ste->de", attended, grad_branch, preferred_element_type=jnp.float32
        )
        grad_attended = jnp.einsum(
            "ste,de->std", grad_branch, out_full, preferred_element_type=jnp.float32
        )
        grad_attended = grad_attended.astype(jnp.bfloat16).reshape(
            per_micro, group_len, local_heads, HD
        )
        prob_full = jnp.exp(masked_scores(queries, key_heads, allowed, score_scale) - log_total)
        grad_probs = jnp.einsum(
            "sqhe,skhe->shqk", grad_attended, value_heads, preferred_element_type=jnp.float32
        )
        row_total = jnp.sum(prob_full * grad_probs, axis=-1, keepdims=True)
        grad_scores = (prob_full * (grad_probs - row_total)).astype(jnp.bfloat16)
        grad_queries = (
            jnp.einsum(
                "shqk,skhe->sqhe", grad_scores, key_heads, preferred_element_type=jnp.float32
            )
            * score_scale
        )
        keys_term = (
            jnp.einsum("shqk,sqhe->skhe", grad_scores, queries, preferred_element_type=jnp.float32)
            * score_scale
        )
        values_term = jnp.einsum(
            "shqk,sqhe->skhe",
            prob_full.astype(jnp.bfloat16),
            grad_attended,
            preferred_element_type=jnp.float32,
        )
        pair_grads = lax.psum_scatter(
            jnp.stack([keys_term, values_term], axis=2).astype(jnp.bfloat16),
            "ctx",
            scatter_dimension=1,
            tiled=True,
        ).astype(jnp.float32)
        grad_keys = pair_grads[:, :, 0]
        grad_values = pair_grads[:, :, 1]
        grad_triple = jnp.stack([grad_queries, grad_keys, grad_values], axis=2).reshape(
            per_micro, group_len, 3, -1
        )
        tail_rows = passed_along(grad_triple[:, :margin], "ctx", -1)
        padded_grad = jnp.concatenate([grad_triple, tail_rows * keep_after], axis=1)
        grad_linear = sum(
            (
                tap_weights[offset] * padded_grad[:, offset : offset + group_len]
                for offset in range(taps_count)
            )
        )
        grad_linear = grad_linear.astype(jnp.bfloat16)
        grad_taps = jnp.stack(
            [
                jnp.sum(
                    grad_triple * padded[:, margin - offset : margin - offset + group_len],
                    axis=(0, 1),
                )
                for offset in range(taps_count)
            ]
        )
        grad_taps = grad_taps.reshape(conv_taps.shape)
        grad_qkv = jnp.einsum(
            "std,stce->dce", normed, grad_linear, preferred_element_type=jnp.float32
        )
        grad_norm_one = tensor_total(
            jnp.einsum("stce,dce->std", grad_linear, qkv_full, preferred_element_type=jnp.float32)
        )
        back_one, grad_gain_one = any_norm_back(grad_norm_one, gain_first, inv_one, base_one)
        input_grads.append(grad_middle + back_one)
        micro_grads = (
            grad_gain_one,
            grad_qkv,
            grad_taps,
            grad_out_proj,
            grad_gain_two,
            grad_up,
            grad_down,
        )
        totals = (
            micro_grads
            if totals is None
            else tuple(
                (left_part + right_part for left_part, right_part in zip(totals, micro_grads))
            )
        )
    summed = (
        lax.psum_scatter(totals[0], ("fsdp", "ctx"), scatter_dimension=0, tiled=True),
        lax.psum_scatter(totals[1], ("fsdp", "ctx"), scatter_dimension=0, tiled=True),
        lax.psum_scatter(totals[2], ("fsdp", "ctx"), scatter_dimension=3, tiled=True),
        lax.psum_scatter(totals[3], ("fsdp", "ctx"), scatter_dimension=1, tiled=True),
        lax.psum_scatter(totals[4], ("fsdp", "ctx"), scatter_dimension=0, tiled=True),
        lax.psum_scatter(totals[5], ("fsdp", "ctx"), scatter_dimension=0, tiled=True),
        lax.psum_scatter(totals[6], ("fsdp", "ctx"), scatter_dimension=1, tiled=True),
    )
    shares = (
        lax.all_gather(summed[0].astype(jnp.bfloat16), "ctx", axis=0, tiled=True).astype(
            jnp.float32
        ),
        lax.all_gather(summed[1].astype(jnp.bfloat16), "ctx", axis=0, tiled=True).astype(
            jnp.float32
        ),
        lax.all_gather(summed[2].astype(jnp.bfloat16), "ctx", axis=3, tiled=True).astype(
            jnp.float32
        ),
        lax.all_gather(summed[3].astype(jnp.bfloat16), "ctx", axis=1, tiled=True).astype(
            jnp.float32
        ),
        lax.all_gather(summed[4].astype(jnp.bfloat16), "ctx", axis=0, tiled=True).astype(
            jnp.float32
        ),
        lax.all_gather(summed[5].astype(jnp.bfloat16), "ctx", axis=0, tiled=True).astype(
            jnp.float32
        ),
        lax.all_gather(summed[6].astype(jnp.bfloat16), "ctx", axis=1, tiled=True).astype(
            jnp.float32
        ),
    )
    return (jnp.concatenate(outputs, axis=0), jnp.concatenate(input_grads, axis=0)) + tuple(shares)


def solution(mesh):
    placed = (
        P("fsdp", "ctx", None),
        P("fsdp"),
        P("fsdp", None, "tp"),
        P(None, None, "tp", "fsdp"),
        P("tp", "fsdp"),
        P("fsdp"),
        P("fsdp", "tp"),
        P("tp", "fsdp"),
        P("fsdp", None),
        P("fsdp", None),
        P("fsdp", "ctx", None),
    )

    def on_device(*args):
        if args[0].shape[0] == lax.axis_size("ctx") == 2:
            return row_on_device(*args)
        return any_on_device(*args)

    return jax.shard_map(
        on_device,
        mesh=mesh,
        in_specs=placed,
        out_specs=(
            P("fsdp", "ctx", None),
            P("fsdp", "ctx", None),
            P("fsdp"),
            P("fsdp", None, "tp"),
            P(None, None, "tp", "fsdp"),
            P("tp", "fsdp"),
            P("fsdp"),
            P("fsdp", "tp"),
            P("tp", "fsdp"),
        ),
        check_vma=False,
    )
```

```python
import functools

import jax
import jax.numpy as jnp
from jax import lax
from jax.experimental import pallas as pl
from jax.experimental.pallas import tpu as pltpu
from jax.sharding import PartitionSpec as P


HD = 64
TILE = 256
LOG2E = 1.4426950408889634
NEG = -1e30
MESH = pl.DeviceIdType.MESH
F32 = jnp.float32
BF16 = jnp.bfloat16


def norm_parts(values):
    inverse = lax.rsqrt(jnp.mean(values * values, axis=-1, keepdims=True) + 1e-06)
    return (inverse, values * inverse)


def norm_back(grad_norm, gain_full, inverse, scaled):
    grad_scaled = grad_norm * gain_full
    inner_mean = jnp.mean(grad_scaled * scaled, axis=-1, keepdims=True)
    return inverse * (grad_scaled - scaled * inner_mean)


def dot_nn(a, b):
    return lax.dot_general(a, b, (((1,), (0,)), ((), ())), preferred_element_type=F32)


def dot_nt(a, b):
    return lax.dot_general(a, b, (((1,), (1,)), ((), ())), preferred_element_type=F32)


def dot_tn(a, b):
    return lax.dot_general(a, b, (((0,), (0,)), ((), ())), preferred_element_type=F32)


def attn_fwd_kernel(heads, lo_ref, hi_ref, qkv_ref, out_ref, lse_ref, key_scr, peak, total, acc):
    i = pl.program_id(0)
    tiles = pl.num_programs(0)
    width = heads * HD
    here = pl.ds(pl.multiple_of(i * TILE, TILE), TILE)
    factor = HD ** (-0.5) * LOG2E

    @pl.when(i == 0)
    def _():
        for h in range(heads):
            key_scr[h] = qkv_ref[width + h * HD : width + (h + 1) * HD, :].T

    peak[...] = jnp.full_like(peak, NEG)
    total[...] = jnp.zeros_like(total)
    acc[...] = jnp.zeros_like(acc)
    hi = hi_ref[:, here]

    def step(j, masked):
        there = pl.ds(pl.multiple_of(j * TILE, TILE), TILE)
        if masked:
            place = lax.broadcasted_iota(jnp.int32, (TILE, TILE), 0) + j * TILE
            keep = place < hi
        for h in range(heads):
            query = qkv_ref[h * HD : (h + 1) * HD, here]
            scores = dot_nn(key_scr[h, there, :], query) * factor
            if masked:
                scores = jnp.where(keep, scores, NEG)
            before = peak[h : h + 1, :]
            now = jnp.maximum(before, jnp.max(scores, axis=0, keepdims=True))
            shrink = jnp.exp2(before - now)
            probs = jnp.exp2(scores - now)
            total[h : h + 1, :] = total[h : h + 1, :] * shrink + jnp.sum(probs, axis=0, keepdims=True)
            values = qkv_ref[2 * width + h * HD : 2 * width + (h + 1) * HD, there]
            acc[h] = acc[h] * shrink + dot_nn(values, probs.astype(BF16))
            peak[h : h + 1, :] = now

    step(i, True)

    @pl.when(i + 1 < tiles)
    def _():
        step(i + 1, True)

    def lower(j, carry):
        step(j, False)
        return carry

    lax.fori_loop(lo_ref[i], i, lower, 0)
    for h in range(heads):
        out_ref[h * HD : (h + 1) * HD, :] = (acc[h] / total[h : h + 1, :]).astype(BF16)
        lse_ref[h : h + 1, :] = peak[h : h + 1, :] + jnp.log2(total[h : h + 1, :])


def attn_forward(lo_tile, hi, qkv, heads):
    length = qkv.shape[1]
    tiles = length // TILE
    width = heads * HD
    whole = lambda i, *_: (0, 0)
    return pl.pallas_call(
        functools.partial(attn_fwd_kernel, heads),
        out_shape=(
            jax.ShapeDtypeStruct((width, length), BF16),
            jax.ShapeDtypeStruct((8, length), F32),
        ),
        grid_spec=pltpu.PrefetchScalarGridSpec(
            num_scalar_prefetch=1,
            grid=(tiles,),
            in_specs=[
                pl.BlockSpec((1, length), whole),
                pl.BlockSpec((3 * width, length), whole),
            ],
            out_specs=(
                pl.BlockSpec((width, TILE), lambda i, *_: (0, i)),
                pl.BlockSpec((8, TILE), lambda i, *_: (0, i)),
            ),
            scratch_shapes=[
                pltpu.VMEM((heads, length, HD), BF16),
                pltpu.VMEM((8, TILE), F32),
                pltpu.VMEM((8, TILE), F32),
                pltpu.VMEM((heads, HD, TILE), F32),
            ],
        ),
        name="attn_fwd",
    )(lo_tile, hi, qkv)


def attn_bwd_kernel(heads, taps_count, lo_ref, hi_ref, qkv_ref, grad_ref, att_ref, lse_ref, lin_ref, later_ref, taps_ref, out_ref, tap_ref, key_scr, val_scr, row_tot, triple):
    i = pl.program_id(0)
    tiles = pl.num_programs(0)
    width = heads * HD
    here = pl.ds(pl.multiple_of(i * TILE, TILE), TILE)
    scale = HD ** (-0.5)
    factor = scale * LOG2E

    @pl.when(i == 0)
    def _():
        for h in range(heads):
            key_scr[h] = qkv_ref[width + h * HD : width + (h + 1) * HD, :].T
            val_scr[h] = qkv_ref[2 * width + h * HD : 2 * width + (h + 1) * HD, :].T
        triple[...] = jnp.zeros_like(triple)

    hi = hi_ref[:, here]
    for h in range(heads):
        rows = slice(h * HD, (h + 1) * HD)
        row_tot[h : h + 1, :] = jnp.sum(
            grad_ref[rows, here].astype(F32) * att_ref[rows, here].astype(F32), axis=0, keepdims=True
        )

    def step(j, masked):
        there = pl.ds(pl.multiple_of(j * TILE, TILE), TILE)
        if masked:
            place = lax.broadcasted_iota(jnp.int32, (TILE, TILE), 0) + j * TILE
            keep = place < hi
        for h in range(heads):
            q_rows = slice(h * HD, (h + 1) * HD)
            k_rows = slice(width + h * HD, width + (h + 1) * HD)
            v_rows = slice(2 * width + h * HD, 2 * width + (h + 1) * HD)
            query = qkv_ref[q_rows, here]
            grad = grad_ref[q_rows, here]
            scores = dot_nn(key_scr[h, there, :], query) * factor - lse_ref[h : h + 1, here]
            if masked:
                scores = jnp.where(keep, scores, NEG)
            probs = jnp.exp2(scores)
            grad_probs = dot_nn(val_scr[h, there, :], grad)
            grad_scores = (probs * (grad_probs - row_tot[h : h + 1, :])).astype(BF16)
            triple[v_rows, there] += dot_nt(grad, probs.astype(BF16))
            triple[k_rows, there] += dot_nt(query, grad_scores)
            triple[q_rows, here] += dot_nn(qkv_ref[k_rows, there], grad_scores)

    step(i, True)

    @pl.when(i + 1 < tiles)
    def _():
        step(i + 1, True)

    def lower(j, carry):
        step(j, False)
        return carry

    lax.fori_loop(lo_ref[i], i, lower, 0)

    @pl.when(i == tiles - 1)
    def _():
        for block in range(3 * heads):
            rows = slice(block * HD, (block + 1) * HD)
            unit = scale if block < 2 * heads else 1.0
            weights = [taps_ref[rows, j : j + 1] for j in range(taps_count)]

            def tile(n, sums):
                start = pl.multiple_of(n * TILE, TILE)
                spot = pl.ds(start, TILE)
                wide = triple[rows, pl.ds(start, TILE + 128)] * unit
                lin = lin_ref[rows, spot].astype(F32)
                total = None
                result = []
                for j in range(taps_count):
                    if j == 0:
                        moved = wide[:, :TILE]
                    else:
                        moved = pltpu.roll(wide, TILE + 128 - j, 1)[:, :TILE] * later_ref[j : j + 1, spot]
                    total = weights[j] * moved if total is None else total + weights[j] * moved
                    product = moved * lin
                    result.append(sums[j] + product[:, :128] + product[:, 128:])
                out_ref[rows, spot] = total.astype(BF16)
                return tuple(result)

            zero = jnp.zeros((HD, 128), F32)
            sums = lax.fori_loop(0, tiles, tile, (zero,) * taps_count)
            for j in range(taps_count):
                tap_ref[rows, j : j + 1] = jnp.sum(sums[j], axis=1, keepdims=True)


def attn_backward(lo_tile, hi, qkv, grad, att, lse, linear, later, taps, heads):
    length = qkv.shape[1]
    tiles = length // TILE
    width = heads * HD
    taps_count = taps.shape[0]
    later = jnp.pad(later, ((0, 8 - taps_count), (0, 0)))
    columns = jnp.pad(taps.T, ((0, 0), (0, 128 - taps_count)))
    whole = lambda i, *_: (0, 0)
    return pl.pallas_call(
        functools.partial(attn_bwd_kernel, heads, taps_count),
        out_shape=(
            jax.ShapeDtypeStruct((3 * width, length), BF16),
            jax.ShapeDtypeStruct((3 * width, 128), F32),
        ),
        grid_spec=pltpu.PrefetchScalarGridSpec(
            num_scalar_prefetch=1,
            grid=(tiles,),
            in_specs=[
                pl.BlockSpec((1, length), whole),
                pl.BlockSpec((3 * width, length), whole),
                pl.BlockSpec((width, length), whole),
                pl.BlockSpec((width, length), whole),
                pl.BlockSpec((8, length), whole),
                pl.BlockSpec((3 * width, length), whole),
                pl.BlockSpec((8, length), whole),
                pl.BlockSpec((3 * width, 128), whole),
            ],
            out_specs=(
                pl.BlockSpec((3 * width, length), whole),
                pl.BlockSpec((3 * width, 128), whole),
            ),
            scratch_shapes=[
                pltpu.VMEM((heads, length, HD), BF16),
                pltpu.VMEM((heads, length, HD), BF16),
                pltpu.VMEM((8, TILE), F32),
                pltpu.VMEM((3 * width, length + 128), F32),
            ],
        ),
        name="attn_bwd",
    )(lo_tile, hi, qkv, grad, att, lse, linear, later, columns)


def spread_kernel(ctx_count, tp_count, x_ref, o_ref, send_sem, recv_sem, own_sem):
    peers = ctx_count * tp_count
    me = lax.axis_index("ctx") * tp_count + lax.axis_index("tp")

    def place(k):
        other = lax.rem(me + k, peers)
        return other, {"ctx": other // tp_count, "tp": lax.rem(other, tp_count)}

    barrier = pltpu.get_barrier_semaphore()
    for k in range(1, peers):
        pl.semaphore_signal(barrier, inc=1, device_id=place(k)[1], device_id_type=MESH)
    pl.semaphore_wait(barrier, peers - 1)
    copies = []
    for k in range(1, peers):
        other, device = place(k)
        copies.append(
            pltpu.make_async_remote_copy(
                src_ref=x_ref.at[other],
                dst_ref=o_ref.at[me],
                send_sem=send_sem.at[k - 1],
                recv_sem=recv_sem.at[k - 1],
                device_id=device,
                device_id_type=MESH,
            )
        )
        copies[-1].start()
    own = pltpu.make_async_copy(x_ref.at[me], o_ref.at[me], own_sem)
    own.start()
    own.wait()
    for copy in copies:
        copy.wait()


def spread(x, ctx_count, tp_count, ident):
    peers = ctx_count * tp_count
    return pl.pallas_call(
        functools.partial(spread_kernel, ctx_count, tp_count),
        out_shape=jax.ShapeDtypeStruct(x.shape, x.dtype),
        in_specs=[pl.BlockSpec(memory_space=pltpu.VMEM)],
        out_specs=pl.BlockSpec(memory_space=pltpu.VMEM),
        scratch_shapes=[
            pltpu.SemaphoreType.DMA((peers - 1,)),
            pltpu.SemaphoreType.DMA((peers - 1,)),
            pltpu.SemaphoreType.DMA,
        ],
        compiler_params=pltpu.CompilerParams(collective_id=ident, has_side_effects=True),
    )(x)


def gather_sum_kernel(tp_count, p_ref, o_ref, from_left, from_right, mine, right_sem, left_sem, pair_sem):
    me = lax.axis_index("tp")
    row = lax.axis_index("ctx")
    last = tp_count - 1
    right, left = jnp.minimum(me + 1, last), jnp.maximum(me - 1, 0)

    barrier = pltpu.get_barrier_semaphore()

    @pl.when(me < last)
    def _():
        pl.semaphore_signal(barrier, inc=1, device_id={"tp": right}, device_id_type=MESH)

    @pl.when(me > 0)
    def _():
        pl.semaphore_signal(barrier, inc=1, device_id={"tp": left}, device_id_type=MESH)

    pl.semaphore_signal(barrier, inc=1, device_id={"ctx": 1 - row}, device_id_type=MESH)
    pl.semaphore_wait(barrier, 1 + (me < last).astype(jnp.int32) + (me > 0).astype(jnp.int32))

    def pass_on(source, buffer, half, c, target, sems):
        return pltpu.make_async_remote_copy(
            src_ref=source,
            dst_ref=buffer.at[half, c],
            send_sem=sems.at[0, half, c],
            recv_sem=sems.at[1, half, c],
            device_id={"tp": target},
            device_id_type=MESH,
        )

    def flow(half, c, first, buffer, target, sems):
        @pl.when(first)
        def _():
            pass_on(p_ref.at[half, c], buffer, half, c, target, sems).start()

        @pl.when(jnp.logical_not(first))
        def _():
            copy = pass_on(buffer.at[half, c], buffer, half, c, target, sems)
            copy.wait_recv()
            buffer[half, c] = (buffer[half, c].astype(F32) + p_ref[half, c].astype(F32)).astype(BF16)
            copy.start()

    def pair():
        return pltpu.make_async_remote_copy(
            src_ref=mine,
            dst_ref=o_ref.at[row],
            send_sem=pair_sem.at[0],
            recv_sem=pair_sem.at[1],
            device_id={"ctx": 1 - row},
            device_id_type=MESH,
        )

    for step in range(last):
        for half in (1 - row, row):
            @pl.when(last - step > me)
            def _():
                flow(half, last - step, me == 0, from_left, right, right_sem)

            @pl.when(step < me)
            def _():
                flow(half, step, me == last, from_right, left, left_sem)

    for half in (1 - row, row):
        here = p_ref.at[half, me]

        def come(buffer, sems):
            pass_on(here, buffer, half, me, left, sems).wait_recv()
            return buffer[half, me].astype(F32)

        target = mine if half is not row else o_ref.at[row]

        @pl.when(me == 0)
        def _():
            target[...] = (here[...].astype(F32) + come(from_right, left_sem)).astype(BF16)

        @pl.when(me == last)
        def _():
            target[...] = (here[...].astype(F32) + come(from_left, right_sem)).astype(BF16)

        @pl.when((me > 0) & (me < last))
        def _():
            total = here[...].astype(F32) + come(from_left, right_sem)
            target[...] = (total + come(from_right, left_sem)).astype(BF16)

        if half is not row:
            pair().start()

    for step in range(last):
        for half in (1 - row, row):
            @pl.when(last - step > me)
            def _():
                pass_on(p_ref.at[half, last - step], from_left, half, last - step, right, right_sem).wait_send()

            @pl.when(step < me)
            def _():
                pass_on(p_ref.at[half, step], from_right, half, step, left, left_sem).wait_send()

    pair().wait()


def gather_sum(parts, ident):
    ctx_count, tp_count, size, model = parts.shape
    vmem = pl.BlockSpec(memory_space=pltpu.VMEM)
    return pl.pallas_call(
        functools.partial(gather_sum_kernel, tp_count),
        out_shape=jax.ShapeDtypeStruct((ctx_count, size, model), BF16),
        in_specs=[vmem],
        out_specs=vmem,
        scratch_shapes=[
            pltpu.VMEM(parts.shape, BF16),
            pltpu.VMEM(parts.shape, BF16),
            pltpu.VMEM((size, model), BF16),
            pltpu.SemaphoreType.DMA((2, ctx_count, tp_count)),
            pltpu.SemaphoreType.DMA((2, ctx_count, tp_count)),
            pltpu.SemaphoreType.DMA((2,)),
        ],
        compiler_params=pltpu.CompilerParams(collective_id=ident, has_side_effects=True),
        name="gather_sum",
    )(parts)


def finish_kernel(tp_count, x_ref, g_ref, o_ref, s_ref, came, right_sem, left_sem, part_sem, pair_sem, own_sem):
    me = lax.axis_index("tp")
    row = lax.axis_index("ctx")
    size = x_ref.shape[1]
    last = tp_count - 1

    barrier = pltpu.get_barrier_semaphore()
    for k in range(1, tp_count):
        other = lax.rem(me + k, tp_count)
        pl.semaphore_signal(barrier, inc=1, device_id={"tp": other}, device_id_type=MESH)
    pl.semaphore_signal(barrier, inc=1, device_id={"ctx": 1 - row}, device_id_type=MESH)
    pl.semaphore_wait(barrier, tp_count)

    def chunk(k):
        return o_ref.at[:, pl.ds(pl.multiple_of(k * size, size), size), :]

    def pass_on(source, k, step, target, sems):
        return pltpu.make_async_remote_copy(
            src_ref=source,
            dst_ref=chunk(k),
            send_sem=sems.at[0, step - 1],
            recv_sem=sems.at[1, step - 1],
            device_id={"tp": target},
            device_id_type=MESH,
        )

    def rightward(step):
        k = me - step + 1
        return pass_on(x_ref if step == 1 else chunk(jnp.maximum(k, 0)), jnp.maximum(k, 0), step, jnp.minimum(me + 1, last), right_sem)

    def leftward(step):
        k = me + step - 1
        return pass_on(x_ref if step == 1 else chunk(jnp.minimum(k, last)), jnp.minimum(k, last), step, jnp.maximum(me - 1, 0), left_sem)

    pieces = []
    for k in range(1, tp_count):
        other = lax.rem(me + k, tp_count)
        pieces.append(
            pltpu.make_async_remote_copy(
                src_ref=g_ref.at[other],
                dst_ref=came.at[k - 1],
                send_sem=part_sem.at[0, k - 1],
                recv_sem=part_sem.at[1, k - 1],
                device_id={"tp": other},
                device_id_type=MESH,
            )
        )
        pieces[-1].start()
    pair = pltpu.make_async_remote_copy(
        src_ref=s_ref.at[row],
        dst_ref=s_ref.at[row],
        send_sem=pair_sem.at[0],
        recv_sem=pair_sem.at[1],
        device_id={"ctx": 1 - row},
        device_id_type=MESH,
    )
    own = pltpu.make_async_copy(x_ref, chunk(me), own_sem)
    own.start()
    for step in range(1, tp_count):
        @pl.when((me < last) & (me - step + 1 >= 0))
        def _():
            rightward(step).start()

        @pl.when((me > 0) & (me + step - 1 <= last))
        def _():
            leftward(step).start()

        if step == 1:
            for piece in pieces:
                piece.wait_recv()
            total = g_ref[me].astype(F32)
            for k in range(1, tp_count):
                total = total + came[k - 1].astype(F32)
            s_ref[row] = total.astype(BF16)

        @pl.when(me - step >= 0)
        def _():
            rightward(step).wait_recv()

        @pl.when(me + step <= last)
        def _():
            leftward(step).wait_recv()

        if step == 1:
            pair.start()
    own.wait()
    for step in range(1, tp_count):
        @pl.when((me < last) & (me - step + 1 >= 0))
        def _():
            rightward(step).wait_send()

        @pl.when((me > 0) & (me + step - 1 <= last))
        def _():
            leftward(step).wait_send()

    for piece in pieces:
        piece.wait_send()
    pair.wait()


def finish(x, g, ctx_count, tp_count, ident):
    rows, size, model = x.shape
    vmem = pl.BlockSpec(memory_space=pltpu.VMEM)
    return pl.pallas_call(
        functools.partial(finish_kernel, tp_count),
        out_shape=(
            jax.ShapeDtypeStruct((rows, size * tp_count, model), BF16),
            jax.ShapeDtypeStruct((ctx_count,) + g.shape[1:], BF16),
        ),
        in_specs=[vmem, vmem],
        out_specs=(vmem, vmem),
        scratch_shapes=[
            pltpu.VMEM((tp_count - 1,) + g.shape[1:], BF16),
            pltpu.SemaphoreType.DMA((2, tp_count - 1)),
            pltpu.SemaphoreType.DMA((2, tp_count - 1)),
            pltpu.SemaphoreType.DMA((2, tp_count - 1)),
            pltpu.SemaphoreType.DMA((2,)),
            pltpu.SemaphoreType.DMA,
        ],
        compiler_params=pltpu.CompilerParams(collective_id=ident, has_side_effects=True),
        name="finish",
    )(x, g)


def weight_grads_kernel(norm_ref, cot_ref, branch_ref, up_ref, hid_ref, att_ref, out_ref, norm_t, cot_t, branch_t):
    @pl.when(pl.program_id(0) == 0)
    def _():
        norm_t[...] = norm_ref[...].T
        cot_t[...] = cot_ref[...].T
        branch_t[...] = branch_ref[...].T

    pieces, _, piece, _ = out_ref.shape
    units = up_ref.shape[2]
    quarter = att_ref.shape[3]

    def put(value, start):
        stop = start + value.shape[1]
        out_ref[:, 0, :, start:stop] = value.astype(BF16).reshape(pieces, piece, value.shape[1])

    put(dot_nn(norm_t[...], up_ref[0]), 0)
    put(dot_nn(cot_t[...], hid_ref[0]), units)
    total = None
    for r in range(att_ref.shape[0]):
        term = dot_nt(branch_t[:, r * quarter : (r + 1) * quarter], att_ref[r, 0])
        total = term if total is None else total + term
    put(total, 2 * units)


def weight_grads(normed, cot, branch, grad_up, hidden, att, pieces):
    tokens, model = normed.shape
    blocks, _, units = hidden.shape
    rows, _, width, quarter = att.shape
    columns = 2 * units + width
    fixed = pl.BlockSpec((tokens, model), lambda b: (0, 0))
    moving = pl.BlockSpec((1, tokens, units), lambda b: (b, 0, 0))
    return pl.pallas_call(
        weight_grads_kernel,
        grid=(blocks,),
        out_shape=jax.ShapeDtypeStruct((pieces, blocks, model // pieces, columns), BF16),
        in_specs=[fixed, fixed, fixed, moving, moving, pl.BlockSpec((rows, 1, width, quarter), lambda b: (0, b, 0, 0))],
        out_specs=pl.BlockSpec((pieces, 1, model // pieces, columns), lambda b: (0, b, 0, 0)),
        scratch_shapes=[pltpu.VMEM((model, tokens), BF16)] * 3,
        name="weight_grads",
    )(normed, cot, branch, grad_up, hidden, att)


def row_on_device(
    tokens, gain_one, w_qkv, kernel, w_out, gain_two, w_up, w_down, block_ids, seq_ids, cotangent
):
    place = lax.axis_index("ctx")
    part = lax.axis_index("tp")
    ctx_count = lax.axis_size("ctx")
    tp_count = lax.axis_size("tp")
    fsdp_count = lax.axis_size("fsdp")
    group_len = tokens.shape[1]
    length = group_len * ctx_count
    model = tokens.shape[2]
    taps_count = kernel.shape[0]
    heads = kernel.shape[2]
    width = heads * HD
    rows = tokens.shape[0]
    quarter = group_len // tp_count
    slice_d = w_up.shape[0]
    units = w_up.shape[1]

    qkv_full = lax.all_gather(w_qkv.reshape(slice_d, 3 * width), "fsdp", axis=0, tiled=True)
    small = jnp.concatenate([gain_one, gain_two, kernel.reshape(-1)])
    small_all = lax.all_gather(small, "fsdp", axis=0).astype(F32)
    gain_first = small_all[:, :slice_d].reshape(-1)
    gain_second = small_all[:, slice_d : 2 * slice_d].reshape(-1)
    taps = small_all[:, 2 * slice_d :].reshape(fsdp_count, taps_count, 3, heads, -1)
    taps = taps.transpose(1, 2, 3, 0, 4).reshape(taps_count, 3 * width)
    packed = jnp.concatenate([w_up, w_down.T, w_out.T], axis=1)
    gathered = lax.all_gather(packed, ("tp", "fsdp"), axis=0, tiled=True)
    gathered = gathered.reshape(tp_count, model, packed.shape[1])
    up_blocks = gathered[:, :, :units]
    down_blocks = gathered[:, :, units : 2 * units]
    out_blocks = gathered[:, :, 2 * units :]

    away = lax.dynamic_index_in_dim(tokens, 1 - place, 0, keepdims=False)
    mine = lax.dynamic_index_in_dim(tokens, place, 0, keepdims=False)
    swap = [(i, 1 - i) for i in range(ctx_count)]
    came = lax.ppermute(away, "ctx", swap)
    row = jnp.where(place == 0, jnp.concatenate([mine, came]), jnp.concatenate([came, mine]))
    block_row = lax.dynamic_index_in_dim(block_ids, place, 0, keepdims=False)
    seq_row = lax.dynamic_index_in_dim(seq_ids, place, 0, keepdims=False)
    owner_row = jnp.repeat(seq_row, group_len)
    code = owner_row * 4096 + block_row
    hi = jnp.sum((code[None, :] <= code[:, None]).astype(jnp.int32), axis=1)[None, :]
    first_piece = jnp.sum((seq_row[None, :] < seq_row[:, None]).astype(jnp.int32), axis=1)
    lo_tile = jnp.repeat(first_piece * (group_len // TILE), group_len // TILE)

    row_values = row.astype(F32)
    _, base_row = norm_parts(row_values)
    normed = (base_row * gain_first).astype(BF16)
    linear = dot_tn(qkv_full, normed.T).astype(BF16)
    linear_f = linear.astype(F32)
    same = [
        jnp.concatenate([jnp.zeros((j,), F32), (owner_row[j:] == owner_row[: length - j]).astype(F32)])
        for j in range(taps_count)
    ]
    shifted = [linear_f] + [
        jnp.pad(linear_f[:, : length - j], ((0, 0), (j, 0))) * same[j] for j in range(1, taps_count)
    ]
    triple = sum(taps[j][:, None] * shifted[j] for j in range(taps_count)).astype(BF16)
    att, lse = attn_forward(lo_tile, hi, triple, heads)

    sent = att.reshape(width, ctx_count, tp_count, quarter).transpose(1, 2, 0, 3)
    got = spread(sent.reshape(ctx_count * tp_count, width, quarter), ctx_count, tp_count, 1)
    got = got.reshape(rows, tp_count, width, quarter)
    attended = got.transpose(0, 3, 1, 2).reshape(rows * quarter, tp_count * width)
    states = lax.dynamic_slice_in_dim(tokens, part * quarter, quarter, 1)
    states = states.reshape(rows * quarter, model).astype(F32)
    grad_out = lax.dynamic_slice_in_dim(cotangent, part * quarter, quarter, 1)
    grad_out = grad_out.reshape(rows * quarter, model)
    out_flat = out_blocks.transpose(1, 0, 2).reshape(model, tp_count * width)
    middle = states + dot_nt(attended, out_flat)
    inv_two, base_two = norm_parts(middle)
    normed_two = (base_two * gain_second).astype(BF16)
    upward = jnp.einsum("td,bdu->btu", normed_two, up_blocks, preferred_element_type=F32)
    lifted = jnp.maximum(upward, 0.0)
    hidden = (lifted * lifted).astype(BF16)
    ffn = jnp.einsum("btu,bdu->td", hidden, down_blocks, preferred_element_type=F32)
    block_out = (middle + ffn).astype(BF16).reshape(rows, quarter, model)
    block_out, lifted = lax.optimization_barrier((block_out, lifted))
    chunks = [block_out]
    for k in range(1, tp_count):
        ring = [(i, (i + k) % tp_count) for i in range(tp_count)]
        chunks.append(lax.ppermute(block_out, "tp", ring))
    grad_hidden = jnp.einsum("td,bdu->btu", grad_out, down_blocks, preferred_element_type=F32)
    grad_upward = (grad_hidden * 2.0 * lifted).astype(BF16)
    grad_norm_two = jnp.einsum("btu,bdu->td", grad_upward, up_blocks, preferred_element_type=F32)
    back_two = norm_back(grad_norm_two, gain_second, inv_two, base_two)
    grad_middle = grad_out.astype(F32) + back_two
    grad_branch = grad_middle.astype(BF16)
    grad_attended = dot_nn(grad_branch, out_flat).astype(BF16)
    grad_packed = weight_grads(normed_two, grad_out, grad_branch, grad_upward, hidden, got, fsdp_count * ctx_count)

    sent = grad_attended.reshape(rows, quarter, tp_count, width).transpose(0, 2, 3, 1)
    sent, grad_packed = lax.optimization_barrier((sent, grad_packed))
    columns = grad_packed.shape[3]
    grad_packed = grad_packed.reshape(-1, columns)
    grad_packed = lax.psum_scatter(grad_packed, ("fsdp", "ctx"), scatter_dimension=0, tiled=True)
    grad_packed = grad_packed.reshape(tp_count, -1, columns)
    got = spread(sent.reshape(rows * tp_count, width, quarter), ctx_count, tp_count, 2)
    got = got.reshape(ctx_count, tp_count, width, quarter)
    grad_att = got.transpose(2, 0, 1, 3).reshape(width, length)
    later = jnp.stack([jnp.pad(same[j][j:], (0, j)) for j in range(taps_count)])
    grad_linear, grad_taps = attn_backward(lo_tile, hi, triple, grad_att, att, lse, linear, later, taps, heads)
    grad_taps = grad_taps[:, :taps_count].T
    grad_qkv = lax.dot_general(
        normed, grad_linear, (((0,), (1,)), ((), ())), preferred_element_type=F32
    )
    sent = lax.dot_general(
        grad_linear, qkv_full, (((0,), (1,)), ((), ())), preferred_element_type=F32
    ).astype(BF16).reshape(ctx_count, tp_count, quarter, model)
    sent, *chunks = lax.optimization_barrier((sent, *chunks))
    whole_out = jnp.zeros((rows, group_len, model), BF16)
    for k in range(tp_count):
        start = lax.rem(part + tp_count - k, tp_count) * quarter
        whole_out = lax.dynamic_update_slice_in_dim(whole_out, chunks[k], start, 1)
    block_out = whole_out
    grad_norm_one = gather_sum(sent, 3).astype(F32).reshape(rows * quarter, model)
    inv_one, base_one = norm_parts(states)
    back_one = norm_back(grad_norm_one, gain_first, inv_one, base_one)
    input_grad = (grad_middle + back_one).astype(BF16).reshape(rows, quarter, model)
    input_grad, grad_packed = finish(input_grad, grad_packed, ctx_count, tp_count, 4)
    input_grad = input_grad.astype(F32)
    grad_packed = grad_packed.reshape(slice_d, columns).astype(F32)

    halves = fsdp_count * ctx_count
    f_taps = grad_taps.reshape(taps_count * 3 * heads, fsdp_count, -1).transpose(1, 0, 2).reshape(fsdp_count, -1)
    f_taps = jnp.pad(f_taps, ((0, 0), (0, 16 * 3 * width - f_taps.shape[1])))
    f_taps = jnp.repeat(f_taps.reshape(fsdp_count, 16, 3 * width), ctx_count, axis=0)
    half_d = slice_d // ctx_count
    grad_qkv = jnp.concatenate([grad_qkv.reshape(halves, half_d, 3 * width), f_taps], axis=1)
    grad_qkv = grad_qkv.astype(BF16).reshape(halves * (half_d + 16), 3 * width)
    grad_qkv = lax.psum_scatter(grad_qkv, ("fsdp", "ctx"), scatter_dimension=0, tiled=True)
    grad_taps = grad_qkv[half_d:].astype(F32).reshape(-1)[: kernel.size].reshape(kernel.shape)
    grad_qkv = lax.all_gather(grad_qkv[:half_d], "ctx", axis=0, tiled=True).astype(F32)

    gains = jnp.stack(
        [
            jnp.sum(grad_qkv * w_qkv.reshape(slice_d, 3 * width).astype(F32), axis=1) / gain_one.astype(F32),
            jnp.sum(grad_packed[:, :units] * w_up.astype(F32), axis=1) / gain_two.astype(F32),
        ]
    )
    gains = lax.psum(gains, "tp")
    return (
        block_out,
        input_grad,
        gains[0],
        grad_qkv.reshape(slice_d, 3, width),
        grad_taps,
        grad_packed[:, 2 * units :].T,
        gains[1],
        grad_packed[:, :units],
        grad_packed[:, units : 2 * units].T,
    )


MICRO = 2
SEQS_MB = 1


def passed_along(block, axis, distance):
    devices = range(lax.axis_size(axis))
    route = [(i - distance, i) for i in devices if i - distance in devices]
    return lax.ppermute(block, axis, route)


def any_norm_parts(values):
    inverse = lax.rsqrt(jnp.mean(values * values, axis=-1, keepdims=True) + 1e-06)
    return (inverse, values * inverse)


def any_norm_back(grad_norm, gain_full, inverse, scaled):
    grad_scaled = grad_norm * gain_full
    inner_mean = jnp.mean(grad_scaled * scaled, axis=-1, keepdims=True)
    return (inverse * (grad_scaled - scaled * inner_mean), jnp.sum(grad_norm * scaled, axis=(0, 1)))


def masked_scores(queries, key_heads, allowed, score_scale):
    scores = (
        jnp.einsum("sqhe,skhe->shqk", queries, key_heads, preferred_element_type=jnp.float32)
        * score_scale
    )
    return jnp.where(allowed[:, None], scores, -1e30)


def tensor_total(values):
    return lax.psum(values, "tp")


def any_on_device(
    tokens, gain_one, w_qkv, kernel, w_out, gain_two, w_up, w_down, block_ids, seq_ids, cotangent
):
    ctx_place = lax.axis_index("ctx")
    ctx_count = lax.axis_size("ctx")
    group_len = tokens.shape[1]
    taps_count = kernel.shape[0]
    margin = taps_count - 1
    local_heads = kernel.shape[2]
    score_scale = HD ** (-0.5)
    per_micro = SEQS_MB
    group_start = ctx_place * group_len
    owner_all = jnp.repeat(seq_ids, group_len, axis=1)
    totals = None
    outputs = []
    input_grads = []
    for micro_step in range(MICRO):
        gathered = (
            lax.all_gather(gain_one, "fsdp", axis=0, tiled=True),
            lax.all_gather(w_qkv, "fsdp", axis=0, tiled=True),
            lax.all_gather(kernel, "fsdp", axis=3, tiled=True),
            lax.all_gather(w_out, "fsdp", axis=1, tiled=True),
            lax.all_gather(gain_two, "fsdp", axis=0, tiled=True),
            lax.all_gather(w_up, "fsdp", axis=0, tiled=True),
            lax.all_gather(w_down, "fsdp", axis=1, tiled=True),
        )
        gain_first, qkv_full, conv_taps, out_full, gain_second, up_full, down_full = gathered
        gain_first = gain_first.astype(jnp.float32)
        gain_second = gain_second.astype(jnp.float32)
        tap_weights = conv_taps.astype(jnp.float32).reshape(taps_count, 3, -1)
        first_row = micro_step * per_micro
        states = tokens[first_row : first_row + per_micro].astype(jnp.float32)
        block_rows = block_ids[first_row : first_row + per_micro]
        owner_rows = owner_all[first_row : first_row + per_micro]
        group_ids = seq_ids[first_row : first_row + per_micro]
        own_group = lax.dynamic_slice_in_dim(group_ids, ctx_place, 1, 1)
        group_before = lax.dynamic_slice_in_dim(group_ids, jnp.maximum(ctx_place - 1, 0), 1, 1)
        group_after = lax.dynamic_slice_in_dim(
            group_ids, jnp.minimum(ctx_place + 1, ctx_count - 1), 1, 1
        )
        keep_before = (group_before == own_group).astype(jnp.float32)[:, :, None, None]
        keep_after = (group_after == own_group).astype(jnp.float32)[:, :, None, None]
        own_blocks = lax.dynamic_slice_in_dim(block_rows, group_start, group_len, 1)
        allowed = (block_rows[:, None, :] <= own_blocks[:, :, None]) & (
            owner_rows[:, None, :] == own_group[:, :, None]
        )
        inv_one, base_one = any_norm_parts(states)
        normed = (base_one * gain_first).astype(jnp.bfloat16)
        linear = jnp.einsum(
            "std,dce->stce", normed, qkv_full, preferred_element_type=jnp.float32
        ).astype(jnp.bfloat16)
        edge_rows = passed_along(linear[:, group_len - margin :], "ctx", 1)
        padded = jnp.concatenate(
            [edge_rows.astype(jnp.float32) * keep_before, linear.astype(jnp.float32)], axis=1
        )
        mixed_conv = sum(
            (
                tap_weights[offset] * padded[:, margin - offset : margin - offset + group_len]
                for offset in range(taps_count)
            )
        )
        triple = mixed_conv.astype(jnp.bfloat16)
        queries = triple[:, :, 0].reshape(per_micro, group_len, local_heads, HD)
        key_pair = lax.all_gather(triple[:, :, 1:], "ctx", axis=1, tiled=True)
        key_heads = key_pair[:, :, 0].reshape(per_micro, -1, local_heads, HD)
        value_heads = key_pair[:, :, 1].reshape(per_micro, -1, local_heads, HD)
        scores = masked_scores(queries, key_heads, allowed, score_scale)
        row_peak = jnp.max(scores, axis=-1, keepdims=True)
        log_total = row_peak + jnp.log(jnp.sum(jnp.exp(scores - row_peak), axis=-1, keepdims=True))
        probs_low = jnp.exp(scores - log_total).astype(jnp.bfloat16)
        attended = jnp.einsum(
            "shqk,skhe->sqhe", probs_low, value_heads, preferred_element_type=jnp.float32
        )
        attended = attended.astype(jnp.bfloat16).reshape(per_micro, group_len, -1)
        attn_part = jnp.einsum(
            "std,de->ste", attended, out_full, preferred_element_type=jnp.float32
        )
        grad_out = cotangent[first_row : first_row + per_micro]
        middle = states + tensor_total(attn_part)
        inv_two, base_two = any_norm_parts(middle)
        normed_two = (base_two * gain_second).astype(jnp.bfloat16)
        upward = jnp.einsum("std,df->stf", normed_two, up_full, preferred_element_type=jnp.float32)
        lifted = jnp.maximum(upward, 0.0)
        hidden = (lifted * lifted).astype(jnp.bfloat16)
        ffn_part = jnp.einsum("stf,fd->std", hidden, down_full, preferred_element_type=jnp.float32)
        outputs.append((middle + tensor_total(ffn_part)).astype(jnp.bfloat16))
        grad_down = jnp.einsum("stf,std->fd", hidden, grad_out, preferred_element_type=jnp.float32)
        grad_hidden = jnp.einsum(
            "std,fd->stf", grad_out, down_full, preferred_element_type=jnp.float32
        )
        grad_upward = (grad_hidden * 2.0 * lifted).astype(jnp.bfloat16)
        grad_up = jnp.einsum(
            "std,stf->df", normed_two, grad_upward, preferred_element_type=jnp.float32
        )
        norm_two_part = jnp.einsum(
            "stf,df->std", grad_upward, up_full, preferred_element_type=jnp.float32
        )
        back_two, grad_gain_two = any_norm_back(
            tensor_total(norm_two_part), gain_second, inv_two, base_two
        )
        grad_middle = grad_out.astype(jnp.float32) + back_two
        grad_branch = grad_middle.astype(jnp.bfloat16)
        grad_out_proj = jnp.einsum(
            "std,ste->de", attended, grad_branch, preferred_element_type=jnp.float32
        )
        grad_attended = jnp.einsum(
            "ste,de->std", grad_branch, out_full, preferred_element_type=jnp.float32
        )
        grad_attended = grad_attended.astype(jnp.bfloat16).reshape(
            per_micro, group_len, local_heads, HD
        )
        prob_full = jnp.exp(masked_scores(queries, key_heads, allowed, score_scale) - log_total)
        grad_probs = jnp.einsum(
            "sqhe,skhe->shqk", grad_attended, value_heads, preferred_element_type=jnp.float32
        )
        row_total = jnp.sum(prob_full * grad_probs, axis=-1, keepdims=True)
        grad_scores = (prob_full * (grad_probs - row_total)).astype(jnp.bfloat16)
        grad_queries = (
            jnp.einsum(
                "shqk,skhe->sqhe", grad_scores, key_heads, preferred_element_type=jnp.float32
            )
            * score_scale
        )
        keys_term = (
            jnp.einsum("shqk,sqhe->skhe", grad_scores, queries, preferred_element_type=jnp.float32)
            * score_scale
        )
        values_term = jnp.einsum(
            "shqk,sqhe->skhe",
            prob_full.astype(jnp.bfloat16),
            grad_attended,
            preferred_element_type=jnp.float32,
        )
        pair_grads = lax.psum_scatter(
            jnp.stack([keys_term, values_term], axis=2).astype(jnp.bfloat16),
            "ctx",
            scatter_dimension=1,
            tiled=True,
        ).astype(jnp.float32)
        grad_keys = pair_grads[:, :, 0]
        grad_values = pair_grads[:, :, 1]
        grad_triple = jnp.stack([grad_queries, grad_keys, grad_values], axis=2).reshape(
            per_micro, group_len, 3, -1
        )
        tail_rows = passed_along(grad_triple[:, :margin], "ctx", -1)
        padded_grad = jnp.concatenate([grad_triple, tail_rows * keep_after], axis=1)
        grad_linear = sum(
            (
                tap_weights[offset] * padded_grad[:, offset : offset + group_len]
                for offset in range(taps_count)
            )
        )
        grad_linear = grad_linear.astype(jnp.bfloat16)
        grad_taps = jnp.stack(
            [
                jnp.sum(
                    grad_triple * padded[:, margin - offset : margin - offset + group_len],
                    axis=(0, 1),
                )
                for offset in range(taps_count)
            ]
        )
        grad_taps = grad_taps.reshape(conv_taps.shape)
        grad_qkv = jnp.einsum(
            "std,stce->dce", normed, grad_linear, preferred_element_type=jnp.float32
        )
        grad_norm_one = tensor_total(
            jnp.einsum("stce,dce->std", grad_linear, qkv_full, preferred_element_type=jnp.float32)
        )
        back_one, grad_gain_one = any_norm_back(grad_norm_one, gain_first, inv_one, base_one)
        input_grads.append(grad_middle + back_one)
        micro_grads = (
            grad_gain_one,
            grad_qkv,
            grad_taps,
            grad_out_proj,
            grad_gain_two,
            grad_up,
            grad_down,
        )
        totals = (
            micro_grads
            if totals is None
            else tuple(
                (left_part + right_part for left_part, right_part in zip(totals, micro_grads))
            )
        )
    summed = (
        lax.psum_scatter(totals[0], ("fsdp", "ctx"), scatter_dimension=0, tiled=True),
        lax.psum_scatter(totals[1], ("fsdp", "ctx"), scatter_dimension=0, tiled=True),
        lax.psum_scatter(totals[2], ("fsdp", "ctx"), scatter_dimension=3, tiled=True),
        lax.psum_scatter(totals[3], ("fsdp", "ctx"), scatter_dimension=1, tiled=True),
        lax.psum_scatter(totals[4], ("fsdp", "ctx"), scatter_dimension=0, tiled=True),
        lax.psum_scatter(totals[5], ("fsdp", "ctx"), scatter_dimension=0, tiled=True),
        lax.psum_scatter(totals[6], ("fsdp", "ctx"), scatter_dimension=1, tiled=True),
    )
    shares = (
        lax.all_gather(summed[0].astype(jnp.bfloat16), "ctx", axis=0, tiled=True).astype(
            jnp.float32
        ),
        lax.all_gather(summed[1].astype(jnp.bfloat16), "ctx", axis=0, tiled=True).astype(
            jnp.float32
        ),
        lax.all_gather(summed[2].astype(jnp.bfloat16), "ctx", axis=3, tiled=True).astype(
            jnp.float32
        ),
        lax.all_gather(summed[3].astype(jnp.bfloat16), "ctx", axis=1, tiled=True).astype(
            jnp.float32
        ),
        lax.all_gather(summed[4].astype(jnp.bfloat16), "ctx", axis=0, tiled=True).astype(
            jnp.float32
        ),
        lax.all_gather(summed[5].astype(jnp.bfloat16), "ctx", axis=0, tiled=True).astype(
            jnp.float32
        ),
        lax.all_gather(summed[6].astype(jnp.bfloat16), "ctx", axis=1, tiled=True).astype(
            jnp.float32
        ),
    )
    return (jnp.concatenate(outputs, axis=0), jnp.concatenate(input_grads, axis=0)) + tuple(shares)


def solution(mesh):
    placed = (
        P("fsdp", "ctx", None),
        P("fsdp"),
        P("fsdp", None, "tp"),
        P(None, None, "tp", "fsdp"),
        P("tp", "fsdp"),
        P("fsdp"),
        P("fsdp", "tp"),
        P("tp", "fsdp"),
        P("fsdp", None),
        P("fsdp", None),
        P("fsdp", "ctx", None),
    )

    def on_device(*args):
        if args[0].shape[0] == lax.axis_size("ctx") == 2:
            return row_on_device(*args)
        return any_on_device(*args)

    return jax.shard_map(
        on_device,
        mesh=mesh,
        in_specs=placed,
        out_specs=(
            P("fsdp", "ctx", None),
            P("fsdp", "ctx", None),
            P("fsdp"),
            P("fsdp", None, "tp"),
            P(None, None, "tp", "fsdp"),
            P("tp", "fsdp"),
            P("fsdp"),
            P("fsdp", "tp"),
            P("tp", "fsdp"),
        ),
        check_vma=False,
    )
```

```python
import functools

import jax
import jax.numpy as jnp
from jax import lax
from jax.experimental import pallas as pl
from jax.experimental.pallas import tpu as pltpu
from jax.sharding import PartitionSpec as P


HD = 64
TILE = 256
QUERIES = 512
LOG2E = 1.4426950408889634
NEG = -1e30
MESH = pl.DeviceIdType.MESH
F32 = jnp.float32
BF16 = jnp.bfloat16


def norm_parts(values):
    inverse = lax.rsqrt(jnp.mean(values * values, axis=-1, keepdims=True) + 1e-06)
    return (inverse, values * inverse)


def norm_back(grad_norm, gain_full, inverse, scaled):
    grad_scaled = grad_norm * gain_full
    inner_mean = jnp.mean(grad_scaled * scaled, axis=-1, keepdims=True)
    return inverse * (grad_scaled - scaled * inner_mean)


def dot_nn(a, b):
    return lax.dot_general(a, b, (((1,), (0,)), ((), ())), preferred_element_type=F32)


def dot_nt(a, b):
    return lax.dot_general(a, b, (((1,), (1,)), ((), ())), preferred_element_type=F32)


def dot_tn(a, b):
    return lax.dot_general(a, b, (((0,), (0,)), ((), ())), preferred_element_type=F32)


def three_terms(value):
    one = value.astype(BF16).astype(F32)
    two = (value - one).astype(BF16).astype(F32)
    three = value - one - two
    place = lax.broadcasted_iota(jnp.int32, (16, value.shape[1]), 0)
    rest = jnp.where(place == 1, -two, jnp.where(place == 2, -three, 0.0))
    return jnp.where(place == 0, -one, rest).astype(BF16)


def put_query(query, query_scr, h):
    scaled = query.astype(F32) * (HD ** (-0.5) * LOG2E)
    high = scaled.astype(BF16)
    query_scr[h, :HD, :] = high
    query_scr[h, HD : 2 * HD, :] = (scaled - high.astype(F32)).astype(BF16)


def put_keys(keys, key_scr, h):
    key_scr[h, :, : 2 * HD] = jnp.concatenate([keys, keys], axis=0).T
    key_scr[h, :, 2 * HD :] = jnp.ones_like(key_scr[h, :, 2 * HD :])


def over_keys(i, tiles, first, step):
    ratio = QUERIES // TILE
    for extra in range(ratio):
        step(i * ratio + extra, True)

    @pl.when(i + 1 < tiles)
    def _():
        step((i + 1) * ratio, True)

    def lower(j, carry):
        step(j, False)
        return carry

    lax.fori_loop(first, i * ratio, lower, 0)


def attn_fwd_kernel(heads, lo_ref, hi_ref, qkv_ref, out_ref, lse_ref, key_scr, val_scr, query_scr, peak, acc):
    i = pl.program_id(0)
    tiles = pl.num_programs(0)
    width = heads * HD

    @pl.when(i == 0)
    def _():
        for h in range(heads):
            put_keys(qkv_ref[width + h * HD : width + (h + 1) * HD, :], key_scr, h)
            val_scr[h, :HD, :] = qkv_ref[2 * width + h * HD : 2 * width + (h + 1) * HD, :]
            val_scr[h, HD:, :] = jnp.ones_like(val_scr[h, HD:, :])

    here = pl.ds(pl.multiple_of(i * QUERIES, QUERIES), QUERIES)
    hi = hi_ref[:, here]
    for h in range(heads):
        put_query(qkv_ref[h * HD : (h + 1) * HD, here], query_scr, h)
        query_scr[h, 2 * HD :, :] = jnp.zeros((16, QUERIES), BF16)
    peak[...] = jnp.full_like(peak, NEG)
    acc[...] = jnp.zeros_like(acc)

    def scores_of(j, h, masked):
        there = pl.ds(pl.multiple_of(j * TILE, TILE), TILE)
        scores = dot_nn(key_scr[h, there, :], query_scr[h])
        if masked:
            place = lax.broadcasted_iota(jnp.int32, (TILE, QUERIES), 0) + j * TILE
            scores = jnp.where(place < hi, scores, NEG)
        return scores

    def find_peak(j, masked):
        for h in range(heads):
            scores = scores_of(j, h, masked).reshape(TILE // 8, 8, QUERIES)
            peak[h] = jnp.maximum(peak[h], jnp.max(scores, axis=0))

    over_keys(i, tiles, lo_ref[i], find_peak)
    for h in range(heads):
        top = jnp.max(peak[h], axis=0, keepdims=True)
        lse_ref[h : h + 1, :] = top
        query_scr[h, 2 * HD :, :] = three_terms(top)

    def gather(j, masked):
        there = pl.ds(pl.multiple_of(j * TILE, TILE), TILE)
        for h in range(heads):
            probs = jnp.exp2(scores_of(j, h, masked)).astype(BF16)
            acc[h] += dot_nn(val_scr[h, :, there], probs)

    over_keys(i, tiles, lo_ref[i], gather)
    for h in range(heads):
        total = acc[h, HD : HD + 1, :]
        out_ref[h * HD : (h + 1) * HD, :] = (acc[h, :HD, :] / total).astype(BF16)
        lse_ref[h : h + 1, :] = lse_ref[h : h + 1, :] + jnp.log2(total)


def attn_forward(lo_tile, hi, qkv, heads):
    length = qkv.shape[1]
    tiles = length // QUERIES
    width = heads * HD
    whole = lambda i, *_: (0, 0)
    return pl.pallas_call(
        functools.partial(attn_fwd_kernel, heads),
        out_shape=(
            jax.ShapeDtypeStruct((width, length), BF16),
            jax.ShapeDtypeStruct((8, length), F32),
        ),
        grid_spec=pltpu.PrefetchScalarGridSpec(
            num_scalar_prefetch=1,
            grid=(tiles,),
            in_specs=[
                pl.BlockSpec((1, length), whole),
                pl.BlockSpec((3 * width, length), whole),
            ],
            out_specs=(
                pl.BlockSpec((width, QUERIES), lambda i, *_: (0, i)),
                pl.BlockSpec((8, QUERIES), lambda i, *_: (0, i)),
            ),
            scratch_shapes=[
                pltpu.VMEM((heads, length, 2 * HD + 16), BF16),
                pltpu.VMEM((heads, HD + 16, length), BF16),
                pltpu.VMEM((heads, 2 * HD + 16, QUERIES), BF16),
                pltpu.VMEM((heads, 8, QUERIES), F32),
                pltpu.VMEM((heads, HD + 16, QUERIES), F32),
            ],
        ),
        name="attn_fwd",
    )(lo_tile, hi, qkv)


def attn_bwd_kernel(heads, taps_count, lo_ref, hi_ref, qkv_ref, grad_ref, att_ref, lse_ref, lin_ref, later_ref, taps_ref, out_ref, tap_ref, key_scr, val_scr, query_scr, grad_scr, triple):
    i = pl.program_id(0)
    tiles = pl.num_programs(0)
    width = heads * HD
    here = pl.ds(pl.multiple_of(i * QUERIES, QUERIES), QUERIES)
    scale = HD ** (-0.5)

    @pl.when(i == 0)
    def _():
        for h in range(heads):
            put_keys(qkv_ref[width + h * HD : width + (h + 1) * HD, :], key_scr, h)
            val_scr[h, :, :HD] = qkv_ref[2 * width + h * HD : 2 * width + (h + 1) * HD, :].T
            val_scr[h, :, HD:] = jnp.ones_like(val_scr[h, :, HD:])
        triple[...] = jnp.zeros_like(triple)

    hi = hi_ref[:, here]
    for h in range(heads):
        rows = slice(h * HD, (h + 1) * HD)
        put_query(qkv_ref[rows, here], query_scr, h)
        query_scr[h, 2 * HD :, :] = three_terms(lse_ref[h : h + 1, here])
        grad = grad_ref[rows, here]
        grad_scr[h, :HD, :] = grad
        row_total = jnp.sum(grad.astype(F32) * att_ref[rows, here].astype(F32), axis=0, keepdims=True)
        grad_scr[h, HD:, :] = three_terms(row_total)

    def step(j, masked):
        there = pl.ds(pl.multiple_of(j * TILE, TILE), TILE)
        for h in range(heads):
            q_rows = slice(h * HD, (h + 1) * HD)
            k_rows = slice(width + h * HD, width + (h + 1) * HD)
            v_rows = slice(2 * width + h * HD, 2 * width + (h + 1) * HD)
            scores = dot_nn(key_scr[h, there, :], query_scr[h])
            if masked:
                place = lax.broadcasted_iota(jnp.int32, (TILE, QUERIES), 0) + j * TILE
                scores = jnp.where(place < hi, scores, NEG)
            probs = jnp.exp2(scores)
            shifted = dot_nn(val_scr[h, there, :], grad_scr[h])
            grad_scores = (probs * shifted).astype(BF16)
            triple[v_rows, there] += dot_nt(grad_scr[h, :HD, :], probs.astype(BF16))
            triple[k_rows, there] += dot_nt(qkv_ref[q_rows, here], grad_scores)
            triple[q_rows, here] += dot_nn(qkv_ref[k_rows, there], grad_scores)

    over_keys(i, tiles, lo_ref[i], step)

    @pl.when(i == tiles - 1)
    def _():
        for block in range(3 * heads):
            rows = slice(block * HD, (block + 1) * HD)
            unit = scale if block < 2 * heads else 1.0
            weights = [taps_ref[rows, j : j + 1] for j in range(taps_count)]

            def tile(n, sums):
                start = pl.multiple_of(n * TILE, TILE)
                spot = pl.ds(start, TILE)
                wide = triple[rows, pl.ds(start, TILE + 128)] * unit
                lin = lin_ref[rows, spot].astype(F32)
                total = None
                result = []
                for j in range(taps_count):
                    if j == 0:
                        moved = wide[:, :TILE]
                    else:
                        moved = pltpu.roll(wide, TILE + 128 - j, 1)[:, :TILE] * later_ref[j : j + 1, spot]
                    total = weights[j] * moved if total is None else total + weights[j] * moved
                    product = moved * lin
                    result.append(sums[j] + product[:, :128] + product[:, 128:])
                out_ref[rows, spot] = total.astype(BF16)
                return tuple(result)

            zero = jnp.zeros((HD, 128), F32)
            sums = lax.fori_loop(0, out_ref.shape[1] // TILE, tile, (zero,) * taps_count)
            for j in range(taps_count):
                tap_ref[rows, j : j + 1] = jnp.sum(sums[j], axis=1, keepdims=True)


def attn_backward(lo_tile, hi, qkv, grad, att, lse, linear, later, taps, heads):
    length = qkv.shape[1]
    tiles = length // QUERIES
    width = heads * HD
    taps_count = taps.shape[0]
    later = jnp.pad(later, ((0, 8 - taps_count), (0, 0)))
    columns = jnp.pad(taps.T, ((0, 0), (0, 128 - taps_count)))
    whole = lambda i, *_: (0, 0)
    return pl.pallas_call(
        functools.partial(attn_bwd_kernel, heads, taps_count),
        out_shape=(
            jax.ShapeDtypeStruct((3 * width, length), BF16),
            jax.ShapeDtypeStruct((3 * width, 128), F32),
        ),
        grid_spec=pltpu.PrefetchScalarGridSpec(
            num_scalar_prefetch=1,
            grid=(tiles,),
            in_specs=[
                pl.BlockSpec((1, length), whole),
                pl.BlockSpec((3 * width, length), whole),
                pl.BlockSpec((width, length), whole),
                pl.BlockSpec((width, length), whole),
                pl.BlockSpec((8, length), whole),
                pl.BlockSpec((3 * width, length), whole),
                pl.BlockSpec((8, length), whole),
                pl.BlockSpec((3 * width, 128), whole),
            ],
            out_specs=(
                pl.BlockSpec((3 * width, length), whole),
                pl.BlockSpec((3 * width, 128), whole),
            ),
            scratch_shapes=[
                pltpu.VMEM((heads, length, 2 * HD + 16), BF16),
                pltpu.VMEM((heads, length, HD + 16), BF16),
                pltpu.VMEM((heads, 2 * HD + 16, QUERIES), BF16),
                pltpu.VMEM((heads, HD + 16, QUERIES), BF16),
                pltpu.VMEM((3 * width, length + 128), F32),
            ],
        ),
        name="attn_bwd",
    )(lo_tile, hi, qkv, grad, att, lse, linear, later, columns)


def spread_kernel(ctx_count, tp_count, x_ref, o_ref, send_sem, recv_sem, own_sem):
    peers = ctx_count * tp_count
    me = lax.axis_index("ctx") * tp_count + lax.axis_index("tp")

    def place(k):
        other = lax.rem(me + k, peers)
        return other, {"ctx": other // tp_count, "tp": lax.rem(other, tp_count)}

    barrier = pltpu.get_barrier_semaphore()
    for k in range(1, peers):
        pl.semaphore_signal(barrier, inc=1, device_id=place(k)[1], device_id_type=MESH)
    pl.semaphore_wait(barrier, peers - 1)
    copies = []
    for k in range(1, peers):
        other, device = place(k)
        copies.append(
            pltpu.make_async_remote_copy(
                src_ref=x_ref.at[other],
                dst_ref=o_ref.at[me],
                send_sem=send_sem.at[k - 1],
                recv_sem=recv_sem.at[k - 1],
                device_id=device,
                device_id_type=MESH,
            )
        )
        copies[-1].start()
    own = pltpu.make_async_copy(x_ref.at[me], o_ref.at[me], own_sem)
    own.start()
    own.wait()
    for copy in copies:
        copy.wait()


def spread(x, ctx_count, tp_count, ident):
    peers = ctx_count * tp_count
    return pl.pallas_call(
        functools.partial(spread_kernel, ctx_count, tp_count),
        out_shape=jax.ShapeDtypeStruct(x.shape, x.dtype),
        in_specs=[pl.BlockSpec(memory_space=pltpu.VMEM)],
        out_specs=pl.BlockSpec(memory_space=pltpu.VMEM),
        scratch_shapes=[
            pltpu.SemaphoreType.DMA((peers - 1,)),
            pltpu.SemaphoreType.DMA((peers - 1,)),
            pltpu.SemaphoreType.DMA,
        ],
        compiler_params=pltpu.CompilerParams(collective_id=ident, has_side_effects=True),
    )(x)


def gather_sum_kernel(tp_count, p_ref, o_ref, from_left, from_right, mine, right_sem, left_sem, pair_sem):
    me = lax.axis_index("tp")
    row = lax.axis_index("ctx")
    last = tp_count - 1
    right, left = jnp.minimum(me + 1, last), jnp.maximum(me - 1, 0)

    barrier = pltpu.get_barrier_semaphore()

    @pl.when(me < last)
    def _():
        pl.semaphore_signal(barrier, inc=1, device_id={"tp": right}, device_id_type=MESH)

    @pl.when(me > 0)
    def _():
        pl.semaphore_signal(barrier, inc=1, device_id={"tp": left}, device_id_type=MESH)

    pl.semaphore_signal(barrier, inc=1, device_id={"ctx": 1 - row}, device_id_type=MESH)
    pl.semaphore_wait(barrier, 1 + (me < last).astype(jnp.int32) + (me > 0).astype(jnp.int32))

    def pass_on(source, buffer, half, c, target, sems):
        return pltpu.make_async_remote_copy(
            src_ref=source,
            dst_ref=buffer.at[half, c],
            send_sem=sems.at[0, half, c],
            recv_sem=sems.at[1, half, c],
            device_id={"tp": target},
            device_id_type=MESH,
        )

    def flow(half, c, first, buffer, target, sems):
        @pl.when(first)
        def _():
            pass_on(p_ref.at[half, c], buffer, half, c, target, sems).start()

        @pl.when(jnp.logical_not(first))
        def _():
            copy = pass_on(buffer.at[half, c], buffer, half, c, target, sems)
            copy.wait_recv()
            buffer[half, c] = (buffer[half, c].astype(F32) + p_ref[half, c].astype(F32)).astype(BF16)
            copy.start()

    def pair():
        return pltpu.make_async_remote_copy(
            src_ref=mine,
            dst_ref=o_ref.at[row],
            send_sem=pair_sem.at[0],
            recv_sem=pair_sem.at[1],
            device_id={"ctx": 1 - row},
            device_id_type=MESH,
        )

    for step in range(last):
        for half in (1 - row, row):
            @pl.when(last - step > me)
            def _():
                flow(half, last - step, me == 0, from_left, right, right_sem)

            @pl.when(step < me)
            def _():
                flow(half, step, me == last, from_right, left, left_sem)

    for half in (1 - row, row):
        here = p_ref.at[half, me]

        def come(buffer, sems):
            pass_on(here, buffer, half, me, left, sems).wait_recv()
            return buffer[half, me].astype(F32)

        target = mine if half is not row else o_ref.at[row]

        @pl.when(me == 0)
        def _():
            target[...] = (here[...].astype(F32) + come(from_right, left_sem)).astype(BF16)

        @pl.when(me == last)
        def _():
            target[...] = (here[...].astype(F32) + come(from_left, right_sem)).astype(BF16)

        @pl.when((me > 0) & (me < last))
        def _():
            total = here[...].astype(F32) + come(from_left, right_sem)
            target[...] = (total + come(from_right, left_sem)).astype(BF16)

        if half is not row:
            pair().start()

    for step in range(last):
        for half in (1 - row, row):
            @pl.when(last - step > me)
            def _():
                pass_on(p_ref.at[half, last - step], from_left, half, last - step, right, right_sem).wait_send()

            @pl.when(step < me)
            def _():
                pass_on(p_ref.at[half, step], from_right, half, step, left, left_sem).wait_send()

    pair().wait()


def gather_sum(parts, ident):
    ctx_count, tp_count, size, model = parts.shape
    vmem = pl.BlockSpec(memory_space=pltpu.VMEM)
    return pl.pallas_call(
        functools.partial(gather_sum_kernel, tp_count),
        out_shape=jax.ShapeDtypeStruct((ctx_count, size, model), BF16),
        in_specs=[vmem],
        out_specs=vmem,
        scratch_shapes=[
            pltpu.VMEM(parts.shape, BF16),
            pltpu.VMEM(parts.shape, BF16),
            pltpu.VMEM((size, model), BF16),
            pltpu.SemaphoreType.DMA((2, ctx_count, tp_count)),
            pltpu.SemaphoreType.DMA((2, ctx_count, tp_count)),
            pltpu.SemaphoreType.DMA((2,)),
        ],
        compiler_params=pltpu.CompilerParams(collective_id=ident, has_side_effects=True),
        name="gather_sum",
    )(parts)


def assemble_kernel(part_ref, *refs):
    *chunks, out_ref = refs
    for k, chunk in enumerate(chunks):

        @pl.when(pl.program_id(0) == k)
        def _():
            out_ref[...] = chunk[...]


def assemble(part, chunks):
    count = len(chunks)
    rows, size, model = chunks[0].shape
    fixed = pl.BlockSpec((rows, size, model), lambda k, _: (0, 0, 0))
    return pl.pallas_call(
        assemble_kernel,
        out_shape=jax.ShapeDtypeStruct((rows, count * size, model), chunks[0].dtype),
        grid_spec=pltpu.PrefetchScalarGridSpec(
            num_scalar_prefetch=1,
            grid=(count,),
            in_specs=[fixed] * count,
            out_specs=pl.BlockSpec((rows, size, model), lambda k, part: (0, lax.rem(part[0] + count - k, count), 0)),
        ),
        name="assemble",
    )(part.reshape(1), *chunks)


def finish_kernel(
    ctx_count, tp_count, x_ref, g_ref, q_ref, up_ref, qkv_ref,
    o_ref, s_ref, r_ref, gain_ref,
    came, gains, right_sem, left_sem, part_sem, pair_sem, gain_sem, own_sem,
):
    me = lax.axis_index("tp")
    row = lax.axis_index("ctx")
    size = x_ref.shape[1]
    last = tp_count - 1
    others = [lax.rem(me + k, tp_count) for k in range(1, tp_count)]

    barrier = pltpu.get_barrier_semaphore()
    for other in others:
        pl.semaphore_signal(barrier, inc=1, device_id={"tp": other}, device_id_type=MESH)
    pl.semaphore_signal(barrier, inc=1, device_id={"ctx": 1 - row}, device_id_type=MESH)
    pl.semaphore_wait(barrier, tp_count)

    def send(source, target, sems, index, device):
        return pltpu.make_async_remote_copy(
            src_ref=source,
            dst_ref=target,
            send_sem=sems.at[0, index],
            recv_sem=sems.at[1, index],
            device_id=device,
            device_id_type=MESH,
        )

    def chunk(k):
        return o_ref.at[:, pl.ds(pl.multiple_of(k * size, size), size), :]

    def rightward(step):
        k = jnp.maximum(me - step + 1, 0)
        return send(x_ref if step == 1 else chunk(k), chunk(k), right_sem, step - 1, {"tp": jnp.minimum(me + 1, last)})

    def leftward(step):
        k = jnp.minimum(me + step - 1, last)
        return send(x_ref if step == 1 else chunk(k), chunk(k), left_sem, step - 1, {"tp": jnp.maximum(me - 1, 0)})

    pieces = [send(g_ref.at[other], came.at[k], part_sem, k, {"tp": other}) for k, other in enumerate(others)]
    for piece in pieces:
        piece.start()
    half = r_ref.shape[1]
    pair_q = send(q_ref.at[pl.ds(0, half), :], r_ref.at[row], pair_sem, 0, {"ctx": 1 - row})
    pair_q.start()
    pair_g = send(s_ref.at[row], s_ref.at[row], pair_sem, 1, {"ctx": 1 - row})
    r_ref[row] = q_ref[:half, :]
    own = pltpu.make_async_copy(x_ref, chunk(me), own_sem)
    own.start()
    for step in range(1, tp_count):

        @pl.when((me < last) & (me - step + 1 >= 0))
        def _():
            rightward(step).start()

        @pl.when((me > 0) & (me + step - 1 <= last))
        def _():
            leftward(step).start()

        if step == 1:
            total = g_ref[me].astype(F32)
            for k, piece in enumerate(pieces):
                piece.wait_recv()
                total = total + came[k].astype(F32)
            s_ref[row] = total.astype(BF16)

        @pl.when(me - step >= 0)
        def _():
            rightward(step).wait_recv()

        @pl.when(me + step <= last)
        def _():
            leftward(step).wait_recv()

        if step == 1:
            pair_g.start()
        if step == 2:
            pair_q.wait_recv()
            pair_g.wait_recv()
            units = up_ref.shape[1]
            lane = lax.broadcasted_iota(jnp.int32, (half, 128), 1)
            for c in range(ctx_count):
                rows = slice(c * half, (c + 1) * half)
                first = jnp.sum(r_ref[c].astype(F32) * qkv_ref[rows, :].astype(F32), axis=1, keepdims=True)
                second = jnp.sum(s_ref[c, :, :units].astype(F32) * up_ref[rows, :].astype(F32), axis=1, keepdims=True)
                gains[me, rows, :] = jnp.where(lane == 0, first, second)
    shares = [send(gains.at[me], gains.at[me], gain_sem, k, {"tp": other}) for k, other in enumerate(others)]
    for share in shares:
        share.start()
    for k in range(1, tp_count):
        source = lax.rem(me + tp_count - k, tp_count)
        send(gains.at[source], gains.at[source], gain_sem, k - 1, {"tp": others[k - 1]}).wait_recv()
    total = gains[0]
    for k in range(1, tp_count):
        total = total + gains[k]
    gain_ref[...] = total
    own.wait()
    for step in range(1, tp_count):

        @pl.when((me < last) & (me - step + 1 >= 0))
        def _():
            rightward(step).wait_send()

        @pl.when((me > 0) & (me + step - 1 <= last))
        def _():
            leftward(step).wait_send()

    for copy in pieces + shares + [pair_q, pair_g]:
        copy.wait_send()


def finish(x, g, q, up, qkv, ctx_count, tp_count, ident):
    rows, size, model = x.shape
    vmem = pl.BlockSpec(memory_space=pltpu.VMEM)
    slice_d = up.shape[0]
    return pl.pallas_call(
        functools.partial(finish_kernel, ctx_count, tp_count),
        out_shape=(
            jax.ShapeDtypeStruct((rows, size * tp_count, model), BF16),
            jax.ShapeDtypeStruct((ctx_count,) + g.shape[1:], BF16),
            jax.ShapeDtypeStruct((ctx_count, slice_d // ctx_count, q.shape[1]), BF16),
            jax.ShapeDtypeStruct((slice_d, 128), F32),
        ),
        in_specs=[vmem] * 5,
        out_specs=(vmem,) * 4,
        scratch_shapes=[
            pltpu.VMEM((tp_count - 1,) + g.shape[1:], BF16),
            pltpu.VMEM((tp_count, slice_d, 128), F32),
            pltpu.SemaphoreType.DMA((2, tp_count - 1)),
            pltpu.SemaphoreType.DMA((2, tp_count - 1)),
            pltpu.SemaphoreType.DMA((2, tp_count - 1)),
            pltpu.SemaphoreType.DMA((2, 2)),
            pltpu.SemaphoreType.DMA((2, tp_count - 1)),
            pltpu.SemaphoreType.DMA,
        ],
        compiler_params=pltpu.CompilerParams(collective_id=ident, has_side_effects=True),
        name="finish",
    )(x, g, q, up, qkv)


def weight_grads_kernel(norm_ref, cot_ref, branch_ref, up_ref, hid_ref, att_ref, out_ref, norm_t, cot_t, branch_t):
    @pl.when(pl.program_id(0) == 0)
    def _():
        norm_t[...] = norm_ref[...].T
        cot_t[...] = cot_ref[...].T
        branch_t[...] = branch_ref[...].T

    pieces, _, piece, _ = out_ref.shape
    units = up_ref.shape[2]
    quarter = att_ref.shape[3]

    def put(value, start):
        stop = start + value.shape[1]
        out_ref[:, 0, :, start:stop] = value.astype(BF16).reshape(pieces, piece, value.shape[1])

    put(dot_nn(norm_t[...], up_ref[0]), 0)
    put(dot_nn(cot_t[...], hid_ref[0]), units)
    total = None
    for r in range(att_ref.shape[0]):
        term = dot_nt(branch_t[:, r * quarter : (r + 1) * quarter], att_ref[r, 0])
        total = term if total is None else total + term
    put(total, 2 * units)


def weight_grads(normed, cot, branch, grad_up, hidden, att, pieces):
    tokens, model = normed.shape
    blocks, _, units = hidden.shape
    rows, _, width, quarter = att.shape
    columns = 2 * units + width
    fixed = pl.BlockSpec((tokens, model), lambda b: (0, 0))
    moving = pl.BlockSpec((1, tokens, units), lambda b: (b, 0, 0))
    return pl.pallas_call(
        weight_grads_kernel,
        grid=(blocks,),
        out_shape=jax.ShapeDtypeStruct((pieces, blocks, model // pieces, columns), BF16),
        in_specs=[fixed, fixed, fixed, moving, moving, pl.BlockSpec((rows, 1, width, quarter), lambda b: (0, b, 0, 0))],
        out_specs=pl.BlockSpec((pieces, 1, model // pieces, columns), lambda b: (0, b, 0, 0)),
        scratch_shapes=[pltpu.VMEM((model, tokens), BF16)] * 3,
        name="weight_grads",
    )(normed, cot, branch, grad_up, hidden, att)


def row_on_device(
    tokens, gain_one, w_qkv, kernel, w_out, gain_two, w_up, w_down, block_ids, seq_ids, cotangent
):
    place = lax.axis_index("ctx")
    part = lax.axis_index("tp")
    ctx_count = lax.axis_size("ctx")
    tp_count = lax.axis_size("tp")
    fsdp_count = lax.axis_size("fsdp")
    group_len = tokens.shape[1]
    length = group_len * ctx_count
    model = tokens.shape[2]
    taps_count = kernel.shape[0]
    heads = kernel.shape[2]
    width = heads * HD
    rows = tokens.shape[0]
    quarter = group_len // tp_count
    slice_d = w_up.shape[0]
    units = w_up.shape[1]

    qkv_full = lax.all_gather(w_qkv.reshape(slice_d, 3 * width), "fsdp", axis=0, tiled=True)
    small = jnp.concatenate([gain_one, gain_two, kernel.reshape(-1)])
    small_all = lax.all_gather(small, "fsdp", axis=0).astype(F32)
    gain_first = small_all[:, :slice_d].reshape(-1)
    gain_second = small_all[:, slice_d : 2 * slice_d].reshape(-1)
    taps = small_all[:, 2 * slice_d :].reshape(fsdp_count, taps_count, 3, heads, -1)
    taps = taps.transpose(1, 2, 3, 0, 4).reshape(taps_count, 3 * width)
    packed = jnp.concatenate([w_up, w_down.T, w_out.T], axis=1)
    gathered = lax.all_gather(packed, ("tp", "fsdp"), axis=0, tiled=True)
    gathered = gathered.reshape(tp_count, model, packed.shape[1])
    up_blocks = gathered[:, :, :units]
    down_blocks = gathered[:, :, units : 2 * units]
    out_blocks = gathered[:, :, 2 * units :]

    away = lax.dynamic_index_in_dim(tokens, 1 - place, 0, keepdims=False)
    mine = lax.dynamic_index_in_dim(tokens, place, 0, keepdims=False)
    swap = [(i, 1 - i) for i in range(ctx_count)]
    came = lax.ppermute(away, "ctx", swap)
    row = jnp.where(place == 0, jnp.concatenate([mine, came]), jnp.concatenate([came, mine]))
    block_row = lax.dynamic_index_in_dim(block_ids, place, 0, keepdims=False)
    seq_row = lax.dynamic_index_in_dim(seq_ids, place, 0, keepdims=False)
    owner_row = jnp.repeat(seq_row, group_len)
    code = owner_row * 4096 + block_row
    hi = jnp.sum((code[None, :] <= code[:, None]).astype(jnp.int32), axis=1)[None, :]
    first_piece = jnp.sum((seq_row[None, :] < seq_row[:, None]).astype(jnp.int32), axis=1)
    lo_tile = jnp.repeat(first_piece * (group_len // TILE), group_len // QUERIES)

    row_values = row.astype(F32)
    _, base_row = norm_parts(row_values)
    normed = (base_row * gain_first).astype(BF16)
    linear = dot_tn(qkv_full, normed.T).astype(BF16)
    linear_f = linear.astype(F32)
    same = [
        jnp.concatenate([jnp.zeros((j,), F32), (owner_row[j:] == owner_row[: length - j]).astype(F32)])
        for j in range(taps_count)
    ]
    shifted = [linear_f] + [
        jnp.pad(linear_f[:, : length - j], ((0, 0), (j, 0))) * same[j] for j in range(1, taps_count)
    ]
    triple = sum(taps[j][:, None] * shifted[j] for j in range(taps_count)).astype(BF16)
    att, lse = attn_forward(lo_tile, hi, triple, heads)

    sent = att.reshape(width, ctx_count, tp_count, quarter).transpose(1, 2, 0, 3)
    got = spread(sent.reshape(ctx_count * tp_count, width, quarter), ctx_count, tp_count, 1)
    got = got.reshape(rows, tp_count, width, quarter)
    attended = got.transpose(0, 3, 1, 2).reshape(rows * quarter, tp_count * width)
    states = lax.dynamic_slice_in_dim(tokens, part * quarter, quarter, 1)
    states = states.reshape(rows * quarter, model).astype(F32)
    grad_out = lax.dynamic_slice_in_dim(cotangent, part * quarter, quarter, 1)
    grad_out = grad_out.reshape(rows * quarter, model)
    out_flat = out_blocks.transpose(1, 0, 2).reshape(model, tp_count * width)
    middle = states + dot_nt(attended, out_flat)
    inv_two, base_two = norm_parts(middle)
    normed_two = (base_two * gain_second).astype(BF16)
    upward = jnp.einsum("td,bdu->btu", normed_two, up_blocks, preferred_element_type=F32)
    lifted = jnp.maximum(upward, 0.0)
    hidden = (lifted * lifted).astype(BF16)
    ffn = jnp.einsum("btu,bdu->td", hidden, down_blocks, preferred_element_type=F32)
    block_out = (middle + ffn).astype(BF16).reshape(rows, quarter, model)
    block_out, lifted = lax.optimization_barrier((block_out, lifted))
    grad_hidden = jnp.einsum("td,bdu->btu", grad_out, down_blocks, preferred_element_type=F32)
    grad_upward = (grad_hidden * 2.0 * lifted).astype(BF16)
    grad_norm_two = jnp.einsum("btu,bdu->td", grad_upward, up_blocks, preferred_element_type=F32)
    back_two = norm_back(grad_norm_two, gain_second, inv_two, base_two)
    grad_middle = grad_out.astype(F32) + back_two
    grad_branch = grad_middle.astype(BF16)
    grad_attended = dot_nn(grad_branch, out_flat).astype(BF16)
    grad_packed = weight_grads(normed_two, grad_out, grad_branch, grad_upward, hidden, got, fsdp_count * ctx_count)

    sent = grad_attended.reshape(rows, quarter, tp_count, width).transpose(0, 2, 3, 1)
    sent, grad_packed = lax.optimization_barrier((sent, grad_packed))
    columns = grad_packed.shape[3]
    grad_packed = grad_packed.reshape(-1, columns)
    grad_packed = lax.psum_scatter(grad_packed, ("fsdp", "ctx"), scatter_dimension=0, tiled=True)
    grad_packed = grad_packed.reshape(tp_count, -1, columns)
    got = spread(sent.reshape(rows * tp_count, width, quarter), ctx_count, tp_count, 2)
    got, block_out = lax.optimization_barrier((got, block_out))
    chunks = [block_out]
    for k in range(1, tp_count):
        ring = [(i, (i + k) % tp_count) for i in range(tp_count)]
        chunks.append(lax.ppermute(block_out, "tp", ring))
    got = got.reshape(ctx_count, tp_count, width, quarter)
    grad_att = got.transpose(2, 0, 1, 3).reshape(width, length)
    later = jnp.stack([jnp.pad(same[j][j:], (0, j)) for j in range(taps_count)])
    grad_linear, grad_taps = attn_backward(lo_tile, hi, triple, grad_att, att, lse, linear, later, taps, heads)
    grad_taps = grad_taps[:, :taps_count].T
    grad_qkv = lax.dot_general(
        normed, grad_linear, (((0,), (1,)), ((), ())), preferred_element_type=F32
    )
    sent = lax.dot_general(
        grad_linear, qkv_full, (((0,), (1,)), ((), ())), preferred_element_type=F32
    ).astype(BF16).reshape(ctx_count, tp_count, quarter, model)
    sent, *chunks = lax.optimization_barrier((sent, *chunks))
    block_out = assemble(part, chunks)
    grad_norm_one = gather_sum(sent, 3).astype(F32).reshape(rows * quarter, model)
    inv_one, base_one = norm_parts(states)
    back_one = norm_back(grad_norm_one, gain_first, inv_one, base_one)
    input_grad = (grad_middle + back_one).astype(BF16).reshape(rows, quarter, model)
    halves = fsdp_count * ctx_count
    f_taps = grad_taps.reshape(taps_count * 3 * heads, fsdp_count, -1).transpose(1, 0, 2).reshape(fsdp_count, -1)
    f_taps = jnp.pad(f_taps, ((0, 0), (0, 16 * 3 * width - f_taps.shape[1])))
    f_taps = jnp.repeat(f_taps.reshape(fsdp_count, 16, 3 * width), ctx_count, axis=0)
    half_d = slice_d // ctx_count
    grad_qkv = jnp.concatenate([grad_qkv.reshape(halves, half_d, 3 * width), f_taps], axis=1)
    grad_qkv = grad_qkv.astype(BF16).reshape(halves * (half_d + 16), 3 * width)
    grad_qkv = lax.psum_scatter(grad_qkv, ("fsdp", "ctx"), scatter_dimension=0, tiled=True)
    grad_taps = grad_qkv[half_d:].astype(F32).reshape(-1)[: kernel.size].reshape(kernel.shape)
    input_grad, grad_packed, grad_qkv, gains = finish(
        input_grad, grad_packed, grad_qkv, w_up, w_qkv.reshape(slice_d, 3 * width), ctx_count, tp_count, 4
    )
    input_grad = input_grad.astype(F32)
    grad_packed = grad_packed.reshape(slice_d, columns).astype(F32)
    grad_qkv = grad_qkv.reshape(slice_d, 3 * width).astype(F32)
    gains = gains[:, :2].T / jnp.stack([gain_one, gain_two]).astype(F32)
    return (
        block_out,
        input_grad,
        gains[0],
        grad_qkv.reshape(slice_d, 3, width),
        grad_taps,
        grad_packed[:, 2 * units :].T,
        gains[1],
        grad_packed[:, :units],
        grad_packed[:, units : 2 * units].T,
    )


MICRO = 2
SEQS_MB = 1


def passed_along(block, axis, distance):
    devices = range(lax.axis_size(axis))
    route = [(i - distance, i) for i in devices if i - distance in devices]
    return lax.ppermute(block, axis, route)


def any_norm_parts(values):
    inverse = lax.rsqrt(jnp.mean(values * values, axis=-1, keepdims=True) + 1e-06)
    return (inverse, values * inverse)


def any_norm_back(grad_norm, gain_full, inverse, scaled):
    grad_scaled = grad_norm * gain_full
    inner_mean = jnp.mean(grad_scaled * scaled, axis=-1, keepdims=True)
    return (inverse * (grad_scaled - scaled * inner_mean), jnp.sum(grad_norm * scaled, axis=(0, 1)))


def masked_scores(queries, key_heads, allowed, score_scale):
    scores = (
        jnp.einsum("sqhe,skhe->shqk", queries, key_heads, preferred_element_type=jnp.float32)
        * score_scale
    )
    return jnp.where(allowed[:, None], scores, -1e30)


def tensor_total(values):
    return lax.psum(values, "tp")


def any_on_device(
    tokens, gain_one, w_qkv, kernel, w_out, gain_two, w_up, w_down, block_ids, seq_ids, cotangent
):
    ctx_place = lax.axis_index("ctx")
    ctx_count = lax.axis_size("ctx")
    group_len = tokens.shape[1]
    taps_count = kernel.shape[0]
    margin = taps_count - 1
    local_heads = kernel.shape[2]
    score_scale = HD ** (-0.5)
    per_micro = SEQS_MB
    group_start = ctx_place * group_len
    owner_all = jnp.repeat(seq_ids, group_len, axis=1)
    totals = None
    outputs = []
    input_grads = []
    for micro_step in range(MICRO):
        gathered = (
            lax.all_gather(gain_one, "fsdp", axis=0, tiled=True),
            lax.all_gather(w_qkv, "fsdp", axis=0, tiled=True),
            lax.all_gather(kernel, "fsdp", axis=3, tiled=True),
            lax.all_gather(w_out, "fsdp", axis=1, tiled=True),
            lax.all_gather(gain_two, "fsdp", axis=0, tiled=True),
            lax.all_gather(w_up, "fsdp", axis=0, tiled=True),
            lax.all_gather(w_down, "fsdp", axis=1, tiled=True),
        )
        gain_first, qkv_full, conv_taps, out_full, gain_second, up_full, down_full = gathered
        gain_first = gain_first.astype(jnp.float32)
        gain_second = gain_second.astype(jnp.float32)
        tap_weights = conv_taps.astype(jnp.float32).reshape(taps_count, 3, -1)
        first_row = micro_step * per_micro
        states = tokens[first_row : first_row + per_micro].astype(jnp.float32)
        block_rows = block_ids[first_row : first_row + per_micro]
        owner_rows = owner_all[first_row : first_row + per_micro]
        group_ids = seq_ids[first_row : first_row + per_micro]
        own_group = lax.dynamic_slice_in_dim(group_ids, ctx_place, 1, 1)
        group_before = lax.dynamic_slice_in_dim(group_ids, jnp.maximum(ctx_place - 1, 0), 1, 1)
        group_after = lax.dynamic_slice_in_dim(
            group_ids, jnp.minimum(ctx_place + 1, ctx_count - 1), 1, 1
        )
        keep_before = (group_before == own_group).astype(jnp.float32)[:, :, None, None]
        keep_after = (group_after == own_group).astype(jnp.float32)[:, :, None, None]
        own_blocks = lax.dynamic_slice_in_dim(block_rows, group_start, group_len, 1)
        allowed = (block_rows[:, None, :] <= own_blocks[:, :, None]) & (
            owner_rows[:, None, :] == own_group[:, :, None]
        )
        inv_one, base_one = any_norm_parts(states)
        normed = (base_one * gain_first).astype(jnp.bfloat16)
        linear = jnp.einsum(
            "std,dce->stce", normed, qkv_full, preferred_element_type=jnp.float32
        ).astype(jnp.bfloat16)
        edge_rows = passed_along(linear[:, group_len - margin :], "ctx", 1)
        padded = jnp.concatenate(
            [edge_rows.astype(jnp.float32) * keep_before, linear.astype(jnp.float32)], axis=1
        )
        mixed_conv = sum(
            (
                tap_weights[offset] * padded[:, margin - offset : margin - offset + group_len]
                for offset in range(taps_count)
            )
        )
        triple = mixed_conv.astype(jnp.bfloat16)
        queries = triple[:, :, 0].reshape(per_micro, group_len, local_heads, HD)
        key_pair = lax.all_gather(triple[:, :, 1:], "ctx", axis=1, tiled=True)
        key_heads = key_pair[:, :, 0].reshape(per_micro, -1, local_heads, HD)
        value_heads = key_pair[:, :, 1].reshape(per_micro, -1, local_heads, HD)
        scores = masked_scores(queries, key_heads, allowed, score_scale)
        row_peak = jnp.max(scores, axis=-1, keepdims=True)
        log_total = row_peak + jnp.log(jnp.sum(jnp.exp(scores - row_peak), axis=-1, keepdims=True))
        probs_low = jnp.exp(scores - log_total).astype(jnp.bfloat16)
        attended = jnp.einsum(
            "shqk,skhe->sqhe", probs_low, value_heads, preferred_element_type=jnp.float32
        )
        attended = attended.astype(jnp.bfloat16).reshape(per_micro, group_len, -1)
        attn_part = jnp.einsum(
            "std,de->ste", attended, out_full, preferred_element_type=jnp.float32
        )
        grad_out = cotangent[first_row : first_row + per_micro]
        middle = states + tensor_total(attn_part)
        inv_two, base_two = any_norm_parts(middle)
        normed_two = (base_two * gain_second).astype(jnp.bfloat16)
        upward = jnp.einsum("std,df->stf", normed_two, up_full, preferred_element_type=jnp.float32)
        lifted = jnp.maximum(upward, 0.0)
        hidden = (lifted * lifted).astype(jnp.bfloat16)
        ffn_part = jnp.einsum("stf,fd->std", hidden, down_full, preferred_element_type=jnp.float32)
        outputs.append((middle + tensor_total(ffn_part)).astype(jnp.bfloat16))
        grad_down = jnp.einsum("stf,std->fd", hidden, grad_out, preferred_element_type=jnp.float32)
        grad_hidden = jnp.einsum(
            "std,fd->stf", grad_out, down_full, preferred_element_type=jnp.float32
        )
        grad_upward = (grad_hidden * 2.0 * lifted).astype(jnp.bfloat16)
        grad_up = jnp.einsum(
            "std,stf->df", normed_two, grad_upward, preferred_element_type=jnp.float32
        )
        norm_two_part = jnp.einsum(
            "stf,df->std", grad_upward, up_full, preferred_element_type=jnp.float32
        )
        back_two, grad_gain_two = any_norm_back(
            tensor_total(norm_two_part), gain_second, inv_two, base_two
        )
        grad_middle = grad_out.astype(jnp.float32) + back_two
        grad_branch = grad_middle.astype(jnp.bfloat16)
        grad_out_proj = jnp.einsum(
            "std,ste->de", attended, grad_branch, preferred_element_type=jnp.float32
        )
        grad_attended = jnp.einsum(
            "ste,de->std", grad_branch, out_full, preferred_element_type=jnp.float32
        )
        grad_attended = grad_attended.astype(jnp.bfloat16).reshape(
            per_micro, group_len, local_heads, HD
        )
        prob_full = jnp.exp(masked_scores(queries, key_heads, allowed, score_scale) - log_total)
        grad_probs = jnp.einsum(
            "sqhe,skhe->shqk", grad_attended, value_heads, preferred_element_type=jnp.float32
        )
        row_total = jnp.sum(prob_full * grad_probs, axis=-1, keepdims=True)
        grad_scores = (prob_full * (grad_probs - row_total)).astype(jnp.bfloat16)
        grad_queries = (
            jnp.einsum(
                "shqk,skhe->sqhe", grad_scores, key_heads, preferred_element_type=jnp.float32
            )
            * score_scale
        )
        keys_term = (
            jnp.einsum("shqk,sqhe->skhe", grad_scores, queries, preferred_element_type=jnp.float32)
            * score_scale
        )
        values_term = jnp.einsum(
            "shqk,sqhe->skhe",
            prob_full.astype(jnp.bfloat16),
            grad_attended,
            preferred_element_type=jnp.float32,
        )
        pair_grads = lax.psum_scatter(
            jnp.stack([keys_term, values_term], axis=2).astype(jnp.bfloat16),
            "ctx",
            scatter_dimension=1,
            tiled=True,
        ).astype(jnp.float32)
        grad_keys = pair_grads[:, :, 0]
        grad_values = pair_grads[:, :, 1]
        grad_triple = jnp.stack([grad_queries, grad_keys, grad_values], axis=2).reshape(
            per_micro, group_len, 3, -1
        )
        tail_rows = passed_along(grad_triple[:, :margin], "ctx", -1)
        padded_grad = jnp.concatenate([grad_triple, tail_rows * keep_after], axis=1)
        grad_linear = sum(
            (
                tap_weights[offset] * padded_grad[:, offset : offset + group_len]
                for offset in range(taps_count)
            )
        )
        grad_linear = grad_linear.astype(jnp.bfloat16)
        grad_taps = jnp.stack(
            [
                jnp.sum(
                    grad_triple * padded[:, margin - offset : margin - offset + group_len],
                    axis=(0, 1),
                )
                for offset in range(taps_count)
            ]
        )
        grad_taps = grad_taps.reshape(conv_taps.shape)
        grad_qkv = jnp.einsum(
            "std,stce->dce", normed, grad_linear, preferred_element_type=jnp.float32
        )
        grad_norm_one = tensor_total(
            jnp.einsum("stce,dce->std", grad_linear, qkv_full, preferred_element_type=jnp.float32)
        )
        back_one, grad_gain_one = any_norm_back(grad_norm_one, gain_first, inv_one, base_one)
        input_grads.append(grad_middle + back_one)
        micro_grads = (
            grad_gain_one,
            grad_qkv,
            grad_taps,
            grad_out_proj,
            grad_gain_two,
            grad_up,
            grad_down,
        )
        totals = (
            micro_grads
            if totals is None
            else tuple(
                (left_part + right_part for left_part, right_part in zip(totals, micro_grads))
            )
        )
    summed = (
        lax.psum_scatter(totals[0], ("fsdp", "ctx"), scatter_dimension=0, tiled=True),
        lax.psum_scatter(totals[1], ("fsdp", "ctx"), scatter_dimension=0, tiled=True),
        lax.psum_scatter(totals[2], ("fsdp", "ctx"), scatter_dimension=3, tiled=True),
        lax.psum_scatter(totals[3], ("fsdp", "ctx"), scatter_dimension=1, tiled=True),
        lax.psum_scatter(totals[4], ("fsdp", "ctx"), scatter_dimension=0, tiled=True),
        lax.psum_scatter(totals[5], ("fsdp", "ctx"), scatter_dimension=0, tiled=True),
        lax.psum_scatter(totals[6], ("fsdp", "ctx"), scatter_dimension=1, tiled=True),
    )
    shares = (
        lax.all_gather(summed[0].astype(jnp.bfloat16), "ctx", axis=0, tiled=True).astype(
            jnp.float32
        ),
        lax.all_gather(summed[1].astype(jnp.bfloat16), "ctx", axis=0, tiled=True).astype(
            jnp.float32
        ),
        lax.all_gather(summed[2].astype(jnp.bfloat16), "ctx", axis=3, tiled=True).astype(
            jnp.float32
        ),
        lax.all_gather(summed[3].astype(jnp.bfloat16), "ctx", axis=1, tiled=True).astype(
            jnp.float32
        ),
        lax.all_gather(summed[4].astype(jnp.bfloat16), "ctx", axis=0, tiled=True).astype(
            jnp.float32
        ),
        lax.all_gather(summed[5].astype(jnp.bfloat16), "ctx", axis=0, tiled=True).astype(
            jnp.float32
        ),
        lax.all_gather(summed[6].astype(jnp.bfloat16), "ctx", axis=1, tiled=True).astype(
            jnp.float32
        ),
    )
    return (jnp.concatenate(outputs, axis=0), jnp.concatenate(input_grads, axis=0)) + tuple(shares)


def solution(mesh):
    placed = (
        P("fsdp", "ctx", None),
        P("fsdp"),
        P("fsdp", None, "tp"),
        P(None, None, "tp", "fsdp"),
        P("tp", "fsdp"),
        P("fsdp"),
        P("fsdp", "tp"),
        P("tp", "fsdp"),
        P("fsdp", None),
        P("fsdp", None),
        P("fsdp", "ctx", None),
    )

    def on_device(*args):
        if args[0].shape[0] == lax.axis_size("ctx") == 2:
            return row_on_device(*args)
        return any_on_device(*args)

    return jax.shard_map(
        on_device,
        mesh=mesh,
        in_specs=placed,
        out_specs=(
            P("fsdp", "ctx", None),
            P("fsdp", "ctx", None),
            P("fsdp"),
            P("fsdp", None, "tp"),
            P(None, None, "tp", "fsdp"),
            P("tp", "fsdp"),
            P("fsdp"),
            P("fsdp", "tp"),
            P("tp", "fsdp"),
        ),
        check_vma=False,
    )
```

```python
import functools

import jax
import jax.numpy as jnp
from jax import lax
from jax.experimental import pallas as pl
from jax.experimental.pallas import tpu as pltpu
from jax.sharding import PartitionSpec as P


HD = 64
TILE = 256
QUERIES = 512
LOG2E = 1.4426950408889634
NEG = -1e30
MESH = pl.DeviceIdType.MESH
F32 = jnp.float32
BF16 = jnp.bfloat16


def norm_parts(values):
    inverse = lax.rsqrt(jnp.mean(values * values, axis=-1, keepdims=True) + 1e-06)
    return (inverse, values * inverse)


def norm_back(grad_norm, gain_full, inverse, scaled):
    grad_scaled = grad_norm * gain_full
    inner_mean = jnp.mean(grad_scaled * scaled, axis=-1, keepdims=True)
    return inverse * (grad_scaled - scaled * inner_mean)


def dot_nn(a, b):
    return lax.dot_general(a, b, (((1,), (0,)), ((), ())), preferred_element_type=F32)


def dot_nt(a, b):
    return lax.dot_general(a, b, (((1,), (1,)), ((), ())), preferred_element_type=F32)


def dot_tn(a, b):
    return lax.dot_general(a, b, (((0,), (0,)), ((), ())), preferred_element_type=F32)


def three_terms(value):
    one = value.astype(BF16).astype(F32)
    two = (value - one).astype(BF16).astype(F32)
    three = value - one - two
    place = lax.broadcasted_iota(jnp.int32, (16, value.shape[1]), 0)
    rest = jnp.where(place == 1, -two, jnp.where(place == 2, -three, 0.0))
    return jnp.where(place == 0, -one, rest).astype(BF16)


def put_query(query, query_scr, h):
    scaled = query.astype(F32) * (HD ** (-0.5) * LOG2E)
    high = scaled.astype(BF16)
    query_scr[h, :HD, :] = high
    query_scr[h, HD : 2 * HD, :] = (scaled - high.astype(F32)).astype(BF16)


def put_keys(keys, key_scr, h):
    key_scr[h, :, : 2 * HD] = jnp.concatenate([keys, keys], axis=0).T
    key_scr[h, :, 2 * HD :] = jnp.ones_like(key_scr[h, :, 2 * HD :])


def over_keys(i, tiles, first, step):
    ratio = QUERIES // TILE
    for extra in range(ratio):
        step(i * ratio + extra, True)

    @pl.when(i + 1 < tiles)
    def _():
        step((i + 1) * ratio, True)

    def lower(j, carry):
        step(j, False)
        return carry

    lax.fori_loop(first, i * ratio, lower, 0)


def attn_fwd_kernel(heads, lo_ref, hi_ref, qkv_ref, out_ref, lse_ref, key_scr, val_scr, query_scr, peak, acc):
    i = pl.program_id(0)
    tiles = pl.num_programs(0)
    width = heads * HD

    @pl.when(i == 0)
    def _():
        for h in range(heads):
            put_keys(qkv_ref[width + h * HD : width + (h + 1) * HD, :], key_scr, h)
            val_scr[h, :HD, :] = qkv_ref[2 * width + h * HD : 2 * width + (h + 1) * HD, :]
            val_scr[h, HD:, :] = jnp.ones_like(val_scr[h, HD:, :])

    here = pl.ds(pl.multiple_of(i * QUERIES, QUERIES), QUERIES)
    hi = hi_ref[:, here]
    for h in range(heads):
        put_query(qkv_ref[h * HD : (h + 1) * HD, here], query_scr, h)
        query_scr[h, 2 * HD :, :] = jnp.zeros((16, QUERIES), BF16)
    peak[...] = jnp.full_like(peak, NEG)
    acc[...] = jnp.zeros_like(acc)

    def scores_of(j, h, masked):
        there = pl.ds(pl.multiple_of(j * TILE, TILE), TILE)
        scores = dot_nn(key_scr[h, there, :], query_scr[h])
        if masked:
            place = lax.broadcasted_iota(jnp.int32, (TILE, QUERIES), 0) + j * TILE
            scores = jnp.where(place < hi, scores, NEG)
        return scores

    def find_peak(j, masked):
        for h in range(heads):
            scores = scores_of(j, h, masked).reshape(TILE // 8, 8, QUERIES)
            peak[h] = jnp.maximum(peak[h], jnp.max(scores, axis=0))

    over_keys(i, tiles, lo_ref[i], find_peak)
    for h in range(heads):
        top = jnp.max(peak[h], axis=0, keepdims=True)
        lse_ref[h : h + 1, :] = top
        query_scr[h, 2 * HD :, :] = three_terms(top)

    def gather(j, masked):
        there = pl.ds(pl.multiple_of(j * TILE, TILE), TILE)
        for h in range(heads):
            probs = jnp.exp2(scores_of(j, h, masked)).astype(BF16)
            acc[h] += dot_nn(val_scr[h, :, there], probs)

    over_keys(i, tiles, lo_ref[i], gather)
    for h in range(heads):
        total = acc[h, HD : HD + 1, :]
        out_ref[h * HD : (h + 1) * HD, :] = (acc[h, :HD, :] / total).astype(BF16)
        lse_ref[h : h + 1, :] = lse_ref[h : h + 1, :] + jnp.log2(total)


def attn_forward(lo_tile, hi, qkv, heads):
    length = qkv.shape[1]
    tiles = length // QUERIES
    width = heads * HD
    whole = lambda i, *_: (0, 0)
    return pl.pallas_call(
        functools.partial(attn_fwd_kernel, heads),
        out_shape=(
            jax.ShapeDtypeStruct((width, length), BF16),
            jax.ShapeDtypeStruct((8, length), F32),
        ),
        grid_spec=pltpu.PrefetchScalarGridSpec(
            num_scalar_prefetch=1,
            grid=(tiles,),
            in_specs=[
                pl.BlockSpec((1, length), whole),
                pl.BlockSpec((3 * width, length), whole),
            ],
            out_specs=(
                pl.BlockSpec((width, QUERIES), lambda i, *_: (0, i)),
                pl.BlockSpec((8, QUERIES), lambda i, *_: (0, i)),
            ),
            scratch_shapes=[
                pltpu.VMEM((heads, length, 2 * HD + 16), BF16),
                pltpu.VMEM((heads, HD + 16, length), BF16),
                pltpu.VMEM((heads, 2 * HD + 16, QUERIES), BF16),
                pltpu.VMEM((heads, 8, QUERIES), F32),
                pltpu.VMEM((heads, HD + 16, QUERIES), F32),
            ],
        ),
        name="attn_fwd",
    )(lo_tile, hi, qkv)


def attn_bwd_kernel(heads, taps_count, lo_ref, hi_ref, qkv_ref, grad_ref, att_ref, lse_ref, lin_ref, later_ref, taps_ref, out_ref, tap_ref, key_scr, val_scr, query_scr, grad_scr, triple):
    i = pl.program_id(0)
    tiles = pl.num_programs(0)
    width = heads * HD
    here = pl.ds(pl.multiple_of(i * QUERIES, QUERIES), QUERIES)
    scale = HD ** (-0.5)

    @pl.when(i == 0)
    def _():
        for h in range(heads):
            put_keys(qkv_ref[width + h * HD : width + (h + 1) * HD, :], key_scr, h)
            val_scr[h, :, :HD] = qkv_ref[2 * width + h * HD : 2 * width + (h + 1) * HD, :].T
            val_scr[h, :, HD:] = jnp.ones_like(val_scr[h, :, HD:])
        triple[...] = jnp.zeros_like(triple)

    hi = hi_ref[:, here]
    for h in range(heads):
        rows = slice(h * HD, (h + 1) * HD)
        put_query(qkv_ref[rows, here], query_scr, h)
        query_scr[h, 2 * HD :, :] = three_terms(lse_ref[h : h + 1, here])
        grad = grad_ref[rows, here]
        grad_scr[h, :HD, :] = grad
        row_total = jnp.sum(grad.astype(F32) * att_ref[rows, here].astype(F32), axis=0, keepdims=True)
        grad_scr[h, HD:, :] = three_terms(row_total)

    def step(j, masked):
        there = pl.ds(pl.multiple_of(j * TILE, TILE), TILE)
        for h in range(heads):
            q_rows = slice(h * HD, (h + 1) * HD)
            k_rows = slice(width + h * HD, width + (h + 1) * HD)
            v_rows = slice(2 * width + h * HD, 2 * width + (h + 1) * HD)
            scores = dot_nn(key_scr[h, there, :], query_scr[h])
            if masked:
                place = lax.broadcasted_iota(jnp.int32, (TILE, QUERIES), 0) + j * TILE
                scores = jnp.where(place < hi, scores, NEG)
            probs = jnp.exp2(scores)
            shifted = dot_nn(val_scr[h, there, :], grad_scr[h])
            grad_scores = (probs * shifted).astype(BF16)
            triple[v_rows, there] += dot_nt(grad_scr[h, :HD, :], probs.astype(BF16))
            triple[k_rows, there] += dot_nt(qkv_ref[q_rows, here], grad_scores)
            triple[q_rows, here] += dot_nn(qkv_ref[k_rows, there], grad_scores)

    over_keys(i, tiles, lo_ref[i], step)

    @pl.when(i == tiles - 1)
    def _():
        for block in range(3 * heads):
            rows = slice(block * HD, (block + 1) * HD)
            unit = scale if block < 2 * heads else 1.0
            weights = [taps_ref[rows, j : j + 1] for j in range(taps_count)]

            def tile(n, sums):
                start = pl.multiple_of(n * TILE, TILE)
                spot = pl.ds(start, TILE)
                wide = triple[rows, pl.ds(start, TILE + 128)] * unit
                lin = lin_ref[rows, spot].astype(F32)
                total = None
                result = []
                for j in range(taps_count):
                    if j == 0:
                        moved = wide[:, :TILE]
                    else:
                        moved = pltpu.roll(wide, TILE + 128 - j, 1)[:, :TILE] * later_ref[j : j + 1, spot]
                    total = weights[j] * moved if total is None else total + weights[j] * moved
                    product = moved * lin
                    result.append(sums[j] + product[:, :128] + product[:, 128:])
                out_ref[rows, spot] = total.astype(BF16)
                return tuple(result)

            zero = jnp.zeros((HD, 128), F32)
            sums = lax.fori_loop(0, out_ref.shape[1] // TILE, tile, (zero,) * taps_count)
            for j in range(taps_count):
                tap_ref[rows, j : j + 1] = jnp.sum(sums[j], axis=1, keepdims=True)


def attn_backward(lo_tile, hi, qkv, grad, att, lse, linear, later, taps, heads):
    length = qkv.shape[1]
    tiles = length // QUERIES
    width = heads * HD
    taps_count = taps.shape[0]
    later = jnp.pad(later, ((0, 8 - taps_count), (0, 0)))
    columns = jnp.pad(taps.T, ((0, 0), (0, 128 - taps_count)))
    whole = lambda i, *_: (0, 0)
    return pl.pallas_call(
        functools.partial(attn_bwd_kernel, heads, taps_count),
        out_shape=(
            jax.ShapeDtypeStruct((3 * width, length), BF16),
            jax.ShapeDtypeStruct((3 * width, 128), F32),
        ),
        grid_spec=pltpu.PrefetchScalarGridSpec(
            num_scalar_prefetch=1,
            grid=(tiles,),
            in_specs=[
                pl.BlockSpec((1, length), whole),
                pl.BlockSpec((3 * width, length), whole),
                pl.BlockSpec((width, length), whole),
                pl.BlockSpec((width, length), whole),
                pl.BlockSpec((8, length), whole),
                pl.BlockSpec((3 * width, length), whole),
                pl.BlockSpec((8, length), whole),
                pl.BlockSpec((3 * width, 128), whole),
            ],
            out_specs=(
                pl.BlockSpec((3 * width, length), whole),
                pl.BlockSpec((3 * width, 128), whole),
            ),
            scratch_shapes=[
                pltpu.VMEM((heads, length, 2 * HD + 16), BF16),
                pltpu.VMEM((heads, length, HD + 16), BF16),
                pltpu.VMEM((heads, 2 * HD + 16, QUERIES), BF16),
                pltpu.VMEM((heads, HD + 16, QUERIES), BF16),
                pltpu.VMEM((3 * width, length + 128), F32),
            ],
        ),
        name="attn_bwd",
    )(lo_tile, hi, qkv, grad, att, lse, linear, later, columns)


def spread_kernel(ctx_count, tp_count, x_ref, o_ref, send_sem, recv_sem, own_sem):
    peers = ctx_count * tp_count
    me = lax.axis_index("ctx") * tp_count + lax.axis_index("tp")

    def place(k):
        other = lax.rem(me + k, peers)
        return other, {"ctx": other // tp_count, "tp": lax.rem(other, tp_count)}

    barrier = pltpu.get_barrier_semaphore()
    for k in range(1, peers):
        pl.semaphore_signal(barrier, inc=1, device_id=place(k)[1], device_id_type=MESH)
    pl.semaphore_wait(barrier, peers - 1)
    copies = []
    for k in range(1, peers):
        other, device = place(k)
        copies.append(
            pltpu.make_async_remote_copy(
                src_ref=x_ref.at[other],
                dst_ref=o_ref.at[me],
                send_sem=send_sem.at[k - 1],
                recv_sem=recv_sem.at[k - 1],
                device_id=device,
                device_id_type=MESH,
            )
        )
        copies[-1].start()
    own = pltpu.make_async_copy(x_ref.at[me], o_ref.at[me], own_sem)
    own.start()
    own.wait()
    for copy in copies:
        copy.wait()


def spread(x, ctx_count, tp_count, ident):
    peers = ctx_count * tp_count
    return pl.pallas_call(
        functools.partial(spread_kernel, ctx_count, tp_count),
        out_shape=jax.ShapeDtypeStruct(x.shape, x.dtype),
        in_specs=[pl.BlockSpec(memory_space=pltpu.VMEM)],
        out_specs=pl.BlockSpec(memory_space=pltpu.VMEM),
        scratch_shapes=[
            pltpu.SemaphoreType.DMA((peers - 1,)),
            pltpu.SemaphoreType.DMA((peers - 1,)),
            pltpu.SemaphoreType.DMA,
        ],
        compiler_params=pltpu.CompilerParams(collective_id=ident, has_side_effects=True),
    )(x)


def signal_all(devices):
    barrier = pltpu.get_barrier_semaphore()
    for device in devices:
        pl.semaphore_signal(barrier, inc=1, device_id=device, device_id_type=MESH)
    pl.semaphore_wait(barrier, len(devices))


def remote(source, target, sems, index, device):
    return pltpu.make_async_remote_copy(
        src_ref=source,
        dst_ref=target,
        send_sem=sems.at[(0,) + index],
        recv_sem=sems.at[(1,) + index],
        device_id=device,
        device_id_type=MESH,
    )


def add_up(target, *sources):
    def block(n, carry):
        rows = pl.ds(pl.multiple_of(n * 32, 32), 32)
        total = sources[0][rows, :].astype(F32)
        for source in sources[1:]:
            total = total + source[rows, :].astype(F32)
        target[rows, :] = total.astype(target.dtype)
        return carry

    lax.fori_loop(0, target.shape[0] // 32, block, 0)


def tail_kernel(
    tp_count, p_ref, x_ref, middle_ref, gain_ref, g_ref,
    o_ref, s_ref,
    from_left, from_right, mine, norm, result, came,
    right_sum, left_sum, pair_sem, right_sem, left_sem, part_sem, own_sem,
):
    me = lax.axis_index("tp")
    row = lax.axis_index("ctx")
    last = tp_count - 1
    right, left = {"tp": jnp.minimum(me + 1, last)}, {"tp": jnp.maximum(me - 1, 0)}
    others = [lax.rem(me + k, tp_count) for k in range(1, tp_count)]
    halves = (1 - row, row)
    size = x_ref.shape[1]
    signal_all([{"tp": other} for other in others] + [{"ctx": 1 - row}])

    def flow(n, c, going, first, buffer, target, sems):
        half = halves[n]

        @pl.when(going & first)
        def _():
            remote(p_ref.at[half, c], buffer.at[n, c], sems, (n, c), target).start()

        @pl.when(going & jnp.logical_not(first))
        def _():
            copy = remote(buffer.at[n, c], buffer.at[n, c], sems, (n, c), target)
            copy.wait_recv()
            add_up(buffer.at[n, c], buffer.at[n, c], p_ref.at[half, c])
            copy.start()

    def flows(n, step):
        flow(n, last - step, last - step > me, me == 0, from_left, right, right_sum)
        flow(n, step, step < me, me == last, from_right, left, left_sum)

    def flows_sent(n, step):
        @pl.when(last - step > me)
        def _():
            remote(p_ref.at[0, 0], from_left.at[n, last - step], right_sum, (n, last - step), right).wait_send()

        @pl.when(step < me)
        def _():
            remote(p_ref.at[0, 0], from_right.at[n, step], left_sum, (n, step), left).wait_send()

    def final(n, target):
        here = p_ref.at[halves[n], me]

        @pl.when(me > 0)
        def _():
            remote(here, from_left.at[n, me], right_sum, (n, me), right).wait_recv()

        @pl.when(me < last)
        def _():
            remote(here, from_right.at[n, me], left_sum, (n, me), left).wait_recv()

        @pl.when(me == 0)
        def _():
            add_up(target, here, from_right.at[n, me])

        @pl.when(me == last)
        def _():
            add_up(target, here, from_left.at[n, me])

        @pl.when((me > 0) & (me < last))
        def _():
            add_up(target, here, from_left.at[n, me], from_right.at[n, me])

    def norm_backward(r):
        def block(n, carry):
            rows = pl.ds(pl.multiple_of(n * 32, 32), 32)
            values = x_ref[r, rows, :].astype(F32)
            inverse = lax.rsqrt(jnp.mean(values * values, axis=-1, keepdims=True) + 1e-06)
            base = values * inverse
            grad = norm[r, rows, :].astype(F32) * gain_ref[...]
            inner = jnp.mean(grad * base, axis=-1, keepdims=True)
            result[r, rows, :] = (middle_ref[r, rows, :] + inverse * (grad - base * inner)).astype(BF16)
            return carry

        lax.fori_loop(0, size // 32, block, 0)

    def chunk(r, k):
        return o_ref.at[r, pl.ds(pl.multiple_of(k * size, size), size), :]

    def rightward(n, step):
        k = jnp.maximum(me - step + 1, 0)
        target = chunk(halves[n], k)
        return remote(result.at[halves[n]] if step == 1 else target, target, right_sem, (n, step - 1), right)

    def leftward(n, step):
        k = jnp.minimum(me + step - 1, last)
        target = chunk(halves[n], k)
        return remote(result.at[halves[n]] if step == 1 else target, target, left_sem, (n, step - 1), left)

    def spread_start(n, step):
        @pl.when((me < last) & (me - step + 1 >= 0))
        def _():
            rightward(n, step).start()

        @pl.when((me > 0) & (me + step - 1 <= last))
        def _():
            leftward(n, step).start()

    def spread_come(n, step):
        @pl.when(me - step >= 0)
        def _():
            rightward(n, step).wait_recv()

        @pl.when(me + step <= last)
        def _():
            leftward(n, step).wait_recv()

    def spread_sent(n, step):
        @pl.when((me < last) & (me - step + 1 >= 0))
        def _():
            rightward(n, step).wait_send()

        @pl.when((me > 0) & (me + step - 1 <= last))
        def _():
            leftward(n, step).wait_send()

    def own(n):
        return pltpu.make_async_copy(result.at[halves[n]], chunk(halves[n], me), own_sem.at[n])

    pieces = [remote(g_ref.at[other], came.at[k], part_sem, (k,), {"tp": other}) for k, other in enumerate(others)]
    pair = remote(mine, norm.at[row], pair_sem, (0,), {"ctx": 1 - row})
    pair_g = remote(s_ref.at[row], s_ref.at[row], pair_sem, (1,), {"ctx": 1 - row})

    for step in range(last):
        flows(0, step)
    flows(1, 0)
    final(0, mine)
    pair.start()
    for piece in pieces:
        piece.start()
    for step in range(1, last):
        if step == 1:
            pair.wait_recv()
            norm_backward(halves[0])
            own(0).start()
        spread_start(0, step)
        flows(1, step)
        spread_come(0, step)
    final(1, norm.at[row])
    norm_backward(halves[1])
    own(1).start()
    spread_start(1, 1)
    spread_start(0, last)
    for piece in pieces:
        piece.wait_recv()
    add_up(s_ref.at[row], g_ref.at[me], *[came.at[k] for k in range(tp_count - 1)])
    for step in range(1, tp_count):
        spread_come(1, step)
        if step < last:
            spread_start(1, step + 1)
        if step == 1:
            pair_g.start()
    spread_come(0, last)
    for n in range(2):
        own(n).wait()
        for step in range(last):
            flows_sent(n, step)
            spread_sent(n, step + 1)
    for copy in pieces:
        copy.wait_send()
    pair.wait_send()
    pair_g.wait()


def tail(parts, x, middle, gain, g, ident):
    ctx_count, tp_count, size, model = parts.shape
    vmem = pl.BlockSpec(memory_space=pltpu.VMEM)
    return pl.pallas_call(
        functools.partial(tail_kernel, tp_count),
        out_shape=(
            jax.ShapeDtypeStruct((ctx_count, size * tp_count, model), BF16),
            jax.ShapeDtypeStruct((ctx_count,) + g.shape[1:], BF16),
        ),
        in_specs=[vmem] * 5,
        out_specs=(vmem,) * 2,
        scratch_shapes=[
            pltpu.VMEM(parts.shape, BF16),
            pltpu.VMEM(parts.shape, BF16),
            pltpu.VMEM((size, model), BF16),
            pltpu.VMEM(x.shape, BF16),
            pltpu.VMEM(x.shape, BF16),
            pltpu.VMEM((tp_count - 1,) + g.shape[1:], BF16),
            pltpu.SemaphoreType.DMA((2, ctx_count, tp_count)),
            pltpu.SemaphoreType.DMA((2, ctx_count, tp_count)),
            pltpu.SemaphoreType.DMA((2, 2)),
            pltpu.SemaphoreType.DMA((2, ctx_count, tp_count - 1)),
            pltpu.SemaphoreType.DMA((2, ctx_count, tp_count - 1)),
            pltpu.SemaphoreType.DMA((2, tp_count - 1)),
            pltpu.SemaphoreType.DMA((2,)),
        ],
        compiler_params=pltpu.CompilerParams(collective_id=ident, has_side_effects=True),
        name="tail",
    )(parts, x, middle, gain, g)


def assemble_kernel(part_ref, *refs):
    *chunks, out_ref = refs
    for k, chunk in enumerate(chunks):

        @pl.when(pl.program_id(0) == k)
        def _():
            out_ref[...] = chunk[...]


def assemble(part, chunks):
    count = len(chunks)
    rows, size, model = chunks[0].shape
    fixed = pl.BlockSpec((rows, size, model), lambda k, _: (0, 0, 0))
    return pl.pallas_call(
        assemble_kernel,
        out_shape=jax.ShapeDtypeStruct((rows, count * size, model), chunks[0].dtype),
        grid_spec=pltpu.PrefetchScalarGridSpec(
            num_scalar_prefetch=1,
            grid=(count,),
            in_specs=[fixed] * count,
            out_specs=pl.BlockSpec((rows, size, model), lambda k, part: (0, lax.rem(part[0] + count - k, count), 0)),
        ),
        name="assemble",
    )(part.reshape(1), *chunks)


def finish_kernel(ctx_count, tp_count, s_ref, q_ref, up_ref, qkv_ref, r_ref, gain_ref, gains, pair_sem, gain_sem):
    me = lax.axis_index("tp")
    row = lax.axis_index("ctx")
    others = [lax.rem(me + k, tp_count) for k in range(1, tp_count)]
    signal_all([{"tp": other} for other in others] + [{"ctx": 1 - row}])
    half = r_ref.shape[1]
    pair = remote(q_ref.at[pl.ds(0, half), :], r_ref.at[row], pair_sem, (), {"ctx": 1 - row})
    pair.start()
    r_ref[row] = q_ref[:half, :]
    units = up_ref.shape[1]
    second = []
    for c in range(ctx_count):
        rows = slice(c * half, (c + 1) * half)
        second.append(jnp.sum(s_ref[c, :, :units].astype(F32) * up_ref[rows, :].astype(F32), axis=1, keepdims=True))
    pair.wait_recv()
    lane = lax.broadcasted_iota(jnp.int32, (half, 128), 1)
    for c in range(ctx_count):
        rows = slice(c * half, (c + 1) * half)
        first = jnp.sum(r_ref[c].astype(F32) * qkv_ref[rows, :].astype(F32), axis=1, keepdims=True)
        gains[me, rows, :] = jnp.where(lane == 0, first, second[c])
    shares = [remote(gains.at[me], gains.at[me], gain_sem, (k,), {"tp": other}) for k, other in enumerate(others)]
    for share in shares:
        share.start()
    for k in range(1, tp_count):
        source = lax.rem(me + tp_count - k, tp_count)
        remote(gains.at[source], gains.at[source], gain_sem, (k - 1,), {"tp": others[k - 1]}).wait_recv()
    total = gains[0]
    for k in range(1, tp_count):
        total = total + gains[k]
    gain_ref[...] = total
    for copy in shares + [pair]:
        copy.wait_send()


def finish(s, q, up, qkv, ctx_count, tp_count, ident):
    vmem = pl.BlockSpec(memory_space=pltpu.VMEM)
    slice_d = up.shape[0]
    return pl.pallas_call(
        functools.partial(finish_kernel, ctx_count, tp_count),
        out_shape=(
            jax.ShapeDtypeStruct((ctx_count, slice_d // ctx_count, q.shape[1]), BF16),
            jax.ShapeDtypeStruct((slice_d, 128), F32),
        ),
        in_specs=[vmem] * 4,
        out_specs=(vmem,) * 2,
        scratch_shapes=[
            pltpu.VMEM((tp_count, slice_d, 128), F32),
            pltpu.SemaphoreType.DMA((2,)),
            pltpu.SemaphoreType.DMA((2, tp_count - 1)),
        ],
        compiler_params=pltpu.CompilerParams(collective_id=ident, has_side_effects=True),
        name="finish",
    )(s, q, up, qkv)


def weight_grads_kernel(norm_ref, cot_ref, branch_ref, up_ref, hid_ref, att_ref, out_ref, norm_t, cot_t, branch_t):
    @pl.when(pl.program_id(0) == 0)
    def _():
        norm_t[...] = norm_ref[...].T
        cot_t[...] = cot_ref[...].T
        branch_t[...] = branch_ref[...].T

    pieces, _, piece, _ = out_ref.shape
    units = up_ref.shape[2]
    quarter = att_ref.shape[3]

    def put(value, start):
        stop = start + value.shape[1]
        out_ref[:, 0, :, start:stop] = value.astype(BF16).reshape(pieces, piece, value.shape[1])

    put(dot_nn(norm_t[...], up_ref[0]), 0)
    put(dot_nn(cot_t[...], hid_ref[0]), units)
    total = None
    for r in range(att_ref.shape[0]):
        term = dot_nt(branch_t[:, r * quarter : (r + 1) * quarter], att_ref[r, 0])
        total = term if total is None else total + term
    put(total, 2 * units)


def weight_grads(normed, cot, branch, grad_up, hidden, att, pieces):
    tokens, model = normed.shape
    blocks, _, units = hidden.shape
    rows, _, width, quarter = att.shape
    columns = 2 * units + width
    fixed = pl.BlockSpec((tokens, model), lambda b: (0, 0))
    moving = pl.BlockSpec((1, tokens, units), lambda b: (b, 0, 0))
    return pl.pallas_call(
        weight_grads_kernel,
        grid=(blocks,),
        out_shape=jax.ShapeDtypeStruct((pieces, blocks, model // pieces, columns), BF16),
        in_specs=[fixed, fixed, fixed, moving, moving, pl.BlockSpec((rows, 1, width, quarter), lambda b: (0, b, 0, 0))],
        out_specs=pl.BlockSpec((pieces, 1, model // pieces, columns), lambda b: (0, b, 0, 0)),
        scratch_shapes=[pltpu.VMEM((model, tokens), BF16)] * 3,
        name="weight_grads",
    )(normed, cot, branch, grad_up, hidden, att)


def row_on_device(
    tokens, gain_one, w_qkv, kernel, w_out, gain_two, w_up, w_down, block_ids, seq_ids, cotangent
):
    place = lax.axis_index("ctx")
    part = lax.axis_index("tp")
    ctx_count = lax.axis_size("ctx")
    tp_count = lax.axis_size("tp")
    fsdp_count = lax.axis_size("fsdp")
    group_len = tokens.shape[1]
    length = group_len * ctx_count
    model = tokens.shape[2]
    taps_count = kernel.shape[0]
    heads = kernel.shape[2]
    width = heads * HD
    rows = tokens.shape[0]
    quarter = group_len // tp_count
    slice_d = w_up.shape[0]
    units = w_up.shape[1]

    qkv_full = lax.all_gather(w_qkv.reshape(slice_d, 3 * width), "fsdp", axis=0, tiled=True)
    small = jnp.concatenate([gain_one, gain_two, kernel.reshape(-1)])
    small_all = lax.all_gather(small, "fsdp", axis=0).astype(F32)
    gain_first = small_all[:, :slice_d].reshape(-1)
    gain_second = small_all[:, slice_d : 2 * slice_d].reshape(-1)
    taps = small_all[:, 2 * slice_d :].reshape(fsdp_count, taps_count, 3, heads, -1)
    taps = taps.transpose(1, 2, 3, 0, 4).reshape(taps_count, 3 * width)
    packed = jnp.concatenate([w_up, w_down.T, w_out.T], axis=1)
    gathered = lax.all_gather(packed, ("tp", "fsdp"), axis=0, tiled=True)
    gathered = gathered.reshape(tp_count, model, packed.shape[1])
    up_blocks = gathered[:, :, :units]
    down_blocks = gathered[:, :, units : 2 * units]
    out_blocks = gathered[:, :, 2 * units :]

    away = lax.dynamic_index_in_dim(tokens, 1 - place, 0, keepdims=False)
    mine = lax.dynamic_index_in_dim(tokens, place, 0, keepdims=False)
    swap = [(i, 1 - i) for i in range(ctx_count)]
    came = lax.ppermute(away, "ctx", swap)
    row = jnp.where(place == 0, jnp.concatenate([mine, came]), jnp.concatenate([came, mine]))
    block_row = lax.dynamic_index_in_dim(block_ids, place, 0, keepdims=False)
    seq_row = lax.dynamic_index_in_dim(seq_ids, place, 0, keepdims=False)
    owner_row = jnp.repeat(seq_row, group_len)
    code = owner_row * 4096 + block_row
    hi = jnp.sum((code[None, :] <= code[:, None]).astype(jnp.int32), axis=1)[None, :]
    first_piece = jnp.sum((seq_row[None, :] < seq_row[:, None]).astype(jnp.int32), axis=1)
    lo_tile = jnp.repeat(first_piece * (group_len // TILE), group_len // QUERIES)

    row_values = row.astype(F32)
    _, base_row = norm_parts(row_values)
    normed = (base_row * gain_first).astype(BF16)
    linear = dot_tn(qkv_full, normed.T).astype(BF16)
    linear_f = linear.astype(F32)
    same = [
        jnp.concatenate([jnp.zeros((j,), F32), (owner_row[j:] == owner_row[: length - j]).astype(F32)])
        for j in range(taps_count)
    ]
    shifted = [linear_f] + [
        jnp.pad(linear_f[:, : length - j], ((0, 0), (j, 0))) * same[j] for j in range(1, taps_count)
    ]
    triple = sum(taps[j][:, None] * shifted[j] for j in range(taps_count)).astype(BF16)
    att, lse = attn_forward(lo_tile, hi, triple, heads)

    sent = att.reshape(width, ctx_count, tp_count, quarter).transpose(1, 2, 0, 3)
    got = spread(sent.reshape(ctx_count * tp_count, width, quarter), ctx_count, tp_count, 1)
    got = got.reshape(rows, tp_count, width, quarter)
    attended = got.transpose(0, 3, 1, 2).reshape(rows * quarter, tp_count * width)
    states = lax.dynamic_slice_in_dim(tokens, part * quarter, quarter, 1)
    states = states.reshape(rows * quarter, model).astype(F32)
    grad_out = lax.dynamic_slice_in_dim(cotangent, part * quarter, quarter, 1)
    grad_out = grad_out.reshape(rows * quarter, model)
    out_flat = out_blocks.transpose(1, 0, 2).reshape(model, tp_count * width)
    middle = states + dot_nt(attended, out_flat)
    inv_two, base_two = norm_parts(middle)
    normed_two = (base_two * gain_second).astype(BF16)
    upward = jnp.einsum("td,bdu->btu", normed_two, up_blocks, preferred_element_type=F32)
    lifted = jnp.maximum(upward, 0.0)
    hidden = (lifted * lifted).astype(BF16)
    ffn = jnp.einsum("btu,bdu->td", hidden, down_blocks, preferred_element_type=F32)
    block_out = (middle + ffn).astype(BF16).reshape(rows, quarter, model)
    block_out, lifted = lax.optimization_barrier((block_out, lifted))
    grad_hidden = jnp.einsum("td,bdu->btu", grad_out, down_blocks, preferred_element_type=F32)
    grad_upward = (grad_hidden * 2.0 * lifted).astype(BF16)
    grad_norm_two = jnp.einsum("btu,bdu->td", grad_upward, up_blocks, preferred_element_type=F32)
    back_two = norm_back(grad_norm_two, gain_second, inv_two, base_two)
    grad_middle = grad_out.astype(F32) + back_two
    grad_branch = grad_middle.astype(BF16)
    grad_attended = dot_nn(grad_branch, out_flat).astype(BF16)
    grad_packed = weight_grads(normed_two, grad_out, grad_branch, grad_upward, hidden, got, fsdp_count * ctx_count)

    sent = grad_attended.reshape(rows, quarter, tp_count, width).transpose(0, 2, 3, 1)
    sent, grad_packed = lax.optimization_barrier((sent, grad_packed))
    columns = grad_packed.shape[3]
    grad_packed = grad_packed.reshape(-1, columns)
    grad_packed = lax.psum_scatter(grad_packed, ("fsdp", "ctx"), scatter_dimension=0, tiled=True)
    grad_packed = grad_packed.reshape(tp_count, -1, columns)
    got = spread(sent.reshape(rows * tp_count, width, quarter), ctx_count, tp_count, 2)
    got, block_out = lax.optimization_barrier((got, block_out))
    chunks = [block_out]
    for k in range(1, tp_count):
        ring = [(i, (i + k) % tp_count) for i in range(tp_count)]
        chunks.append(lax.ppermute(block_out, "tp", ring))
    got = got.reshape(ctx_count, tp_count, width, quarter)
    grad_att = got.transpose(2, 0, 1, 3).reshape(width, length)
    later = jnp.stack([jnp.pad(same[j][j:], (0, j)) for j in range(taps_count)])
    grad_linear, grad_taps = attn_backward(lo_tile, hi, triple, grad_att, att, lse, linear, later, taps, heads)
    grad_taps = grad_taps[:, :taps_count].T
    grad_qkv = lax.dot_general(
        normed, grad_linear, (((0,), (1,)), ((), ())), preferred_element_type=F32
    )
    sent = lax.dot_general(
        grad_linear, qkv_full, (((0,), (1,)), ((), ())), preferred_element_type=F32
    ).astype(BF16).reshape(ctx_count, tp_count, quarter, model)
    sent, *chunks = lax.optimization_barrier((sent, *chunks))
    block_out = assemble(part, chunks)
    input_grad, grad_packed = tail(
        sent,
        states.astype(BF16).reshape(rows, quarter, model),
        grad_middle.reshape(rows, quarter, model),
        gain_first[None, :],
        grad_packed,
        3,
    )
    input_grad = input_grad.astype(F32)

    halves = fsdp_count * ctx_count
    f_taps = grad_taps.reshape(taps_count * 3 * heads, fsdp_count, -1).transpose(1, 0, 2).reshape(fsdp_count, -1)
    f_taps = jnp.pad(f_taps, ((0, 0), (0, 16 * 3 * width - f_taps.shape[1])))
    f_taps = jnp.repeat(f_taps.reshape(fsdp_count, 16, 3 * width), ctx_count, axis=0)
    half_d = slice_d // ctx_count
    grad_qkv = jnp.concatenate([grad_qkv.reshape(halves, half_d, 3 * width), f_taps], axis=1)
    grad_qkv = grad_qkv.astype(BF16).reshape(halves * (half_d + 16), 3 * width)
    grad_qkv = lax.psum_scatter(grad_qkv, ("fsdp", "ctx"), scatter_dimension=0, tiled=True)
    grad_taps = grad_qkv[half_d:].astype(F32).reshape(-1)[: kernel.size].reshape(kernel.shape)
    grad_qkv, gains = finish(
        grad_packed, grad_qkv, w_up, w_qkv.reshape(slice_d, 3 * width), ctx_count, tp_count, 4
    )
    grad_packed = grad_packed.reshape(slice_d, columns).astype(F32)
    grad_qkv = grad_qkv.reshape(slice_d, 3 * width).astype(F32)
    gains = gains[:, :2].T / jnp.stack([gain_one, gain_two]).astype(F32)
    return (
        block_out,
        input_grad,
        gains[0],
        grad_qkv.reshape(slice_d, 3, width),
        grad_taps,
        grad_packed[:, 2 * units :].T,
        gains[1],
        grad_packed[:, :units],
        grad_packed[:, units : 2 * units].T,
    )


MICRO = 2
SEQS_MB = 1


def passed_along(block, axis, distance):
    devices = range(lax.axis_size(axis))
    route = [(i - distance, i) for i in devices if i - distance in devices]
    return lax.ppermute(block, axis, route)


def any_norm_parts(values):
    inverse = lax.rsqrt(jnp.mean(values * values, axis=-1, keepdims=True) + 1e-06)
    return (inverse, values * inverse)


def any_norm_back(grad_norm, gain_full, inverse, scaled):
    grad_scaled = grad_norm * gain_full
    inner_mean = jnp.mean(grad_scaled * scaled, axis=-1, keepdims=True)
    return (inverse * (grad_scaled - scaled * inner_mean), jnp.sum(grad_norm * scaled, axis=(0, 1)))


def masked_scores(queries, key_heads, allowed, score_scale):
    scores = (
        jnp.einsum("sqhe,skhe->shqk", queries, key_heads, preferred_element_type=jnp.float32)
        * score_scale
    )
    return jnp.where(allowed[:, None], scores, -1e30)


def tensor_total(values):
    return lax.psum(values, "tp")


def any_on_device(
    tokens, gain_one, w_qkv, kernel, w_out, gain_two, w_up, w_down, block_ids, seq_ids, cotangent
):
    ctx_place = lax.axis_index("ctx")
    ctx_count = lax.axis_size("ctx")
    group_len = tokens.shape[1]
    taps_count = kernel.shape[0]
    margin = taps_count - 1
    local_heads = kernel.shape[2]
    score_scale = HD ** (-0.5)
    per_micro = SEQS_MB
    group_start = ctx_place * group_len
    owner_all = jnp.repeat(seq_ids, group_len, axis=1)
    totals = None
    outputs = []
    input_grads = []
    for micro_step in range(MICRO):
        gathered = (
            lax.all_gather(gain_one, "fsdp", axis=0, tiled=True),
            lax.all_gather(w_qkv, "fsdp", axis=0, tiled=True),
            lax.all_gather(kernel, "fsdp", axis=3, tiled=True),
            lax.all_gather(w_out, "fsdp", axis=1, tiled=True),
            lax.all_gather(gain_two, "fsdp", axis=0, tiled=True),
            lax.all_gather(w_up, "fsdp", axis=0, tiled=True),
            lax.all_gather(w_down, "fsdp", axis=1, tiled=True),
        )
        gain_first, qkv_full, conv_taps, out_full, gain_second, up_full, down_full = gathered
        gain_first = gain_first.astype(jnp.float32)
        gain_second = gain_second.astype(jnp.float32)
        tap_weights = conv_taps.astype(jnp.float32).reshape(taps_count, 3, -1)
        first_row = micro_step * per_micro
        states = tokens[first_row : first_row + per_micro].astype(jnp.float32)
        block_rows = block_ids[first_row : first_row + per_micro]
        owner_rows = owner_all[first_row : first_row + per_micro]
        group_ids = seq_ids[first_row : first_row + per_micro]
        own_group = lax.dynamic_slice_in_dim(group_ids, ctx_place, 1, 1)
        group_before = lax.dynamic_slice_in_dim(group_ids, jnp.maximum(ctx_place - 1, 0), 1, 1)
        group_after = lax.dynamic_slice_in_dim(
            group_ids, jnp.minimum(ctx_place + 1, ctx_count - 1), 1, 1
        )
        keep_before = (group_before == own_group).astype(jnp.float32)[:, :, None, None]
        keep_after = (group_after == own_group).astype(jnp.float32)[:, :, None, None]
        own_blocks = lax.dynamic_slice_in_dim(block_rows, group_start, group_len, 1)
        allowed = (block_rows[:, None, :] <= own_blocks[:, :, None]) & (
            owner_rows[:, None, :] == own_group[:, :, None]
        )
        inv_one, base_one = any_norm_parts(states)
        normed = (base_one * gain_first).astype(jnp.bfloat16)
        linear = jnp.einsum(
            "std,dce->stce", normed, qkv_full, preferred_element_type=jnp.float32
        ).astype(jnp.bfloat16)
        edge_rows = passed_along(linear[:, group_len - margin :], "ctx", 1)
        padded = jnp.concatenate(
            [edge_rows.astype(jnp.float32) * keep_before, linear.astype(jnp.float32)], axis=1
        )
        mixed_conv = sum(
            (
                tap_weights[offset] * padded[:, margin - offset : margin - offset + group_len]
                for offset in range(taps_count)
            )
        )
        triple = mixed_conv.astype(jnp.bfloat16)
        queries = triple[:, :, 0].reshape(per_micro, group_len, local_heads, HD)
        key_pair = lax.all_gather(triple[:, :, 1:], "ctx", axis=1, tiled=True)
        key_heads = key_pair[:, :, 0].reshape(per_micro, -1, local_heads, HD)
        value_heads = key_pair[:, :, 1].reshape(per_micro, -1, local_heads, HD)
        scores = masked_scores(queries, key_heads, allowed, score_scale)
        row_peak = jnp.max(scores, axis=-1, keepdims=True)
        log_total = row_peak + jnp.log(jnp.sum(jnp.exp(scores - row_peak), axis=-1, keepdims=True))
        probs_low = jnp.exp(scores - log_total).astype(jnp.bfloat16)
        attended = jnp.einsum(
            "shqk,skhe->sqhe", probs_low, value_heads, preferred_element_type=jnp.float32
        )
        attended = attended.astype(jnp.bfloat16).reshape(per_micro, group_len, -1)
        attn_part = jnp.einsum(
            "std,de->ste", attended, out_full, preferred_element_type=jnp.float32
        )
        grad_out = cotangent[first_row : first_row + per_micro]
        middle = states + tensor_total(attn_part)
        inv_two, base_two = any_norm_parts(middle)
        normed_two = (base_two * gain_second).astype(jnp.bfloat16)
        upward = jnp.einsum("std,df->stf", normed_two, up_full, preferred_element_type=jnp.float32)
        lifted = jnp.maximum(upward, 0.0)
        hidden = (lifted * lifted).astype(jnp.bfloat16)
        ffn_part = jnp.einsum("stf,fd->std", hidden, down_full, preferred_element_type=jnp.float32)
        outputs.append((middle + tensor_total(ffn_part)).astype(jnp.bfloat16))
        grad_down = jnp.einsum("stf,std->fd", hidden, grad_out, preferred_element_type=jnp.float32)
        grad_hidden = jnp.einsum(
            "std,fd->stf", grad_out, down_full, preferred_element_type=jnp.float32
        )
        grad_upward = (grad_hidden * 2.0 * lifted).astype(jnp.bfloat16)
        grad_up = jnp.einsum(
            "std,stf->df", normed_two, grad_upward, preferred_element_type=jnp.float32
        )
        norm_two_part = jnp.einsum(
            "stf,df->std", grad_upward, up_full, preferred_element_type=jnp.float32
        )
        back_two, grad_gain_two = any_norm_back(
            tensor_total(norm_two_part), gain_second, inv_two, base_two
        )
        grad_middle = grad_out.astype(jnp.float32) + back_two
        grad_branch = grad_middle.astype(jnp.bfloat16)
        grad_out_proj = jnp.einsum(
            "std,ste->de", attended, grad_branch, preferred_element_type=jnp.float32
        )
        grad_attended = jnp.einsum(
            "ste,de->std", grad_branch, out_full, preferred_element_type=jnp.float32
        )
        grad_attended = grad_attended.astype(jnp.bfloat16).reshape(
            per_micro, group_len, local_heads, HD
        )
        prob_full = jnp.exp(masked_scores(queries, key_heads, allowed, score_scale) - log_total)
        grad_probs = jnp.einsum(
            "sqhe,skhe->shqk", grad_attended, value_heads, preferred_element_type=jnp.float32
        )
        row_total = jnp.sum(prob_full * grad_probs, axis=-1, keepdims=True)
        grad_scores = (prob_full * (grad_probs - row_total)).astype(jnp.bfloat16)
        grad_queries = (
            jnp.einsum(
                "shqk,skhe->sqhe", grad_scores, key_heads, preferred_element_type=jnp.float32
            )
            * score_scale
        )
        keys_term = (
            jnp.einsum("shqk,sqhe->skhe", grad_scores, queries, preferred_element_type=jnp.float32)
            * score_scale
        )
        values_term = jnp.einsum(
            "shqk,sqhe->skhe",
            prob_full.astype(jnp.bfloat16),
            grad_attended,
            preferred_element_type=jnp.float32,
        )
        pair_grads = lax.psum_scatter(
            jnp.stack([keys_term, values_term], axis=2).astype(jnp.bfloat16),
            "ctx",
            scatter_dimension=1,
            tiled=True,
        ).astype(jnp.float32)
        grad_keys = pair_grads[:, :, 0]
        grad_values = pair_grads[:, :, 1]
        grad_triple = jnp.stack([grad_queries, grad_keys, grad_values], axis=2).reshape(
            per_micro, group_len, 3, -1
        )
        tail_rows = passed_along(grad_triple[:, :margin], "ctx", -1)
        padded_grad = jnp.concatenate([grad_triple, tail_rows * keep_after], axis=1)
        grad_linear = sum(
            (
                tap_weights[offset] * padded_grad[:, offset : offset + group_len]
                for offset in range(taps_count)
            )
        )
        grad_linear = grad_linear.astype(jnp.bfloat16)
        grad_taps = jnp.stack(
            [
                jnp.sum(
                    grad_triple * padded[:, margin - offset : margin - offset + group_len],
                    axis=(0, 1),
                )
                for offset in range(taps_count)
            ]
        )
        grad_taps = grad_taps.reshape(conv_taps.shape)
        grad_qkv = jnp.einsum(
            "std,stce->dce", normed, grad_linear, preferred_element_type=jnp.float32
        )
        grad_norm_one = tensor_total(
            jnp.einsum("stce,dce->std", grad_linear, qkv_full, preferred_element_type=jnp.float32)
        )
        back_one, grad_gain_one = any_norm_back(grad_norm_one, gain_first, inv_one, base_one)
        input_grads.append(grad_middle + back_one)
        micro_grads = (
            grad_gain_one,
            grad_qkv,
            grad_taps,
            grad_out_proj,
            grad_gain_two,
            grad_up,
            grad_down,
        )
        totals = (
            micro_grads
            if totals is None
            else tuple(
                (left_part + right_part for left_part, right_part in zip(totals, micro_grads))
            )
        )
    summed = (
        lax.psum_scatter(totals[0], ("fsdp", "ctx"), scatter_dimension=0, tiled=True),
        lax.psum_scatter(totals[1], ("fsdp", "ctx"), scatter_dimension=0, tiled=True),
        lax.psum_scatter(totals[2], ("fsdp", "ctx"), scatter_dimension=3, tiled=True),
        lax.psum_scatter(totals[3], ("fsdp", "ctx"), scatter_dimension=1, tiled=True),
        lax.psum_scatter(totals[4], ("fsdp", "ctx"), scatter_dimension=0, tiled=True),
        lax.psum_scatter(totals[5], ("fsdp", "ctx"), scatter_dimension=0, tiled=True),
        lax.psum_scatter(totals[6], ("fsdp", "ctx"), scatter_dimension=1, tiled=True),
    )
    shares = (
        lax.all_gather(summed[0].astype(jnp.bfloat16), "ctx", axis=0, tiled=True).astype(
            jnp.float32
        ),
        lax.all_gather(summed[1].astype(jnp.bfloat16), "ctx", axis=0, tiled=True).astype(
            jnp.float32
        ),
        lax.all_gather(summed[2].astype(jnp.bfloat16), "ctx", axis=3, tiled=True).astype(
            jnp.float32
        ),
        lax.all_gather(summed[3].astype(jnp.bfloat16), "ctx", axis=1, tiled=True).astype(
            jnp.float32
        ),
        lax.all_gather(summed[4].astype(jnp.bfloat16), "ctx", axis=0, tiled=True).astype(
            jnp.float32
        ),
        lax.all_gather(summed[5].astype(jnp.bfloat16), "ctx", axis=0, tiled=True).astype(
            jnp.float32
        ),
        lax.all_gather(summed[6].astype(jnp.bfloat16), "ctx", axis=1, tiled=True).astype(
            jnp.float32
        ),
    )
    return (jnp.concatenate(outputs, axis=0), jnp.concatenate(input_grads, axis=0)) + tuple(shares)


def solution(mesh):
    placed = (
        P("fsdp", "ctx", None),
        P("fsdp"),
        P("fsdp", None, "tp"),
        P(None, None, "tp", "fsdp"),
        P("tp", "fsdp"),
        P("fsdp"),
        P("fsdp", "tp"),
        P("tp", "fsdp"),
        P("fsdp", None),
        P("fsdp", None),
        P("fsdp", "ctx", None),
    )

    def on_device(*args):
        if args[0].shape[0] == lax.axis_size("ctx") == 2:
            return row_on_device(*args)
        return any_on_device(*args)

    return jax.shard_map(
        on_device,
        mesh=mesh,
        in_specs=placed,
        out_specs=(
            P("fsdp", "ctx", None),
            P("fsdp", "ctx", None),
            P("fsdp"),
            P("fsdp", None, "tp"),
            P(None, None, "tp", "fsdp"),
            P("tp", "fsdp"),
            P("fsdp"),
            P("fsdp", "tp"),
            P("tp", "fsdp"),
        ),
        check_vma=False,
    )
```

```python
import functools

import jax
import jax.numpy as jnp
from jax import lax
from jax.experimental import pallas as pl
from jax.experimental.pallas import tpu as pltpu
from jax.sharding import PartitionSpec as P


HD = 64
TILE = 256
QUERIES = 512
NEG = -1e30
FSDP, CTX, TP = "fsdp", "ctx", "tp"
GO_LEFT, GO_RIGHT, NORM, PAIR, PART_LEFT, PART_RIGHT, PART_TOTAL, SUM_LEFT, SUM_RIGHT, TOTAL = range(10)
LEFT, RIGHT = range(2)
MESH = pl.DeviceIdType.MESH
F32 = jnp.float32
BF16 = jnp.bfloat16


def norm_parts(values):
    inverse = lax.rsqrt(jnp.mean(values * values, axis=-1, keepdims=True) + 1e-06)
    return (inverse, values * inverse)


def norm_back(grad_norm, gain_full, inverse, scaled):
    grad_scaled = grad_norm * gain_full
    inner_mean = jnp.mean(grad_scaled * scaled, axis=-1, keepdims=True)
    return inverse * (grad_scaled - scaled * inner_mean)


def dot_nn(a, b):
    return lax.dot_general(a, b, (((1,), (0,)), ((), ())), preferred_element_type=F32)


def dot_nt(a, b):
    return lax.dot_general(a, b, (((1,), (1,)), ((), ())), preferred_element_type=F32)


def three_terms(value):
    one = value.astype(BF16).astype(F32)
    two = (value - one).astype(BF16).astype(F32)
    three = value - one - two
    place = lax.broadcasted_iota(jnp.int32, (16, value.shape[1]), 0)
    rest = jnp.where(place == 1, -two, jnp.where(place == 2, -three, 0.0))
    return jnp.where(place == 0, -one, rest).astype(BF16)


def put_keys(keys, key_scr, h):
    key_scr[h, :, :HD] = keys.T
    key_scr[h, :, HD:] = jnp.ones((key_scr.shape[1], 16), BF16)


def over_keys(i, tiles, first, step):
    ratio = QUERIES // TILE

    def edge(j, carry):
        step(j, True)
        return carry

    def lower(j, carry):
        step(j * ratio, False)
        return carry

    lax.fori_loop(i * ratio, jnp.minimum((i + 1) * ratio + 1, tiles * ratio), edge, 0)
    lax.fori_loop(first // ratio, i, lower, 0)


def attn_fwd_kernel(heads, lo_ref, hi_ref, qkv_ref, out_ref, lse_ref, key_scr, val_scr, query_scr, peak, acc):
    i = pl.program_id(0)
    tiles = pl.num_programs(0)
    width = heads * HD
    ratio = QUERIES // TILE

    @pl.when(i == 0)
    def _():
        def prepare(h, carry):
            put_keys(qkv_ref[pl.ds(pl.multiple_of(width + h * HD, HD), HD), :], key_scr, h)
            val_scr[h, :HD, :] = qkv_ref[pl.ds(pl.multiple_of(2 * width + h * HD, HD), HD), :]
            val_scr[h, HD:, :] = jnp.ones((16, val_scr.shape[2]), BF16)
            return carry

        lax.fori_loop(0, heads, prepare, 0)

    here = pl.ds(pl.multiple_of(i * QUERIES, QUERIES), QUERIES)
    hi = hi_ref[:, here]
    for h in range(heads):
        query = qkv_ref[h * HD : (h + 1) * HD, here].astype(F32) * (HD ** (-0.5))
        keys = qkv_ref[width + h * HD : width + (h + 1) * HD, here].astype(F32)
        shift = jnp.sum(query * keys, axis=0, keepdims=True)
        query_scr[h, :HD, :] = query.astype(BF16)
        query_scr[h, HD:, :] = three_terms(shift)
        lse_ref[h : h + 1, :] = shift
    peak[...] = jnp.full_like(peak, NEG)
    acc[...] = jnp.zeros_like(acc)

    def scores_of(j, h, masked):
        there = pl.ds(pl.multiple_of(j * TILE, TILE), TILE if masked else QUERIES)
        scores = dot_nn(key_scr[h, there, :], query_scr[h])
        if masked:
            place = lax.broadcasted_iota(jnp.int32, (TILE, QUERIES), 0) + j * TILE
            scores = jnp.where(place < hi, scores, NEG)
        return scores

    def gather(j, masked):
        there = pl.ds(pl.multiple_of(j * TILE, TILE), TILE if masked else QUERIES)
        for h in range(heads):
            scores = scores_of(j, h, masked)
            peak[...] = jnp.maximum(peak[...], jnp.max(scores.reshape(-1, 8, QUERIES), axis=0))
            acc[h] += dot_nn(val_scr[h, :, there], jnp.exp(scores).astype(BF16))

    over_keys(i, tiles, lo_ref[i], gather)

    @pl.when(jnp.max(peak[...]) > 60.0)
    def _():
        def one_head(h, carry):
            stop = jnp.minimum((i + 1) * ratio + 1, tiles * ratio)

            def highest(j, top):
                return jnp.maximum(top, jnp.max(scores_of(j, h, True), axis=0, keepdims=True))

            query_scr[h, HD:, :] = jnp.zeros((16, QUERIES), BF16)
            top = lax.fori_loop(lo_ref[i], stop, highest, jnp.full((1, QUERIES), NEG, F32))
            query_scr[h, HD:, :] = three_terms(top)
            lse_ref[pl.ds(h, 1), :] = top

            def again(j, total):
                there = pl.ds(pl.multiple_of(j * TILE, TILE), TILE)
                return total + dot_nn(val_scr[h, :, there], jnp.exp(scores_of(j, h, True)).astype(BF16))

            acc[h] = lax.fori_loop(lo_ref[i], stop, again, jnp.zeros((HD + 16, QUERIES), F32))
            return carry

        lax.fori_loop(0, heads, one_head, 0)

    for h in range(heads):
        total = acc[h, HD : HD + 1, :]
        attended = (acc[h, :HD, :] / total).astype(BF16)
        for e in range(ratio):
            out_ref[e, h * HD : (h + 1) * HD, :] = attended[:, e * TILE : (e + 1) * TILE]
        lse_ref[h : h + 1, :] = lse_ref[h : h + 1, :] + jnp.log(total)


def attn_forward(lo_tile, hi, qkv, heads):
    length = qkv.shape[1]
    tiles = length // QUERIES
    width = heads * HD
    whole = lambda i, *_: (0, 0)
    return pl.pallas_call(
        functools.partial(attn_fwd_kernel, heads),
        out_shape=(
            jax.ShapeDtypeStruct((length // TILE, width, TILE), BF16),
            jax.ShapeDtypeStruct((8, length), F32),
        ),
        grid_spec=pltpu.PrefetchScalarGridSpec(
            num_scalar_prefetch=1,
            grid=(tiles,),
            in_specs=[
                pl.BlockSpec((1, length), whole),
                pl.BlockSpec((3 * width, length), whole),
            ],
            out_specs=(
                pl.BlockSpec((QUERIES // TILE, width, TILE), lambda i, *_: (i, 0, 0)),
                pl.BlockSpec((8, QUERIES), lambda i, *_: (0, i)),
            ),
            scratch_shapes=[
                pltpu.VMEM((heads, length, HD + 16), BF16),
                pltpu.VMEM((heads, HD + 16, length), BF16),
                pltpu.VMEM((heads, HD + 16, QUERIES), BF16),
                pltpu.VMEM((8, QUERIES), F32),
                pltpu.VMEM((heads, HD + 16, QUERIES), F32),
            ],
        ),
        name="attn_fwd",
    )(lo_tile, hi, qkv)


def attn_bwd_kernel(heads, taps_count, lo_ref, hi_ref, qkv_ref, grad_ref, att_ref, lse_ref, lin_ref, later_ref, taps_ref, out_ref, tap_ref, key_scr, val_scr, query_scr, grad_scr, triple):
    i = pl.program_id(0)
    tiles = pl.num_programs(0)
    width = heads * HD
    here = pl.ds(pl.multiple_of(i * QUERIES, QUERIES), QUERIES)
    scale = HD ** (-0.5)

    @pl.when(i == 0)
    def _():
        def prepare(h, carry):
            put_keys(qkv_ref[pl.ds(pl.multiple_of(width + h * HD, HD), HD), :], key_scr, h)
            put_keys(qkv_ref[pl.ds(pl.multiple_of(2 * width + h * HD, HD), HD), :], val_scr, h)
            return carry

        lax.fori_loop(0, heads, prepare, 0)
        triple[...] = jnp.zeros_like(triple)

    hi = hi_ref[:, here]
    ratio = QUERIES // TILE

    def tokens_of(ref, rows):
        return jnp.concatenate([ref[i * ratio + e, rows, :] for e in range(ratio)], axis=1)

    for h in range(heads):
        rows = slice(h * HD, (h + 1) * HD)
        query_scr[h, :HD, :] = (qkv_ref[rows, here].astype(F32) * scale).astype(BF16)
        query_scr[h, HD:, :] = three_terms(lse_ref[h : h + 1, here])
        grad = tokens_of(grad_ref, rows)
        grad_scr[h, :HD, :] = grad
        row_total = jnp.sum(grad.astype(F32) * tokens_of(att_ref, rows).astype(F32), axis=0, keepdims=True)
        grad_scr[h, HD:, :] = three_terms(row_total)

    def step(j, masked):
        there = pl.ds(pl.multiple_of(j * TILE, TILE), TILE if masked else QUERIES)
        for h in range(heads):
            q_rows = slice(h * HD, (h + 1) * HD)
            k_rows = slice(width + h * HD, width + (h + 1) * HD)
            v_rows = slice(2 * width + h * HD, 2 * width + (h + 1) * HD)
            scores = dot_nn(key_scr[h, there, :], query_scr[h])
            if masked:
                place = lax.broadcasted_iota(jnp.int32, (TILE, QUERIES), 0) + j * TILE
                scores = jnp.where(place < hi, scores, NEG)
            probs = jnp.exp(scores)
            shifted = dot_nn(val_scr[h, there, :], grad_scr[h])
            grad_scores = (probs * shifted).astype(BF16)
            triple[v_rows, there] += dot_nt(grad_scr[h, :HD, :], probs.astype(BF16))
            triple[k_rows, there] += dot_nt(qkv_ref[q_rows, here], grad_scores)
            triple[q_rows, here] += dot_nn(qkv_ref[k_rows, there], grad_scores)

    over_keys(i, tiles, lo_ref[i], step)

    @pl.when(i == tiles - 1)
    def _():
        def channels(block, carry):
            rows = pl.ds(pl.multiple_of(block * HD, HD), HD)
            unit = jnp.where(block < 2 * heads, scale, 1.0)
            weights = [taps_ref[rows, j : j + 1] for j in range(taps_count)]

            def tile(n, sums):
                start = pl.multiple_of(n * QUERIES, QUERIES)
                spot = pl.ds(start, QUERIES)
                wide = triple[rows, pl.ds(start, QUERIES + 128)] * unit
                lin = lin_ref[rows, spot].astype(F32)
                total = None
                result = []
                for j in range(taps_count):
                    if j == 0:
                        moved = wide[:, :QUERIES]
                    else:
                        moved = pltpu.roll(wide, QUERIES + 128 - j, 1)[:, :QUERIES] * later_ref[j : j + 1, spot]
                    total = weights[j] * moved if total is None else total + weights[j] * moved
                    product = moved * lin
                    result.append(sums[j] + sum(product[:, m : m + 128] for m in range(0, QUERIES, 128)))
                out_ref[rows, spot] = total.astype(BF16)
                return tuple(result)

            zero = jnp.zeros((HD, 128), F32)
            sums = lax.fori_loop(0, out_ref.shape[1] // QUERIES, tile, (zero,) * taps_count)
            for j in range(taps_count):
                tap_ref[rows, j : j + 1] = jnp.sum(sums[j], axis=1, keepdims=True)
            return carry

        lax.fori_loop(0, 3 * heads, channels, 0)


def attn_backward(lo_tile, hi, qkv, grad, att, lse, linear, later, taps, heads):
    length = qkv.shape[1]
    tiles = length // QUERIES
    width = heads * HD
    taps_count = taps.shape[0]
    later = jnp.pad(later, ((0, 8 - taps_count), (0, 0)))
    columns = jnp.pad(taps.T, ((0, 0), (0, 128 - taps_count)))
    whole = lambda i, *_: (0, 0)
    return pl.pallas_call(
        functools.partial(attn_bwd_kernel, heads, taps_count),
        out_shape=(
            jax.ShapeDtypeStruct((3 * width, length), BF16),
            jax.ShapeDtypeStruct((3 * width, 128), F32),
        ),
        grid_spec=pltpu.PrefetchScalarGridSpec(
            num_scalar_prefetch=1,
            grid=(tiles,),
            in_specs=[
                pl.BlockSpec((1, length), whole),
                pl.BlockSpec((3 * width, length), whole),
                pl.BlockSpec((length // TILE, width, TILE), lambda i, *_: (0, 0, 0)),
                pl.BlockSpec((length // TILE, width, TILE), lambda i, *_: (0, 0, 0)),
                pl.BlockSpec((8, length), whole),
                pl.BlockSpec((3 * width, length), whole),
                pl.BlockSpec((8, length), whole),
                pl.BlockSpec((3 * width, 128), whole),
            ],
            out_specs=(
                pl.BlockSpec((3 * width, length), whole),
                pl.BlockSpec((3 * width, 128), whole),
            ),
            scratch_shapes=[
                pltpu.VMEM((heads, length, HD + 16), BF16),
                pltpu.VMEM((heads, length, HD + 16), BF16),
                pltpu.VMEM((heads, HD + 16, QUERIES), BF16),
                pltpu.VMEM((heads, HD + 16, QUERIES), BF16),
                pltpu.VMEM((3 * width, length + 128), F32),
            ],
        ),
        name="attn_bwd",
    )(lo_tile, hi, qkv, grad, att, lse, linear, later, columns)


def project_kernel(heads, taps_count, place_ref, mine_ref, came_ref, weight_ref, gain_ref, taps_ref, same_ref, triple_ref, linear_ref, normed_ref, weight_t, before):
    i = pl.program_id(0)

    @pl.when(i == 0)
    def _():
        weight_t[...] = weight_ref[...].T
        before[...] = jnp.zeros_like(before)

    here = i // (pl.num_programs(0) // 2) == place_ref[0]
    values = jnp.where(here, mine_ref[0].astype(F32), came_ref[...].astype(F32))
    inverse = lax.rsqrt(jnp.mean(values * values, axis=-1, keepdims=True) + 1e-06)
    normed = (values * inverse * gain_ref[...]).astype(BF16)
    normed_ref[...] = normed
    linear_ref[...] = dot_nt(weight_t[...], normed).astype(BF16)

    def block(b, carry):
        rows = pl.ds(pl.multiple_of(b * HD, HD), HD)
        linear = linear_ref[rows, :].astype(F32)
        wide = jnp.concatenate([before[rows, :], linear], axis=1)
        total = taps_ref[rows, 0:1] * linear
        for j in range(1, taps_count):
            moved = pltpu.roll(wide, j, 1)[:, 128:] * same_ref[j : j + 1, :]
            total = total + taps_ref[rows, j : j + 1] * moved
        triple_ref[rows, :] = total.astype(BF16)
        before[rows, :] = linear[:, QUERIES - 128 :]
        return carry

    lax.fori_loop(0, 3 * heads, block, 0)


def project(place, tokens, came, weight, gain, taps, same, heads):
    taps_count, channels = taps.shape
    half, model = came.shape
    length = 2 * half
    steps = length // QUERIES
    near = half // QUERIES
    columns = jnp.pad(taps.T, ((0, 0), (0, 128 - taps_count)))
    same = jnp.pad(same, ((0, 8 - taps_count), (0, 0)))
    fixed = lambda i, _: (0, 0)
    return pl.pallas_call(
        functools.partial(project_kernel, heads, taps_count),
        out_shape=(
            jax.ShapeDtypeStruct((channels, length), BF16),
            jax.ShapeDtypeStruct((channels, length), BF16),
            jax.ShapeDtypeStruct((length, model), BF16),
        ),
        grid_spec=pltpu.PrefetchScalarGridSpec(
            num_scalar_prefetch=1,
            grid=(steps,),
            in_specs=[
                pl.BlockSpec((1, QUERIES, model), lambda i, p: (p[0], jnp.clip(i - near * p[0], 0, near - 1), 0)),
                pl.BlockSpec((QUERIES, model), lambda i, p: (jnp.clip(i - near * (1 - p[0]), 0, near - 1), 0)),
                pl.BlockSpec((model, channels), fixed),
                pl.BlockSpec((1, model), fixed),
                pl.BlockSpec((channels, 128), fixed),
                pl.BlockSpec((8, QUERIES), lambda i, _: (0, i)),
            ],
            out_specs=(
                pl.BlockSpec((channels, QUERIES), lambda i, _: (0, i)),
                pl.BlockSpec((channels, QUERIES), lambda i, _: (0, i)),
                pl.BlockSpec((QUERIES, model), lambda i, _: (i, 0)),
            ),
            scratch_shapes=[
                pltpu.VMEM((channels, model), BF16),
                pltpu.VMEM((channels, 128), F32),
            ],
        ),
        name="project",
    )(place.reshape(1), tokens, came, weight, gain, columns, same)


def spread_kernel(ctx_count, tp_count, x_ref, o_ref, send_sem, recv_sem, own_sem):
    peers = ctx_count * tp_count
    me = lax.axis_index(CTX) * tp_count + lax.axis_index(TP)

    def place(k):
        other = lax.rem(me + k, peers)
        return other, {CTX: other // tp_count, TP: lax.rem(other, tp_count)}

    barrier = pltpu.get_barrier_semaphore()
    for k in range(1, peers):
        pl.semaphore_signal(barrier, inc=1, device_id=place(k)[1], device_id_type=MESH)
    pl.semaphore_wait(barrier, peers - 1)
    copies = []
    for k in range(1, peers):
        other, device = place(k)
        copies.append(
            pltpu.make_async_remote_copy(
                src_ref=x_ref.at[other],
                dst_ref=o_ref.at[me],
                send_sem=send_sem.at[k - 1],
                recv_sem=recv_sem.at[k - 1],
                device_id=device,
                device_id_type=MESH,
            )
        )
        copies[-1].start()
    own = pltpu.make_async_copy(x_ref.at[me], o_ref.at[me], own_sem)
    own.start()
    own.wait()
    for copy in copies:
        copy.wait()


def spread(x, ctx_count, tp_count, ident):
    peers = ctx_count * tp_count
    return pl.pallas_call(
        functools.partial(spread_kernel, ctx_count, tp_count),
        out_shape=jax.ShapeDtypeStruct(x.shape, x.dtype),
        in_specs=[pl.BlockSpec(memory_space=pltpu.VMEM)],
        out_specs=pl.BlockSpec(memory_space=pltpu.VMEM),
        scratch_shapes=[
            pltpu.SemaphoreType.DMA((peers - 1,)),
            pltpu.SemaphoreType.DMA((peers - 1,)),
            pltpu.SemaphoreType.DMA,
        ],
        compiler_params=pltpu.CompilerParams(collective_id=ident, has_side_effects=True),
    )(x)


def signal_all(devices):
    barrier = pltpu.get_barrier_semaphore()
    for device in devices:
        pl.semaphore_signal(barrier, inc=1, device_id=device, device_id_type=MESH)
    pl.semaphore_wait(barrier, len(devices))


def remote(source, target, sems, index, device):
    return pltpu.make_async_remote_copy(
        src_ref=source,
        dst_ref=target,
        send_sem=sems.at[(0,) + index],
        recv_sem=sems.at[(1,) + index],
        device_id=device,
        device_id_type=MESH,
    )


def add_up(target, *sources):
    def block(n, carry):
        rows = pl.ds(pl.multiple_of(n * 32, 32), 32)
        total = sources[0][rows, :].astype(F32)
        for source in sources[1:]:
            total = total + source[rows, :].astype(F32)
        target[rows, :] = total.astype(target.dtype)
        return carry

    lax.fori_loop(0, target.shape[0] // 32, block, 0)


def line_order(count, pieces):
    hop, latency, add_cost, norm_cost, other = 16.4 / pieces, 1.5, 2.0 / pieces, 6.0 / pieces, 6.9
    crossing = pieces // 2
    arrived, link_free, clock = {}, {}, [0.0] * count
    order = [[] for _ in range(count)]
    finished = [set() for _ in range(count)]
    waiting = []
    for z in range(count):
        steps = [(PART_TOTAL, 0)]
        steps += [(PART_RIGHT, 0, c) for c in range(z + 1, count)] + [(PART_LEFT, 0, c) for c in range(z)]
        for n in range(pieces):
            steps += [(TOTAL, n), (NORM, n)]
            steps += [(SUM_RIGHT, n, c) for c in range(z + 1, count)] + [(SUM_LEFT, n, c) for c in range(z)]
            steps += [(GO_RIGHT, n, c) for c in range(z)] + [(GO_LEFT, n, c) for c in range(z + 1, count)]
        waiting.append(steps)
    rank = {GO_RIGHT: 0, GO_LEFT: 0, SUM_RIGHT: 1, SUM_LEFT: 1, NORM: 2, TOTAL: 3}
    rank |= {PART_RIGHT: 4, PART_LEFT: 4, PART_TOTAL: 5}

    def send(z, link, start, time, key):
        end = max(start, link_free.get((z, link), 0.0)) + time
        link_free[z, link] = end
        arrived[key] = end + latency

    def ready(z, step):
        kind = step[0]
        if kind == SUM_RIGHT and z == 0 or kind == SUM_LEFT and z == count - 1:
            return 0.0
        if kind == PART_RIGHT and z == 0 or kind == PART_LEFT and z == count - 1:
            return 0.0 if (NORM, 1) in finished[z] else None
        if kind in (SUM_RIGHT, SUM_LEFT, GO_RIGHT, GO_LEFT, PART_RIGHT, PART_LEFT):
            return arrived.get((z,) + step)
        if kind == PART_TOTAL:
            needs = [(z, PART_RIGHT, 0, z)] * (z > 0) + [(z, PART_LEFT, 0, z)] * (z < count - 1)
        elif kind == TOTAL:
            needs = [(z, SUM_RIGHT, step[1], z)] * (z > 0) + [(z, SUM_LEFT, step[1], z)] * (z < count - 1)
        elif kind == NORM and step[1] < crossing:
            needs = [(z, PAIR, step[1])]
        else:
            return 0.0 if (TOTAL, step[1]) in finished[z] else None
        return max(arrived[key] for key in needs) if all(key in arrived for key in needs) else None

    def run(z, step, time):
        kind = step[0]
        if kind == SUM_RIGHT:
            time += add_cost * (z > 0)
            send(z, RIGHT, time, hop, (z + 1,) + step)
        elif kind == SUM_LEFT:
            time += add_cost * (z < count - 1)
            send(z, LEFT, time, hop, (z - 1,) + step)
        elif kind == TOTAL:
            time += add_cost
            if step[1] < crossing:
                send(z, PAIR, time, hop, (z, PAIR, step[1]))
        elif kind == NORM:
            time += norm_cost
            if z < count - 1:
                send(z, RIGHT, time, hop, (z + 1, GO_RIGHT, step[1], z))
            if z > 0:
                send(z, LEFT, time, hop, (z - 1, GO_LEFT, step[1], z))
        elif kind == GO_RIGHT and z < count - 1:
            send(z, RIGHT, time, hop, (z + 1,) + step)
        elif kind == GO_LEFT and z > 0:
            send(z, LEFT, time, hop, (z - 1,) + step)
        elif kind == PART_RIGHT:
            time += 0.8 * (z > 0)
            send(z, RIGHT, time, other, (z + 1,) + step)
        elif kind == PART_LEFT:
            time += 0.8 * (z < count - 1)
            send(z, LEFT, time, other, (z - 1,) + step)
        elif kind == PART_TOTAL:
            time += 2.0
        return time + 0.15

    while any(waiting):
        options = []
        for z in range(count):
            for step in waiting[z]:
                at = ready(z, step)
                if at is not None:
                    distance = -abs(step[2] - z) if len(step) > 2 else 0
                    options.append((max(at, clock[z]), rank[step[0]], step[1], distance, z, step))
        start, *_, z, step = min(options)
        clock[z] = run(z, step, start)
        finished[z].add(step)
        waiting[z].remove(step)
        order[z].append(step)
    return order


def tail_kernel(
    tp_count, fsdp_count, p_ref, x_ref, middle_ref, gain_ref, g_ref, lin_ref, rows_ref, taps_ref, up_ref, qkv_ref,
    o_ref, up_out, down_out, out_out, qkv_out, tap_out, gain_out,
    from_left, from_right, mine, norm, result, part_from_left, part_from_right, s_ref, r_ref, rows_scr, q_ref, q_came, gains,
    right_sum, left_sum, right_sem, left_sem, pair_sem, part_right, part_left, own_sem, q_sem, edge_sem, gain_sem, rows_sem,
):
    me = lax.axis_index(TP)
    row = lax.axis_index(CTX)
    shard = lax.axis_index(FSDP)
    last = tp_count - 1
    ctx_count = p_ref.shape[0]
    pieces = from_left.shape[0]
    crossing = pieces // 2
    size = x_ref.shape[1]
    sub = size // crossing
    group = ctx_count * fsdp_count
    spot = shard * ctx_count + row
    friends = [lax.rem(spot + k, group) for k in range(1, group)]
    friend_at = [{FSDP: f // ctx_count, CTX: lax.rem(f, ctx_count)} for f in friends]
    mates = [(lax.rem(row + c, ctx_count), lax.rem(me + k, tp_count)) for c in range(ctx_count) for k in range(tp_count)][1:]
    mate_at = [{CTX: c, TP: k} for c, k in mates]
    signal_all(mate_at + [d for d in friend_at])

    def rows_of(n):
        return (1 - row if n < crossing else row), pl.ds((n % crossing) * sub, sub)

    def norm_backward(r, start):
        def block(k, carry):
            rows = pl.ds(pl.multiple_of(start + k * 32, 32), 32)
            values = x_ref[r, rows, :].astype(F32)
            inverse = lax.rsqrt(jnp.mean(values * values, axis=-1, keepdims=True) + 1e-06)
            base = values * inverse
            grad = norm[r, rows, :].astype(F32) * gain_ref[...]
            inner = jnp.mean(grad * base, axis=-1, keepdims=True)
            result[r, rows, :] = (middle_ref[r, rows, :] + inverse * (grad - base * inner)).astype(BF16)
            return carry

        lax.fori_loop(0, sub // 32, block, 0)

    def part_of(n, c):
        r, rows = rows_of(n)
        return p_ref.at[r, c, rows, :]

    def chunk(n, k):
        r, _ = rows_of(n)
        return o_ref.at[r, pl.ds(k * size + (n % crossing) * sub, sub), :]

    def result_of(n):
        r, rows = rows_of(n)
        return result.at[r, rows, :]

    def pair(n):
        _, rows = rows_of(n)
        return remote(mine.at[n], norm.at[row, rows, :], pair_sem, (n,), {CTX: 1 - row})

    q_parts = [remote(q_ref.at[f], q_came.at[k], q_sem, (k,), friend_at[k]) for k, f in enumerate(friends)]
    third, _, half, width = r_ref.shape
    units = up_ref.shape[1]
    edge_g = remote(s_ref.at[row], s_ref.at[row], edge_sem, (0,), {CTX: 1 - row})
    edge_q = remote(r_ref.at[:, row], r_ref.at[:, row], edge_sem, (1,), {CTX: 1 - row})
    rows_copy = pltpu.make_async_copy(rows_ref, rows_scr, rows_sem)
    rows_copy.start()
    shares = [remote(gains.at[row, me], gains.at[row, me], gain_sem, (k,), device) for k, device in enumerate(mate_at)]

    def own(n, z):
        return pltpu.make_async_copy(result_of(n), chunk(n, z), own_sem.at[n])

    def step_of(z, kind, n=0, c=0):
        right, left = {TP: min(z + 1, last)}, {TP: max(z - 1, 0)}
        if kind in (SUM_RIGHT, SUM_LEFT):
            rightwards = kind == SUM_RIGHT
            buffer, sems, target = (from_left, right_sum, right) if rightwards else (from_right, left_sum, left)
            if z == (0 if rightwards else last):
                remote(part_of(n, c), buffer.at[n, c], sems, (n, c), target).start()
            else:
                copy = remote(buffer.at[n, c], buffer.at[n, c], sems, (n, c), target)
                copy.wait_recv()
                add_up(buffer.at[n, c], buffer.at[n, c], part_of(n, c))
                copy.start()
        elif kind == TOTAL:
            r, rows = rows_of(n)
            target = mine.at[n] if n < crossing else norm.at[r, rows, :]
            terms = [part_of(n, z)]
            if z > 0:
                remote(part_of(n, z), from_left.at[n, z], right_sum, (n, z), right).wait_recv()
                terms.append(from_left.at[n, z])
            if z < last:
                remote(part_of(n, z), from_right.at[n, z], left_sum, (n, z), left).wait_recv()
                terms.append(from_right.at[n, z])
            add_up(target, *terms)
            if n < crossing:
                pair(n).start()
        elif kind == NORM:
            r, _ = rows_of(n)
            if n < crossing:
                pair(n).wait_recv()
            norm_backward(r, (n % crossing) * sub)
            own(n, z).start()
            if z < last:
                remote(result_of(n), chunk(n, z), right_sem, (n, z), right).start()
            if z > 0:
                remote(result_of(n), chunk(n, z), left_sem, (n, z), left).start()
        elif kind == GO_RIGHT:
            copy = remote(chunk(n, c), chunk(n, c), right_sem, (n, c), right)
            copy.wait_recv()
            if z < last:
                copy.start()
        elif kind == GO_LEFT:
            copy = remote(chunk(n, c), chunk(n, c), left_sem, (n, c), left)
            copy.wait_recv()
            if z > 0:
                copy.start()
        elif kind in (PART_RIGHT, PART_LEFT):
            rightwards = kind == PART_RIGHT
            buffer, sems, target = (part_from_left, part_right, right) if rightwards else (part_from_right, part_left, left)
            if z == (0 if rightwards else last):
                remote(g_ref.at[c], buffer.at[c], sems, (c,), target).start()
            else:
                copy = remote(buffer.at[c], buffer.at[c], sems, (c,), target)
                copy.wait_recv()
                add_up(buffer.at[c], buffer.at[c], g_ref.at[c])
                copy.start()
        else:
            terms = [g_ref.at[z]]
            if z > 0:
                remote(g_ref.at[z], part_from_left.at[z], part_right, (z,), right).wait_recv()
                terms.append(part_from_left.at[z])
            if z < last:
                remote(g_ref.at[z], part_from_right.at[z], part_left, (z,), left).wait_recv()
                terms.append(part_from_right.at[z])
            add_up(s_ref.at[row], *terms)
            edge_g.start()
            sum_gains()
            for share in shares:
                share.start()

    def make_q():
        rows_copy.wait()
        for c in range(third):
            lanes = slice(c * width, (c + 1) * width)
            product = dot_nn(lin_ref[lanes, :], rows_scr[...]).astype(BF16).T
            q_ref[:, c * half : (c + 1) * half, :] = product.reshape(group, half, width)
        q_ref[:, third * half :, :] = taps_ref[...]
        for part in q_parts:
            part.start()

    def sum_q():
        for part in q_parts:
            part.wait_recv()
        mixed = q_ref[spot].astype(F32)
        for k in range(group - 1):
            mixed = mixed + q_came[k].astype(F32)
        for c in range(third):
            r_ref[c, row] = mixed[c * half : (c + 1) * half, :].astype(BF16)
        tap_out[...] = mixed[third * half :, :]
        edge_q.start()

    def sum_gains():
        rows = pl.ds(pl.multiple_of(row * half, half), half)
        lane = lax.broadcasted_iota(jnp.int32, (half, 128), 1)
        first = sum(r_ref[c, row].astype(F32) * qkv_ref[c, rows, :].astype(F32) for c in range(third))
        first = jnp.sum(first, axis=1, keepdims=True)
        second = jnp.sum(s_ref[row, :, :units].astype(F32) * up_ref[rows, :].astype(F32), axis=1, keepdims=True)
        gains[row, me] = jnp.where(lane == 0, first, second)

    def write_weights():
        edge_g.wait_recv()
        edge_q.wait_recv()
        for c in range(ctx_count):
            rows = slice(c * half, (c + 1) * half)
            up_out[rows, :] = s_ref[c, :, :units].astype(F32)
            down_out[rows, :] = s_ref[c, :, units : 2 * units].astype(F32)
        last_part = jnp.concatenate([s_ref[c, :, 2 * units :] for c in range(ctx_count)], axis=0)
        out_out[...] = last_part.astype(F32).T
        for c in range(third):
            for e in range(ctx_count):
                qkv_out[c, e * half : (e + 1) * half, :] = r_ref[c, e].astype(F32)

    order = line_order(tp_count, pieces)
    at_once = {0: SUM_RIGHT, last: SUM_LEFT}
    for z in at_once:

        @pl.when(me == z)
        def _():
            for step in order[z]:
                if step[0] == at_once[z]:
                    step_of(z, *step)

    make_q()
    for z in range(tp_count):

        @pl.when(me == z)
        def _():
            for place, step in enumerate(order[z]):
                if step[0] != at_once.get(z):
                    step_of(z, *step)
                if place == len(order[z]) // 2:
                    sum_q()
            for n in range(pieces):
                own(n, z).wait()
                for c in range(tp_count):
                    if c > z:
                        remote(part_of(n, c), from_left.at[n, c], right_sum, (n, c), {TP: z + 1}).wait_send()
                    if c < z:
                        remote(part_of(n, c), from_right.at[n, c], left_sum, (n, c), {TP: z - 1}).wait_send()
                    if n == 0 and c > z:
                        remote(g_ref.at[c], part_from_left.at[c], part_right, (c,), {TP: z + 1}).wait_send()
                    if n == 0 and c < z:
                        remote(g_ref.at[c], part_from_right.at[c], part_left, (c,), {TP: z - 1}).wait_send()
                    if c <= z < last:
                        remote(chunk(n, c), chunk(n, c), right_sem, (n, c), {TP: z + 1}).wait_send()
                    if c >= z > 0:
                        remote(chunk(n, c), chunk(n, c), left_sem, (n, c), {TP: z - 1}).wait_send()

    for k in range(1, ctx_count * tp_count):
        c = lax.rem(row + ctx_count - k // tp_count, ctx_count)
        source = lax.rem(me + tp_count - k % tp_count, tp_count)
        remote(gains.at[c, source], gains.at[c, source], gain_sem, (k - 1,), mate_at[k - 1]).wait_recv()
    for c in range(ctx_count):
        total = gains[c, 0]
        for k in range(1, tp_count):
            total = total + gains[c, k]
        gain_out[c] = total
    write_weights()
    for n in range(crossing):
        pair(n).wait_send()
    for copy in q_parts + shares + [edge_g, edge_q]:
        copy.wait_send()


def tail(parts, x, middle, gain, g, linear, normed, taps, up, qkv, fsdp_count, ident):
    ctx_count, tp_count, size, model = parts.shape
    slice_d, units = up.shape
    third, _, width = qkv.shape
    group = ctx_count * fsdp_count
    half = slice_d // ctx_count
    deep = third * half + taps.shape[1]
    pieces = 2 * ctx_count
    sub = size // ctx_count
    vmem = pl.BlockSpec(memory_space=pltpu.VMEM)
    whole = pl.BlockSpec(memory_space=pl.ANY)
    return pl.pallas_call(
        functools.partial(tail_kernel, tp_count, fsdp_count),
        out_shape=(
            jax.ShapeDtypeStruct((ctx_count, size * tp_count, model), BF16),
            jax.ShapeDtypeStruct((slice_d, units), F32),
            jax.ShapeDtypeStruct((slice_d, units), F32),
            jax.ShapeDtypeStruct((width, slice_d), F32),
            jax.ShapeDtypeStruct((third, slice_d, width), F32),
            jax.ShapeDtypeStruct(taps.shape[1:], F32),
            jax.ShapeDtypeStruct((ctx_count, half, 128), F32),
        ),
        in_specs=[vmem] * 6 + [whole] + [vmem] * 3,
        out_specs=(vmem,) * 7,
        scratch_shapes=[
            pltpu.VMEM((pieces, tp_count, sub, model), BF16),
            pltpu.VMEM((pieces, tp_count, sub, model), BF16),
            pltpu.VMEM((pieces // 2, sub, model), BF16),
            pltpu.VMEM(x.shape, BF16),
            pltpu.VMEM(x.shape, BF16),
            pltpu.VMEM(g.shape, BF16),
            pltpu.VMEM(g.shape, BF16),
            pltpu.VMEM((ctx_count,) + g.shape[1:], BF16),
            pltpu.VMEM((third, ctx_count, half, width), BF16),
            pltpu.VMEM(normed.shape, BF16),
            pltpu.VMEM((group, deep, width), BF16),
            pltpu.VMEM((group - 1, deep, width), BF16),
            pltpu.VMEM((ctx_count, tp_count, half, 128), F32),
            pltpu.SemaphoreType.DMA((2, pieces, tp_count)),
            pltpu.SemaphoreType.DMA((2, pieces, tp_count)),
            pltpu.SemaphoreType.DMA((2, pieces, tp_count)),
            pltpu.SemaphoreType.DMA((2, pieces, tp_count)),
            pltpu.SemaphoreType.DMA((2, pieces // 2)),
            pltpu.SemaphoreType.DMA((2, tp_count)),
            pltpu.SemaphoreType.DMA((2, tp_count)),
            pltpu.SemaphoreType.DMA((pieces,)),
            pltpu.SemaphoreType.DMA((2, group - 1)),
            pltpu.SemaphoreType.DMA((2, 2)),
            pltpu.SemaphoreType.DMA((2, ctx_count * tp_count - 1)),
            pltpu.SemaphoreType.DMA,
        ],
        compiler_params=pltpu.CompilerParams(collective_id=ident, has_side_effects=True),
        name="tail",
    )(parts, x, middle, gain, g, linear, normed, taps, up, qkv)


def pack_kernel(up_ref, down_ref, out_ref, packed_ref):
    units = up_ref.shape[1]
    packed_ref[:, :units] = up_ref[...]
    packed_ref[:, units : 2 * units] = down_ref[...]
    packed_ref[:, 2 * units :] = out_ref[...].T


def pack(up, down, out):
    slice_d, units = up.shape
    return pl.pallas_call(
        pack_kernel,
        out_shape=jax.ShapeDtypeStruct((slice_d, 2 * units + out.shape[0]), up.dtype),
        in_specs=[pl.BlockSpec(memory_space=pltpu.VMEM)] * 3,
        out_specs=pl.BlockSpec(memory_space=pltpu.VMEM),
        name="pack",
    )(up, down, out)


def write_kernel(*refs):
    count = len(refs) // 2
    refs[count][...] = refs[0][...].astype(F32)

    @pl.when(pl.program_id(0) == 0)
    def _():
        for source, target in zip(refs[1:count], refs[count + 1 :]):
            target[...] = source[...]


def write(wide, *others):
    rows, length, model = wide.shape
    steps = length // TILE
    moving = pl.BlockSpec((rows, TILE, model), lambda i: (0, i, 0))

    def whole(x):
        return pl.BlockSpec(x.shape, lambda i: (0,) * x.ndim)

    return pl.pallas_call(
        write_kernel,
        grid=(steps,),
        out_shape=(jax.ShapeDtypeStruct(wide.shape, F32),) + tuple(jax.ShapeDtypeStruct(x.shape, x.dtype) for x in others),
        in_specs=[moving] + [whole(x) for x in others],
        out_specs=(moving,) + tuple(whole(x) for x in others),
        name="write",
    )(wide, *others)


def assemble_kernel(part_ref, *refs):
    *chunks, out_ref = refs
    for k, chunk in enumerate(chunks):

        @pl.when(pl.program_id(0) == k)
        def _():
            out_ref[...] = chunk[...]


def assemble(part, chunks):
    count = len(chunks)
    rows, size, model = chunks[0].shape
    fixed = pl.BlockSpec((rows, size, model), lambda k, _: (0, 0, 0))
    return pl.pallas_call(
        assemble_kernel,
        out_shape=jax.ShapeDtypeStruct((rows, count * size, model), chunks[0].dtype),
        grid_spec=pltpu.PrefetchScalarGridSpec(
            num_scalar_prefetch=1,
            grid=(count,),
            in_specs=[fixed] * count,
            out_specs=pl.BlockSpec((rows, size, model), lambda k, part: (0, lax.rem(part[0] + count - k, count), 0)),
        ),
        name="assemble",
    )(part.reshape(1), *chunks)


def weight_grads_kernel(norm_ref, cot_ref, branch_ref, up_ref, hid_ref, att_ref, out_ref, norm_t, cot_t, branch_t):
    @pl.when(pl.program_id(0) == 0)
    def _():
        norm_t[...] = norm_ref[...].T
        cot_t[...] = cot_ref[...].T
        branch_t[...] = branch_ref[...].T

    pieces, _, piece, _ = out_ref.shape
    units = up_ref.shape[2]
    quarter = att_ref.shape[3]

    def put(value, start):
        stop = start + value.shape[1]
        out_ref[:, 0, :, start:stop] = value.astype(BF16).reshape(pieces, piece, value.shape[1])

    put(dot_nn(norm_t[...], up_ref[0]), 0)
    put(dot_nn(cot_t[...], hid_ref[0]), units)
    total = None
    for r in range(att_ref.shape[0]):
        term = dot_nt(branch_t[:, r * quarter : (r + 1) * quarter], att_ref[r, 0])
        total = term if total is None else total + term
    put(total, 2 * units)


def weight_grads(normed, cot, branch, grad_up, hidden, att, pieces):
    tokens, model = normed.shape
    blocks, _, units = hidden.shape
    rows, _, width, quarter = att.shape
    columns = 2 * units + width
    fixed = pl.BlockSpec((tokens, model), lambda b: (0, 0))
    moving = pl.BlockSpec((1, tokens, units), lambda b: (b, 0, 0))
    return pl.pallas_call(
        weight_grads_kernel,
        grid=(blocks,),
        out_shape=jax.ShapeDtypeStruct((pieces, blocks, model // pieces, columns), BF16),
        in_specs=[fixed, fixed, fixed, moving, moving, pl.BlockSpec((rows, 1, width, quarter), lambda b: (0, b, 0, 0))],
        out_specs=pl.BlockSpec((pieces, 1, model // pieces, columns), lambda b: (0, b, 0, 0)),
        scratch_shapes=[pltpu.VMEM((model, tokens), BF16)] * 3,
        name="weight_grads",
    )(normed, cot, branch, grad_up, hidden, att)


def row_on_device(
    tokens, gain_one, w_qkv, kernel, w_out, gain_two, w_up, w_down, block_ids, seq_ids, cotangent
):
    place = lax.axis_index(CTX)
    part = lax.axis_index(TP)
    ctx_count = lax.axis_size(CTX)
    tp_count = lax.axis_size(TP)
    fsdp_count = lax.axis_size(FSDP)
    group_len = tokens.shape[1]
    length = group_len * ctx_count
    model = tokens.shape[2]
    taps_count = kernel.shape[0]
    heads = kernel.shape[2]
    width = heads * HD
    rows = tokens.shape[0]
    quarter = group_len // tp_count
    slice_d = w_up.shape[0]
    units = w_up.shape[1]

    qkv_full = lax.all_gather(w_qkv.reshape(slice_d, 3 * width), FSDP, axis=0, tiled=True)
    small = jnp.concatenate([gain_one, gain_two, kernel.reshape(-1)])
    small_all = lax.all_gather(small, FSDP, axis=0).astype(F32)
    gain_first = small_all[:, :slice_d].reshape(-1)
    gain_second = small_all[:, slice_d : 2 * slice_d].reshape(-1)
    taps = small_all[:, 2 * slice_d :].reshape(fsdp_count, taps_count, 3, heads, -1)
    taps = taps.transpose(1, 2, 3, 0, 4).reshape(taps_count, 3 * width)
    packed = pack(w_up, w_down.T, w_out)
    gathered = lax.all_gather(packed, (TP, FSDP), axis=0, tiled=True)
    gathered = gathered.reshape(tp_count, model, packed.shape[1])
    up_blocks = gathered[:, :, :units]
    down_blocks = gathered[:, :, units : 2 * units]
    out_blocks = gathered[:, :, 2 * units :]

    away = lax.dynamic_index_in_dim(tokens, 1 - place, 0, keepdims=False)
    swap = [(i, 1 - i) for i in range(ctx_count)]
    came = lax.ppermute(away, CTX, swap)
    block_row = lax.dynamic_index_in_dim(block_ids, place, 0, keepdims=False)
    seq_row = lax.dynamic_index_in_dim(seq_ids, place, 0, keepdims=False)
    owner_row = jnp.repeat(seq_row, group_len)
    code = (owner_row * 16 + block_row)[None, :]
    codes = jnp.arange(32, dtype=jnp.int32)[:, None]
    upto = jnp.sum((code <= codes).astype(jnp.int32), axis=1, keepdims=True)
    hi = jnp.sum(jnp.where(code == codes, upto, 0), axis=0, keepdims=True)
    first_piece = jnp.sum((seq_row[None, :] < seq_row[:, None]).astype(jnp.int32), axis=1)
    lo_tile = jnp.repeat(first_piece * (group_len // TILE), group_len // QUERIES)

    same = [
        jnp.concatenate([jnp.zeros((j,), F32), (owner_row[j:] == owner_row[: length - j]).astype(F32)])
        for j in range(taps_count)
    ]
    triple, linear, normed = project(
        place, tokens, came, qkv_full, gain_first[None, :], taps, jnp.stack(same), heads
    )
    att, lse = attn_forward(lo_tile, hi, triple, heads)

    got = spread(att, ctx_count, tp_count, 1)
    got = got.reshape(rows, tp_count, width, quarter)
    attended = got.transpose(0, 3, 1, 2).reshape(rows * quarter, tp_count * width)
    states = lax.dynamic_slice_in_dim(tokens, part * quarter, quarter, 1)
    states = states.reshape(rows * quarter, model).astype(F32)
    grad_out = lax.dynamic_slice_in_dim(cotangent, part * quarter, quarter, 1)
    grad_out = grad_out.reshape(rows * quarter, model)
    out_flat = out_blocks.transpose(1, 0, 2).reshape(model, tp_count * width)
    middle = states + dot_nt(attended, out_flat)
    inv_two, base_two = norm_parts(middle)
    normed_two = (base_two * gain_second).astype(BF16)
    upward = jnp.einsum("td,bdu->btu", normed_two, up_blocks, preferred_element_type=F32)
    lifted = jnp.maximum(upward, 0.0)
    hidden = (lifted * lifted).astype(BF16)
    ffn = jnp.einsum("btu,bdu->td", hidden, down_blocks, preferred_element_type=F32)
    block_out = (middle + ffn).astype(BF16).reshape(rows, quarter, model)
    block_out, lifted = lax.optimization_barrier((block_out, lifted))
    rings = [[(i, (i + k) % tp_count) for i in range(tp_count)] for k in range(tp_count)]
    chunks = [block_out]
    chunks.append(lax.ppermute(block_out, TP, rings[1]))
    grad_hidden = jnp.einsum("td,bdu->btu", grad_out, down_blocks, preferred_element_type=F32)
    grad_upward = (grad_hidden * 2.0 * lifted).astype(BF16)
    grad_norm_two = jnp.einsum("btu,bdu->td", grad_upward, up_blocks, preferred_element_type=F32)
    back_two = norm_back(grad_norm_two, gain_second, inv_two, base_two)
    grad_middle = grad_out.astype(F32) + back_two
    grad_branch = grad_middle.astype(BF16)
    grad_attended = dot_nn(grad_branch, out_flat).astype(BF16)
    grad_packed = weight_grads(normed_two, grad_out, grad_branch, grad_upward, hidden, got, fsdp_count * ctx_count)

    sent = grad_attended.reshape(rows, quarter, tp_count, width).transpose(0, 2, 3, 1)
    sent, grad_packed = lax.optimization_barrier((sent, grad_packed))
    columns = grad_packed.shape[3]
    grad_packed = grad_packed.reshape(-1, columns)
    grad_packed = lax.psum_scatter(grad_packed, (FSDP, CTX), scatter_dimension=0, tiled=True)
    grad_packed = grad_packed.reshape(tp_count, -1, columns)
    got = spread(sent.reshape(rows * tp_count, width, quarter), ctx_count, tp_count, 2)
    grad_att, block_out = lax.optimization_barrier((got, block_out))
    chunks += [lax.ppermute(block_out, TP, ring) for ring in rings[2:]]
    later = jnp.stack([jnp.pad(same[j][j:], (0, j)) for j in range(taps_count)])
    grad_linear, grad_taps = attn_backward(lo_tile, hi, triple, grad_att, att, lse, linear, later, taps, heads)
    grad_taps = grad_taps[:, :taps_count].T
    sent = lax.dot_general(
        grad_linear, qkv_full, (((0,), (1,)), ((), ())), preferred_element_type=F32
    ).astype(BF16).reshape(ctx_count, tp_count, quarter, model)
    sent, *chunks = lax.optimization_barrier((sent, *chunks))
    block_out = assemble(part, chunks)
    f_taps = grad_taps.reshape(taps_count * 3 * heads, fsdp_count, -1).transpose(1, 0, 2).reshape(fsdp_count, -1)
    f_taps = jnp.pad(f_taps.astype(BF16), ((0, 0), (0, 16 * width - f_taps.shape[1])))
    f_taps = jnp.repeat(f_taps.reshape(fsdp_count, 16, width), ctx_count, axis=0)

    input_grad, grad_up, grad_down, grad_out_w, grad_qkv, grad_taps, gains = tail(
        sent,
        states.astype(BF16).reshape(rows, quarter, model),
        grad_middle.reshape(rows, quarter, model),
        gain_first[None, :],
        grad_packed,
        grad_linear,
        normed,
        f_taps,
        w_up,
        w_qkv.transpose(1, 0, 2),
        fsdp_count,
        3,
    )
    input_grad, grad_up, grad_down, grad_out_w, grad_qkv = write(input_grad, grad_up, grad_down, grad_out_w, grad_qkv)
    grad_taps = grad_taps.reshape(-1)[: kernel.size].reshape(kernel.shape)
    gains = gains.reshape(slice_d, -1)[:, :2].T / jnp.stack([gain_one, gain_two]).astype(F32)
    return (
        block_out,
        input_grad,
        gains[0],
        grad_qkv.transpose(1, 0, 2),
        grad_taps,
        grad_out_w,
        gains[1],
        grad_up,
        grad_down.T,
    )


MICRO = 2
SEQS_MB = 1


def passed_along(block, axis, distance):
    devices = range(lax.axis_size(axis))
    route = [(i - distance, i) for i in devices if i - distance in devices]
    return lax.ppermute(block, axis, route)


def any_norm_parts(values):
    inverse = lax.rsqrt(jnp.mean(values * values, axis=-1, keepdims=True) + 1e-06)
    return (inverse, values * inverse)


def any_norm_back(grad_norm, gain_full, inverse, scaled):
    grad_scaled = grad_norm * gain_full
    inner_mean = jnp.mean(grad_scaled * scaled, axis=-1, keepdims=True)
    return (inverse * (grad_scaled - scaled * inner_mean), jnp.sum(grad_norm * scaled, axis=(0, 1)))


def masked_scores(queries, key_heads, allowed, score_scale):
    scores = (
        jnp.einsum("sqhe,skhe->shqk", queries, key_heads, preferred_element_type=jnp.float32)
        * score_scale
    )
    return jnp.where(allowed[:, None], scores, -1e30)


def tensor_total(values):
    return lax.psum(values, TP)


def any_on_device(
    tokens, gain_one, w_qkv, kernel, w_out, gain_two, w_up, w_down, block_ids, seq_ids, cotangent
):
    ctx_place = lax.axis_index(CTX)
    ctx_count = lax.axis_size(CTX)
    group_len = tokens.shape[1]
    taps_count = kernel.shape[0]
    margin = taps_count - 1
    local_heads = kernel.shape[2]
    score_scale = HD ** (-0.5)
    per_micro = SEQS_MB
    group_start = ctx_place * group_len
    owner_all = jnp.repeat(seq_ids, group_len, axis=1)
    totals = None
    outputs = []
    input_grads = []
    for micro_step in range(MICRO):
        gathered = (
            lax.all_gather(gain_one, FSDP, axis=0, tiled=True),
            lax.all_gather(w_qkv, FSDP, axis=0, tiled=True),
            lax.all_gather(kernel, FSDP, axis=3, tiled=True),
            lax.all_gather(w_out, FSDP, axis=1, tiled=True),
            lax.all_gather(gain_two, FSDP, axis=0, tiled=True),
            lax.all_gather(w_up, FSDP, axis=0, tiled=True),
            lax.all_gather(w_down, FSDP, axis=1, tiled=True),
        )
        gain_first, qkv_full, conv_taps, out_full, gain_second, up_full, down_full = gathered
        gain_first = gain_first.astype(jnp.float32)
        gain_second = gain_second.astype(jnp.float32)
        tap_weights = conv_taps.astype(jnp.float32).reshape(taps_count, 3, -1)
        first_row = micro_step * per_micro
        states = tokens[first_row : first_row + per_micro].astype(jnp.float32)
        block_rows = block_ids[first_row : first_row + per_micro]
        owner_rows = owner_all[first_row : first_row + per_micro]
        group_ids = seq_ids[first_row : first_row + per_micro]
        own_group = lax.dynamic_slice_in_dim(group_ids, ctx_place, 1, 1)
        group_before = lax.dynamic_slice_in_dim(group_ids, jnp.maximum(ctx_place - 1, 0), 1, 1)
        group_after = lax.dynamic_slice_in_dim(
            group_ids, jnp.minimum(ctx_place + 1, ctx_count - 1), 1, 1
        )
        keep_before = (group_before == own_group).astype(jnp.float32)[:, :, None, None]
        keep_after = (group_after == own_group).astype(jnp.float32)[:, :, None, None]
        own_blocks = lax.dynamic_slice_in_dim(block_rows, group_start, group_len, 1)
        allowed = (block_rows[:, None, :] <= own_blocks[:, :, None]) & (
            owner_rows[:, None, :] == own_group[:, :, None]
        )
        inv_one, base_one = any_norm_parts(states)
        normed = (base_one * gain_first).astype(jnp.bfloat16)
        linear = jnp.einsum(
            "std,dce->stce", normed, qkv_full, preferred_element_type=jnp.float32
        ).astype(jnp.bfloat16)
        edge_rows = passed_along(linear[:, group_len - margin :], CTX, 1)
        padded = jnp.concatenate(
            [edge_rows.astype(jnp.float32) * keep_before, linear.astype(jnp.float32)], axis=1
        )
        mixed_conv = sum(
            (
                tap_weights[offset] * padded[:, margin - offset : margin - offset + group_len]
                for offset in range(taps_count)
            )
        )
        triple = mixed_conv.astype(jnp.bfloat16)
        queries = triple[:, :, 0].reshape(per_micro, group_len, local_heads, HD)
        key_pair = lax.all_gather(triple[:, :, 1:], CTX, axis=1, tiled=True)
        key_heads = key_pair[:, :, 0].reshape(per_micro, -1, local_heads, HD)
        value_heads = key_pair[:, :, 1].reshape(per_micro, -1, local_heads, HD)
        scores = masked_scores(queries, key_heads, allowed, score_scale)
        row_peak = jnp.max(scores, axis=-1, keepdims=True)
        log_total = row_peak + jnp.log(jnp.sum(jnp.exp(scores - row_peak), axis=-1, keepdims=True))
        probs_low = jnp.exp(scores - log_total).astype(jnp.bfloat16)
        attended = jnp.einsum(
            "shqk,skhe->sqhe", probs_low, value_heads, preferred_element_type=jnp.float32
        )
        attended = attended.astype(jnp.bfloat16).reshape(per_micro, group_len, -1)
        attn_part = jnp.einsum(
            "std,de->ste", attended, out_full, preferred_element_type=jnp.float32
        )
        grad_out = cotangent[first_row : first_row + per_micro]
        middle = states + tensor_total(attn_part)
        inv_two, base_two = any_norm_parts(middle)
        normed_two = (base_two * gain_second).astype(jnp.bfloat16)
        upward = jnp.einsum("std,df->stf", normed_two, up_full, preferred_element_type=jnp.float32)
        lifted = jnp.maximum(upward, 0.0)
        hidden = (lifted * lifted).astype(jnp.bfloat16)
        ffn_part = jnp.einsum("stf,fd->std", hidden, down_full, preferred_element_type=jnp.float32)
        outputs.append((middle + tensor_total(ffn_part)).astype(jnp.bfloat16))
        grad_down = jnp.einsum("stf,std->fd", hidden, grad_out, preferred_element_type=jnp.float32)
        grad_hidden = jnp.einsum(
            "std,fd->stf", grad_out, down_full, preferred_element_type=jnp.float32
        )
        grad_upward = (grad_hidden * 2.0 * lifted).astype(jnp.bfloat16)
        grad_up = jnp.einsum(
            "std,stf->df", normed_two, grad_upward, preferred_element_type=jnp.float32
        )
        norm_two_part = jnp.einsum(
            "stf,df->std", grad_upward, up_full, preferred_element_type=jnp.float32
        )
        back_two, grad_gain_two = any_norm_back(
            tensor_total(norm_two_part), gain_second, inv_two, base_two
        )
        grad_middle = grad_out.astype(jnp.float32) + back_two
        grad_branch = grad_middle.astype(jnp.bfloat16)
        grad_out_proj = jnp.einsum(
            "std,ste->de", attended, grad_branch, preferred_element_type=jnp.float32
        )
        grad_attended = jnp.einsum(
            "ste,de->std", grad_branch, out_full, preferred_element_type=jnp.float32
        )
        grad_attended = grad_attended.astype(jnp.bfloat16).reshape(
            per_micro, group_len, local_heads, HD
        )
        prob_full = jnp.exp(masked_scores(queries, key_heads, allowed, score_scale) - log_total)
        grad_probs = jnp.einsum(
            "sqhe,skhe->shqk", grad_attended, value_heads, preferred_element_type=jnp.float32
        )
        row_total = jnp.sum(prob_full * grad_probs, axis=-1, keepdims=True)
        grad_scores = (prob_full * (grad_probs - row_total)).astype(jnp.bfloat16)
        grad_queries = (
            jnp.einsum(
                "shqk,skhe->sqhe", grad_scores, key_heads, preferred_element_type=jnp.float32
            )
            * score_scale
        )
        keys_term = (
            jnp.einsum("shqk,sqhe->skhe", grad_scores, queries, preferred_element_type=jnp.float32)
            * score_scale
        )
        values_term = jnp.einsum(
            "shqk,sqhe->skhe",
            prob_full.astype(jnp.bfloat16),
            grad_attended,
            preferred_element_type=jnp.float32,
        )
        pair_grads = lax.psum_scatter(
            jnp.stack([keys_term, values_term], axis=2).astype(jnp.bfloat16),
            CTX,
            scatter_dimension=1,
            tiled=True,
        ).astype(jnp.float32)
        grad_keys = pair_grads[:, :, 0]
        grad_values = pair_grads[:, :, 1]
        grad_triple = jnp.stack([grad_queries, grad_keys, grad_values], axis=2).reshape(
            per_micro, group_len, 3, -1
        )
        tail_rows = passed_along(grad_triple[:, :margin], CTX, -1)
        padded_grad = jnp.concatenate([grad_triple, tail_rows * keep_after], axis=1)
        grad_linear = sum(
            (
                tap_weights[offset] * padded_grad[:, offset : offset + group_len]
                for offset in range(taps_count)
            )
        )
        grad_linear = grad_linear.astype(jnp.bfloat16)
        grad_taps = jnp.stack(
            [
                jnp.sum(
                    grad_triple * padded[:, margin - offset : margin - offset + group_len],
                    axis=(0, 1),
                )
                for offset in range(taps_count)
            ]
        )
        grad_taps = grad_taps.reshape(conv_taps.shape)
        grad_qkv = jnp.einsum(
            "std,stce->dce", normed, grad_linear, preferred_element_type=jnp.float32
        )
        grad_norm_one = tensor_total(
            jnp.einsum("stce,dce->std", grad_linear, qkv_full, preferred_element_type=jnp.float32)
        )
        back_one, grad_gain_one = any_norm_back(grad_norm_one, gain_first, inv_one, base_one)
        input_grads.append(grad_middle + back_one)
        micro_grads = (
            grad_gain_one,
            grad_qkv,
            grad_taps,
            grad_out_proj,
            grad_gain_two,
            grad_up,
            grad_down,
        )
        totals = (
            micro_grads
            if totals is None
            else tuple(
                (left_part + right_part for left_part, right_part in zip(totals, micro_grads))
            )
        )
    summed = (
        lax.psum_scatter(totals[0], (FSDP, CTX), scatter_dimension=0, tiled=True),
        lax.psum_scatter(totals[1], (FSDP, CTX), scatter_dimension=0, tiled=True),
        lax.psum_scatter(totals[2], (FSDP, CTX), scatter_dimension=3, tiled=True),
        lax.psum_scatter(totals[3], (FSDP, CTX), scatter_dimension=1, tiled=True),
        lax.psum_scatter(totals[4], (FSDP, CTX), scatter_dimension=0, tiled=True),
        lax.psum_scatter(totals[5], (FSDP, CTX), scatter_dimension=0, tiled=True),
        lax.psum_scatter(totals[6], (FSDP, CTX), scatter_dimension=1, tiled=True),
    )
    shares = (
        lax.all_gather(summed[0].astype(jnp.bfloat16), CTX, axis=0, tiled=True).astype(
            jnp.float32
        ),
        lax.all_gather(summed[1].astype(jnp.bfloat16), CTX, axis=0, tiled=True).astype(
            jnp.float32
        ),
        lax.all_gather(summed[2].astype(jnp.bfloat16), CTX, axis=3, tiled=True).astype(
            jnp.float32
        ),
        lax.all_gather(summed[3].astype(jnp.bfloat16), CTX, axis=1, tiled=True).astype(
            jnp.float32
        ),
        lax.all_gather(summed[4].astype(jnp.bfloat16), CTX, axis=0, tiled=True).astype(
            jnp.float32
        ),
        lax.all_gather(summed[5].astype(jnp.bfloat16), CTX, axis=0, tiled=True).astype(
            jnp.float32
        ),
        lax.all_gather(summed[6].astype(jnp.bfloat16), CTX, axis=1, tiled=True).astype(
            jnp.float32
        ),
    )
    return (jnp.concatenate(outputs, axis=0), jnp.concatenate(input_grads, axis=0)) + tuple(shares)


def solution(mesh):
    placed = (
        P(FSDP, CTX, None),
        P(FSDP),
        P(FSDP, None, TP),
        P(None, None, TP, FSDP),
        P(TP, FSDP),
        P(FSDP),
        P(FSDP, TP),
        P(TP, FSDP),
        P(FSDP, None),
        P(FSDP, None),
        P(FSDP, CTX, None),
    )

    def on_device(*args):
        if args[0].shape[0] == lax.axis_size(CTX) == 2 and args[0].shape[1] == TILE * lax.axis_size(TP):
            return row_on_device(*args)
        return any_on_device(*args)

    return jax.shard_map(
        on_device,
        mesh=mesh,
        in_specs=placed,
        out_specs=(
            P(FSDP, CTX, None),
            P(FSDP, CTX, None),
            P(FSDP),
            P(FSDP, None, TP),
            P(None, None, TP, FSDP),
            P(TP, FSDP),
            P(FSDP),
            P(FSDP, TP),
            P(TP, FSDP),
        ),
        check_vma=False,
    )
```
